32 devices in a mesh: dp: 8 (over z, y), fsdp: 4 (over x, core).
Axes of the slice: x: 2, y: 2, z: 4, core: 2. Of those that a mesh axis runs over, the one named last changes fastest.
Arguments:
- tokens: bfloat16 [8192, 768], P(('dp', 'fsdp')), may hold values from -6 to 6
- starts: int32 [32], P(('dp', 'fsdp')), may hold values from 0 to 1, as said below
- valid: int32 [8192], P(('dp', 'fsdp')), may hold values from 0 to 1, as said below
- norm_gain: bfloat16 [2, 768], P(None, ('dp', 'fsdp')), may hold values from 0.5 to 1.5
- w_gate: bfloat16 [2, 768, 1536], P(None, ('dp', 'fsdp')), may hold values from -0.21875 to 0.21875
- w_xbc: bfloat16 [2, 768, 1792], P(None, ('dp', 'fsdp')), may hold values from -0.21875 to 0.21875
- w_dt: bfloat16 [2, 768, 24], P(None, ('dp', 'fsdp')), may hold values from -0.21875 to 0.21875
- conv_weight: bfloat16 [2, 4, 1792], P(None, None, ('dp', 'fsdp')), may hold values from -3 to 3
- conv_bias: bfloat16 [2, 1792], P(None, ('dp', 'fsdp')), may hold values from -0.5 to 0.5
- dt_bias: float32 [2, 24], replicated, may hold values from -9 to -2
- a_log: float32 [2, 24], replicated, may hold values from -2 to 2
- skip_weight: float32 [2, 24], replicated, may hold values from 0.5 to 1.5
- gate_gain: bfloat16 [2, 1536], P(None, ('dp', 'fsdp')), may hold values from 0.5 to 1.5
- w_out: bfloat16 [2, 1536, 768], P(None, ('dp', 'fsdp')), may hold values from -0.15625 to 0.15625
- cotangent: bfloat16 [8192, 768], P(('dp', 'fsdp')), may hold values from -6 to 6
Outputs:
- activations: float32 [8192, 768], P(('dp', 'fsdp'))
- input_grad: float32 [8192, 768], P(('dp', 'fsdp'))
- grad_norm_gain: float32 [2, 768], P(None, ('dp', 'fsdp'))
- grad_w_gate: float32 [2, 768, 1536], P(None, ('dp', 'fsdp'))
- grad_w_xbc: float32 [2, 768, 1792], P(None, ('dp', 'fsdp'))
- grad_w_dt: float32 [2, 768, 24], P(None, ('dp', 'fsdp'))
- grad_conv_weight: float32 [2, 4, 1792], P(None, None, ('dp', 'fsdp'))
- grad_conv_bias: float32 [2, 1792], P(None, ('dp', 'fsdp'))
- grad_dt_bias: float32 [2, 24], replicated
- grad_a_log: float32 [2, 24], replicated
- grad_skip_weight: float32 [2, 24], replicated
- grad_gate_gain: float32 [2, 1536], P(None, ('dp', 'fsdp'))
- grad_w_out: float32 [2, 1536, 768], P(None, ('dp', 'fsdp'))
The draws below stay inside these ranges and needn't reach their ends.
Inputs may be any that keep to these rules, and one draw needn't show every extreme that they name: starts is 1 where a span of 256 tokens begins a packed sequence; within every 1024 tokens of one dp index the first span is 1 and the second is 0. valid is 0 only on fewer than 128 padding tokens at the end of a sequence's last span.
All inputs are finite; a program needn't handle non-finite values.
Results may differ from the reference program's by a relative error of at most 0.02.
Values may be sent and summed in bfloat16 or wider, within the bound.
No kernel may reach another device: no remote copies, remote signals or barrier semaphores. Data moves between devices by JAX's collectives and lax.ppermute only.
A program may use at most 256 MiB of HBM per device.

```python
import jax
import jax.numpy as jnp
from jax import lax

D = 768
INNER = 1536
HEADS = 24
HEAD_DIM = 64
STATE = 128
KCONV = 4
SPAN = 256
LAYERS = 2
TOK_DEV = 256
XBC = 1792
TOKENS = 8192
N_DP = 8
N_FSDP = 4


def layout(key):
    count = TOKENS // SPAN
    per_group = N_FSDP * TOK_DEV // SPAN
    first_key = jax.random.fold_in(key, 11)
    second_key = jax.random.fold_in(key, 23)
    flips = jax.random.randint(first_key, (count,), 0, 3)
    local = jnp.arange(count) % per_group
    starts = jnp.where(local == 0, 1, jnp.where(local == 1, 0, jnp.where(flips == 0, 1, 0))).astype(jnp.int32)
    following = jnp.concatenate([starts[1:], jnp.ones((1,), jnp.int32)])
    closing = jnp.where(local == per_group - 1, 1, following)
    padding = jax.random.randint(second_key, (count,), 0, SPAN // 2)
    offset = jnp.arange(SPAN)
    inside = jnp.logical_or(closing[:, None] == 0, offset[None, :] < SPAN - padding[:, None])
    return (starts, inside.astype(jnp.int32).reshape(TOKENS))


def draw_starts(key, part):
    return layout(key)[0]


def draw_valid(key, part):
    return layout(key)[1]


def shard_levels(own_key, shape, cuts, smallest, high):
    def one(axis_at, blocks):
        steps = jax.random.uniform(jax.random.fold_in(jax.random.fold_in(own_key, 6), axis_at), (blocks,), jnp.float32, smallest / len(cuts), high / len(cuts))
        return jnp.repeat(jnp.exp(steps), shape[axis_at] // blocks).reshape((-1,) + (1,) * (len(shape) - axis_at - 1))

    level = one(*cuts[0])
    for cut in cuts[1:]:
        level = level * one(*cut)
    return level


def bell_draw(stream_key, dims, deviation, reach, split=(), dtype=jnp.bfloat16):
    level = shard_levels(stream_key, dims, split, -0.22, 0.18) if split else 1.0
    entries = jax.random.normal(stream_key, dims, jnp.float32) * deviation * level
    return jnp.minimum(jnp.maximum(entries, -reach), reach).astype(dtype)


def setup_inputs(seed: int = 0) -> dict:
    arg_keys = jax.random.split(jax.random.key(seed), 16)
    tokens = bell_draw(arg_keys[0], (TOKENS, D), 1.0, 6.0, ((0, 32),))
    starts = draw_starts(jax.random.fold_in(arg_keys[15], 71), 0)
    valid = draw_valid(jax.random.fold_in(arg_keys[15], 71), 0)
    norm_gain = jnp.clip(1.0 + 0.1 * jax.random.normal(arg_keys[3], (LAYERS, D), jnp.float32), 0.5, 1.5).astype(jnp.bfloat16)
    w_gate = bell_draw(arg_keys[4], (LAYERS, D, INNER), D ** -0.5, 0.21875, ((1, 32),))
    w_xbc = bell_draw(arg_keys[5], (LAYERS, D, XBC), D ** -0.5, 0.21875, ((1, 32),))
    w_dt = bell_draw(arg_keys[6], (LAYERS, D, HEADS), D ** -0.5, 0.21875, ((1, 32),))
    conv_weight = bell_draw(arg_keys[7], (LAYERS, KCONV, XBC), KCONV ** -0.5, 3.0, ((2, 32),))
    conv_bias = jnp.clip(jax.random.uniform(arg_keys[8], (LAYERS, XBC), jnp.float32, -0.5, 0.5) * shard_levels(arg_keys[8], (LAYERS, XBC), ((1, 32),), -0.4, 0.0), -0.5, 0.5).astype(jnp.bfloat16)
    dt_bias = jnp.clip(jax.random.uniform(arg_keys[9], (LAYERS, HEADS), jnp.float32, -9.0, -2.0), -9.0, -2.0)
    a_log = jnp.clip(jax.random.uniform(arg_keys[10], (LAYERS, HEADS), jnp.float32, -2.0, 2.0), -2.0, 2.0)
    skip_weight = jnp.clip(1.0 + 0.1 * jax.random.normal(arg_keys[11], (LAYERS, HEADS), jnp.float32), 0.5, 1.5)
    gate_gain = jnp.clip(1.0 + 0.1 * jax.random.normal(arg_keys[12], (LAYERS, INNER), jnp.float32), 0.5, 1.5).astype(jnp.bfloat16)
    w_out = bell_draw(arg_keys[13], (LAYERS, INNER, D), INNER ** -0.5, 0.15625, ((1, 32),))
    cotangent = bell_draw(arg_keys[14], (TOKENS, D), 1.0, 6.0, ((0, 32),))
    return {"tokens": tokens, "starts": starts, "valid": valid, "norm_gain": norm_gain, "w_gate": w_gate, "w_xbc": w_xbc, "w_dt": w_dt, "conv_weight": conv_weight, "conv_bias": conv_bias, "dt_bias": dt_bias, "a_log": a_log, "skip_weight": skip_weight, "gate_gain": gate_gain, "w_out": w_out, "cotangent": cotangent}


@jax.custom_vjp
def low(v):
    return lax.optimization_barrier(v.astype(jnp.bfloat16)).astype(jnp.float32)

@jax.custom_vjp
def low_back(v):
    return v

def low_keep(v):
    return (low(v), None)

def low_pass(kept, grad):
    return (grad,)

def back_keep(v):
    return (v, None)

def back_low(kept, grad):
    return (low(grad),)
low.defvjp(low_keep, low_pass)
low_back.defvjp(back_keep, back_low)
epsilon = 1e-05
highest = lax.Precision.HIGHEST

def rms_scale(hidden, gain):
    return hidden * lax.rsqrt(lax.optimization_barrier(jnp.mean(hidden * hidden, axis=-1, keepdims=True)) + epsilon) * gain

def gated_norm(mixed, gate, gain):
    return rms_scale(mixed * jax.nn.silu(gate), gain)

def tap_masks(starts, count):
    offset = jnp.arange(count) % SPAN
    begins = jnp.repeat(starts, SPAN) > 0
    rows = []
    for shift in range(1, KCONV):
        rows.append(jnp.where(jnp.logical_and(begins, offset < shift), 0.0, 1.0))
    return jnp.stack(rows).astype(jnp.float32)

def conv_act(extended, weight, bias, masks):
    count = masks.shape[1]
    total = bias[None, :] + weight[KCONV - 1][None, :] * extended[KCONV - 1:]
    for shift in range(1, KCONV):
        window = lax.slice_in_dim(extended, KCONV - 1 - shift, KCONV - 1 - shift + count, axis=0)
        total = total + weight[KCONV - 1 - shift][None, :] * window * masks[shift - 1][:, None]
    return jax.nn.silu(total)

def mixer_layer(hidden, params, starts, valid):
    norm_gain, w_gate, w_xbc, w_dt, conv_weight, conv_bias, dt_bias, a_log, skip_weight, gate_gain, w_out = params
    count = hidden.shape[0]
    spans = count // SPAN
    normed = low(rms_scale(hidden, norm_gain))
    gate = low_back(jnp.dot(normed, w_gate, precision=highest))
    conv_in = low(low_back(jnp.dot(normed, w_xbc, precision=highest)))
    dt_raw = low_back(jnp.dot(normed, w_dt, precision=highest))
    extended = jnp.concatenate([jnp.zeros((KCONV - 1, XBC), jnp.float32), conv_in], axis=0)
    activated = conv_act(extended, conv_weight, conv_bias, tap_masks(starts, count))
    inputs = activated[:, :INNER]
    input_heads = inputs.reshape(spans, SPAN, HEADS, HEAD_DIM)
    rounded_in = low(input_heads)
    keys = low(activated[:, INNER:INNER + STATE]).reshape(spans, SPAN, STATE)
    queries = low(activated[:, INNER + STATE:]).reshape(spans, SPAN, STATE)
    step_size = jax.nn.softplus(dt_raw + dt_bias) * valid[:, None]
    decay = -jnp.exp(a_log) * step_size
    step_spans = step_size.reshape(spans, SPAN, HEADS)
    cumulative = jnp.cumsum(decay.reshape(spans, SPAN, HEADS), axis=1)
    scores = low_back(jnp.einsum('cin,cjn->cij', queries, keys, precision=highest))
    lower = jnp.arange(SPAN)[:, None] >= jnp.arange(SPAN)[None, :]
    along = jnp.transpose(cumulative, (0, 2, 1))
    spread = along[:, :, :, None] - along[:, :, None, :]
    factor = jnp.exp(jnp.where(lower, spread, 0.0)) * lower
    step_cols = jnp.transpose(step_spans, (0, 2, 1))
    mixing = low(scores[:, None] * factor * step_cols[:, :, None, :])
    diag_out = low_back(jnp.einsum('chij,cjhp->cihp', mixing, rounded_in, precision=highest))
    tail = jnp.exp(cumulative[:, -1:, :] - cumulative) * step_spans
    weighted = low(rounded_in * tail[..., None])
    span_state = low_back(jnp.einsum('cjhp,cjn->chpn', weighted, keys, precision=highest))
    growth = jnp.exp(cumulative[:, -1, :])
    keep = 1.0 - starts.astype(jnp.float32)

    def advance(carry, member):
        grow, kept, fresh = member
        entering = kept * carry
        return (grow[:, None, None] * entering + fresh, entering)
    _, entering = lax.scan(advance, jnp.zeros((HEADS, HEAD_DIM, STATE), jnp.float32), (growth, keep, span_state))
    carried = low(entering)
    from_state = low_back(jnp.einsum('cin,chpn->cihp', queries, carried, precision=highest))
    state_out = jnp.exp(cumulative)[..., None] * from_state
    mixed = diag_out + state_out + skip_weight[None, None, :, None] * input_heads
    mixed = mixed.reshape(count, INNER)
    normed_out = low(gated_norm(mixed, gate, gate_gain))
    return hidden + low_back(jnp.dot(normed_out, w_out, precision=highest))

def reference(tokens, starts, valid, norm_gain, w_gate, w_xbc, w_dt, conv_weight, conv_bias, dt_bias, a_log, skip_weight, gate_gain, w_out, cotangent):
    weights = tuple((member.astype(jnp.float32) for member in (norm_gain, w_gate, w_xbc, w_dt, conv_weight, conv_bias, dt_bias, a_log, skip_weight, gate_gain, w_out)))
    group_tok = TOKENS // N_DP
    blocks = tokens.astype(jnp.float32).reshape(N_DP, group_tok, D)
    flags = starts.reshape(N_DP, group_tok // SPAN)
    row_masks = valid.astype(jnp.float32).reshape(N_DP, group_tok)
    backs = cotangent.astype(jnp.float32).reshape(N_DP, group_tok, D)

    def one_group(totals, member):
        block, flag, row_mask, back = member

        def forward(block_in, params):
            hidden = block_in
            for layer_index in range(LAYERS):
                hidden = mixer_layer(hidden, tuple((param[layer_index] for param in params)), flag, row_mask)
            return hidden
        result, pullback = jax.vjp(forward, block, weights)
        grad_block, grad_params = pullback(back)
        return (jax.tree.map(jnp.add, totals, grad_params), (result, grad_block))
    zeros = jax.tree.map(jnp.zeros_like, weights)
    totals, outputs = lax.scan(one_group, zeros, (blocks, flags, row_masks, backs))
    results, grads = outputs
    return (results.reshape(TOKENS, D), grads.reshape(TOKENS, D), totals[0], totals[1], totals[2], totals[3], totals[4], totals[5], totals[6], totals[7], totals[8], totals[9], totals[10])
```

```python
from functools import partial

import jax
import jax.numpy as jnp
from jax import lax
from jax.sharding import PartitionSpec as P

INNER = 1536
HEADS = 24
HEAD_DIM = 64
STATE = 128
KCONV = 4
SPAN = 256


epsilon = 1e-05


def shifted(block, axis, distance):
    devices = range(lax.axis_size(axis))
    route = [(i - distance, i) for i in devices if i - distance in devices]
    return lax.ppermute(block, axis, route)


AXES = ("dp", "fsdp")


def radices(count):
    factors = []
    for radix in (2, 2, 2, 4):
        if count % radix == 0 and count > 1:
            factors.append(radix)
            count //= radix
    radix = 2
    while count > 1:
        while count % radix:
            radix += 1
        factors.append(radix)
        count //= radix
    return factors


class Grid:
    def __init__(self):
        self.count = lax.axis_size("dp") * lax.axis_size("fsdp")
        self.factors = radices(self.count)
        self.place = lax.axis_index("dp") * lax.axis_size("fsdp") + lax.axis_index("fsdp")
        self.strides = []
        stride = 1
        for radix in self.factors:
            self.strides.append(stride)
            stride *= radix
        self.depth = len(self.factors)

    def digit(self, k):
        return (self.place // self.strides[k]) % self.factors[k]

    def dims(self):
        return tuple(reversed(self.factors))

    def axis(self, k):
        return self.depth - 1 - k

    def swap(self, block, k):
        stride = self.strides[k]
        route = []
        for i in range(self.count):
            up = (i // stride) % 2 == 0
            route.append((i, i + stride if up else i - stride))
        return lax.ppermute(block, AXES, route)

    def hop(self, block, k, way, keep):
        stride, radix = self.strides[k], self.factors[k]
        route = []
        for i in range(self.count):
            digit = (i // stride) % radix
            if 0 <= digit + way < radix and keep(digit):
                route.append((i, i + way * stride))
        return lax.ppermute(block, AXES, route)

    def gather_step(self, block, k):
        axis, radix = self.axis(k), self.factors[k]
        digit = self.digit(k)
        if radix == 2:
            other = self.swap(block, k)
            first = jnp.where(digit == 0, block, other)
            second = jnp.where(digit == 0, other, block)
            return jnp.concatenate([first, second], axis=axis)
        before, after = [], []
        left = right = block
        for d in range(1, radix):
            left = self.hop(left, k, 1, lambda digit: digit >= d - 1)
            right = self.hop(right, k, -1, lambda digit: digit + d - 1 < radix)
            before.insert(0, left)
            after.append(right)
        line = jnp.concatenate(before + [block] + after, axis=axis)
        return lax.dynamic_slice_in_dim(line, radix - 1 - digit, radix, axis)

    def scatter_step(self, block, k, kind):
        axis, radix = self.axis(k), self.factors[k]
        digit = self.digit(k)

        def pick(index):
            index = jnp.clip(index, 0, radix - 1)
            return lax.dynamic_slice_in_dim(block, index, 1, axis)

        wide = jnp.float32
        if radix == 2:
            got = self.swap(pick(1 - digit), k)
            return (pick(digit).astype(wide) + got.astype(wide)).astype(kind)
        total = pick(digit).astype(wide)
        for way in (1, -1):
            run = None
            for d in range(radix - 1, 0, -1):
                part = pick(digit + way * d)
                if run is not None:
                    part = (part.astype(wide) + run.astype(wide)).astype(block.dtype)
                run = self.hop(part, k, way, lambda digit: 0 <= digit + way * d < radix)
            total = total + run.astype(wide)
        return total.astype(kind)

    def orders(self):
        far = list(range(self.depth - 1, 2, -1))
        if self.depth < 3:
            one = list(range(self.depth - 1, -1, -1))
            return far, one[:-1], one[:-1]
        return far, [1, 2], [2, 1]

    def sum_all(self, value):
        for k in range(self.depth):
            if self.factors[k] == 2:
                value = value + self.swap(value, k)
            else:
                value = lax.psum(value, AXES) if False else self.sum_line(value, k)
        return value

    def sum_line(self, value, k):
        stride, radix = self.strides[k], self.factors[k]
        if radix & (radix - 1):
            raise ValueError(radix)
        step = 1
        while step < radix:
            route = []
            for i in range(self.count):
                digit = (i // stride) % radix
                route.append((i, i + ((digit ^ step) - digit) * stride))
            value = value + lax.ppermute(value, AXES, route)
            step *= 2
        return value


def tied(value, *others):
    others = [o for o in others if o is not None]
    if not others:
        return value
    return lax.optimization_barrier((value, *others))[0]


def gather_weights(grid, shards_list):
    far, first, second = grid.orders()
    gathered = []
    last_far = last_near = None
    for shard in shards_list:
        rows, cols = shard.shape
        block = shard.reshape((1,) * grid.depth + shard.shape)
        block = tied(block, last_far)
        for k in far:
            block = grid.gather_step(block, k)
        last_far = block
        block = tied(block, last_near)
        cut = cols // 256 * 128
        parts = []
        for order, part in ((first, block[..., :cut]), (second, block[..., cut:])):
            for k in order:
                part = grid.gather_step(part, k)
            parts.append(part)
        last_near = parts[0]
        gathered.append(
            [grid.gather_step(p, 0).reshape(grid.count * rows, p.shape[-1]) for p in parts]
        )
    return gathered


def scatter_grads(grid, whole):
    far, first, second = grid.orders()
    rows = whole.shape[0] // grid.count
    cols = whole.shape[1]
    block = whole.reshape(grid.dims() + (rows, cols))
    cut = cols // 256 * 128
    parts = []
    for order, part in ((first, block[..., :cut]), (second, block[..., cut:])):
        part = grid.scatter_step(part, 0, jnp.bfloat16)
        for k in order:
            part = grid.scatter_step(part, k, jnp.bfloat16)
        parts.append(part)
    block = jnp.concatenate(parts, axis=-1)
    for k in reversed(far):
        block = grid.scatter_step(block, k, jnp.bfloat16 if k != far[0] else jnp.float32)
    return block.reshape(rows, cols).astype(jnp.float32)


def state_chain(growth, keep, fresh, axis, way):
    devices = lax.axis_size(axis)
    carry = jnp.zeros_like(fresh)
    for s in range(1, devices):
        leaving = (growth * carry + fresh) * keep
        at = s - 1 if way == 1 else devices - s
        got = lax.ppermute(leaving.astype(jnp.bfloat16), axis, [(at, at + way)])
        carry = carry + got.astype(jnp.float32)
    return carry


def rms_scale(hidden, gain):
    return hidden * lax.rsqrt(jnp.mean(hidden * hidden, axis=-1, keepdims=True) + epsilon) * gain


def gated_norm(mixed, gate, gain):
    return rms_scale(mixed * jax.nn.silu(gate), gain)


def tap_masks(starts, count):
    offset = jnp.arange(count) % SPAN
    begins = jnp.repeat(starts, SPAN) > 0
    rows = []
    for shift in range(1, KCONV):
        rows.append(jnp.where(jnp.logical_and(begins, offset < shift), 0.0, 1.0))
    return jnp.stack(rows).astype(jnp.float32)


def conv_act(extended, weight, bias, masks):
    count = masks.shape[1]
    total = bias[None, :] + weight[KCONV - 1][None, :] * extended[KCONV - 1 :]
    for shift in range(1, KCONV):
        window = lax.slice_in_dim(extended, KCONV - 1 - shift, KCONV - 1 - shift + count, axis=0)
        total = total + weight[KCONV - 1 - shift][None, :] * window * masks[shift - 1][:, None]
    return jax.nn.silu(total)


def layer_forward(hidden, weights, heads, starts, valid):
    norm_gain, w_gate, w_xbc, w_dt, conv_weight, conv_bias, gate_gain, w_out = weights
    dt_bias, a_log, skip_weight = heads
    count = hidden.shape[0]
    spans = count // SPAN
    norm_scale = norm_gain.astype(jnp.float32)
    normed = rms_scale(hidden, norm_scale).astype(jnp.bfloat16)
    gate = jnp.dot(normed, w_gate, preferred_element_type=jnp.float32)
    conv_in = jnp.dot(normed, w_xbc, preferred_element_type=jnp.float32).astype(jnp.bfloat16)
    dt_raw = jnp.dot(normed, w_dt, preferred_element_type=jnp.float32)
    rim = shifted(conv_in[count - (KCONV - 1) :], "fsdp", 1)
    extended = jnp.concatenate([rim, conv_in], axis=0).astype(jnp.float32)
    masks = tap_masks(starts, count)
    conv_kernel = conv_weight.astype(jnp.float32)
    conv_offset = conv_bias.astype(jnp.float32)
    activated = conv_act(extended, conv_kernel, conv_offset, masks)
    input_heads = activated[:, :INNER].reshape(spans, SPAN, HEADS, HEAD_DIM)
    rounded_in = input_heads.astype(jnp.bfloat16)
    keys = activated[:, INNER : INNER + STATE].astype(jnp.bfloat16).reshape(spans, SPAN, STATE)
    queries = activated[:, INNER + STATE :].astype(jnp.bfloat16).reshape(spans, SPAN, STATE)
    valid_rows = valid.astype(jnp.float32)
    step_size = jax.nn.softplus(dt_raw + dt_bias) * valid_rows[:, None]
    decay = -jnp.exp(a_log) * step_size
    step_spans = step_size.reshape(spans, SPAN, HEADS)
    cumulative = jnp.cumsum(decay.reshape(spans, SPAN, HEADS), axis=1)
    scores = jnp.einsum("cin,cjn->cij", queries, keys, preferred_element_type=jnp.float32)
    lower = jnp.arange(SPAN)[:, None] >= jnp.arange(SPAN)[None, :]
    along = jnp.transpose(cumulative, (0, 2, 1))
    spread = along[:, :, :, None] - along[:, :, None, :]
    factor = jnp.exp(jnp.where(lower, spread, 0.0)) * lower
    step_cols = jnp.transpose(step_spans, (0, 2, 1))
    kernel = scores[:, None] * factor
    mixing = (kernel * step_cols[:, :, None, :]).astype(jnp.bfloat16)
    diag_out = jnp.einsum("chij,cjhp->cihp", mixing, rounded_in, preferred_element_type=jnp.float32)
    fade = jnp.exp(cumulative[:, -1:, :] - cumulative)
    tail = fade * step_spans
    weighted = (rounded_in * tail[..., None]).astype(jnp.bfloat16)
    span_state = jnp.einsum("cjhp,cjn->chpn", weighted, keys, preferred_element_type=jnp.float32)
    growth = jnp.exp(cumulative[:, -1, :])
    keep = 1.0 - starts.astype(jnp.float32)
    carry = state_chain((keep * growth[0])[:, None, None], 1.0, span_state[0], "fsdp", 1)
    entering = (keep * carry)[None]
    carried = entering.astype(jnp.bfloat16)
    from_state = jnp.einsum("cin,chpn->cihp", queries, carried, preferred_element_type=jnp.float32)
    rise = jnp.exp(cumulative)
    state_out = rise[..., None] * from_state
    mixed = (diag_out + state_out + skip_weight[None, None, :, None] * input_heads).reshape(
        count, INNER
    )
    gate_scale = gate_gain.astype(jnp.float32)
    normed_out = gated_norm(mixed, gate, gate_scale).astype(jnp.bfloat16)
    result = hidden + jnp.dot(normed_out, w_out, preferred_element_type=jnp.float32)
    saved = dict(
        hidden=hidden,
        norm_scale=norm_scale,
        normed=normed,
        gate=gate,
        extended=extended,
        masks=masks,
        conv_kernel=conv_kernel,
        conv_offset=conv_offset,
        input_heads=input_heads,
        rounded_in=rounded_in,
        keys=keys,
        queries=queries,
        valid_rows=valid_rows,
        dt_raw=dt_raw,
        decay=decay,
        step_cols=step_cols,
        factor=factor,
        kernel=kernel,
        mixing=mixing,
        fade=fade,
        tail=tail,
        weighted=weighted,
        growth=growth,
        keep=keep,
        entering=entering,
        carried=carried,
        rise=rise,
        state_out=state_out,
        mixed=mixed,
        gate_scale=gate_scale,
        normed_out=normed_out,
    )
    return (result, saved)


def layer_backward(grad_in, saved, weights, heads):
    norm_gain, w_gate, w_xbc, w_dt, conv_weight, conv_bias, gate_gain, w_out = weights
    dt_bias, a_log, skip_weight = heads
    hidden = saved["hidden"]
    count = hidden.shape[0]
    spans = count // SPAN
    rounded_in = saved["rounded_in"]
    keys = saved["keys"]
    queries = saved["queries"]
    out_low = grad_in.astype(jnp.bfloat16)
    grad_w_out = jnp.dot(saved["normed_out"].T, out_low, preferred_element_type=jnp.float32)
    grad_normed_out = jnp.dot(out_low, w_out.T, preferred_element_type=jnp.float32)
    _, pull_norm = jax.vjp(gated_norm, saved["mixed"], saved["gate"], saved["gate_scale"])
    grad_mixed, grad_gate, grad_gate_gain = pull_norm(grad_normed_out)
    gate_low = grad_gate.astype(jnp.bfloat16)
    grad_heads = grad_mixed.reshape(spans, SPAN, HEADS, HEAD_DIM)
    grad_skip = jnp.sum(grad_heads * saved["input_heads"], axis=(0, 1, 3))
    grad_inputs = skip_weight[None, None, :, None] * grad_heads
    diag_low = grad_heads.astype(jnp.bfloat16)
    state_low = (saved["rise"][..., None] * grad_heads).astype(jnp.bfloat16)
    grad_cum = jnp.sum(grad_heads * saved["state_out"], axis=-1)
    grad_mixing = jnp.einsum(
        "cihp,cjhp->chij", diag_low, rounded_in, preferred_element_type=jnp.float32
    )
    grad_x = jnp.einsum(
        "chij,cihp->cjhp", saved["mixing"], diag_low, preferred_element_type=jnp.float32
    )
    grad_queries = jnp.einsum(
        "cihp,chpn->cin", state_low, saved["carried"], preferred_element_type=jnp.float32
    )
    grad_entering = jnp.einsum(
        "cihp,cin->chpn", state_low, queries, preferred_element_type=jnp.float32
    )
    scaled = grad_mixing * saved["step_cols"][:, :, None, :]
    grad_scores = jnp.sum(scaled * saved["factor"], axis=1)
    grad_spread = scaled * saved["kernel"]
    grad_step_cols = jnp.sum(grad_mixing * saved["kernel"], axis=2)
    grad_cum = grad_cum + jnp.transpose(
        jnp.sum(grad_spread, axis=3) - jnp.sum(grad_spread, axis=2), (0, 2, 1)
    )
    scores_low = grad_scores.astype(jnp.bfloat16)
    grad_queries = grad_queries + jnp.einsum(
        "cij,cjn->cin", scores_low, keys, preferred_element_type=jnp.float32
    )
    grad_keys = jnp.einsum("cij,cin->cjn", scores_low, queries, preferred_element_type=jnp.float32)
    entering = saved["entering"]
    growth = saved["growth"]
    keep = saved["keep"]
    pending = state_chain(growth[0][:, None, None], keep, grad_entering[0], "fsdp", -1)
    grad_span = pending[None]
    grad_growth = jnp.sum(pending * entering[0], axis=(1, 2))[None]
    span_low = grad_span.astype(jnp.bfloat16)
    grad_weighted = jnp.einsum("chpn,cjn->cjhp", span_low, keys, preferred_element_type=jnp.float32)
    grad_keys = grad_keys + jnp.einsum(
        "cjhp,chpn->cjn", saved["weighted"], span_low, preferred_element_type=jnp.float32
    )
    tail = saved["tail"]
    grad_x = grad_x + grad_weighted * tail[..., None]
    grad_tail = jnp.sum(grad_weighted * rounded_in, axis=-1)
    grad_steps = grad_tail * saved["fade"] + jnp.transpose(grad_step_cols, (0, 2, 1))
    through_tail = grad_tail * tail
    grad_cum = grad_cum - through_tail
    grad_last = jnp.sum(through_tail, axis=1) + grad_growth * growth
    grad_cum = grad_cum.at[:, SPAN - 1, :].add(grad_last)
    grad_decay = jnp.cumsum(grad_cum[:, ::-1], axis=1)[:, ::-1].reshape(count, HEADS)
    grad_steps = grad_steps.reshape(count, HEADS) - jnp.exp(a_log) * grad_decay
    grad_a_log = jnp.sum(grad_decay * saved["decay"], axis=0)
    grad_pre = grad_steps * saved["valid_rows"][:, None] * jax.nn.sigmoid(saved["dt_raw"] + dt_bias)
    grad_dt_bias = jnp.sum(grad_pre, axis=0)
    dt_low = grad_pre.astype(jnp.bfloat16)
    grad_act = jnp.concatenate(
        [
            (grad_inputs + grad_x).reshape(count, INNER),
            grad_keys.reshape(count, STATE),
            grad_queries.reshape(count, STATE),
        ],
        axis=1,
    )
    _, pull_conv = jax.vjp(
        partial(conv_act, masks=saved["masks"]),
        saved["extended"],
        saved["conv_kernel"],
        saved["conv_offset"],
    )
    grad_ext, grad_conv_weight, grad_conv_bias = pull_conv(grad_act)
    returned = shifted(grad_ext[: KCONV - 1], "fsdp", -1)
    grad_conv_in = grad_ext[KCONV - 1 :].at[count - (KCONV - 1) :].add(returned)
    conv_low = grad_conv_in.astype(jnp.bfloat16)
    normed = saved["normed"]
    grad_normed = jnp.dot(gate_low, w_gate.T, preferred_element_type=jnp.float32)
    grad_normed = grad_normed + jnp.dot(conv_low, w_xbc.T, preferred_element_type=jnp.float32)
    grad_normed = grad_normed + jnp.dot(dt_low, w_dt.T, preferred_element_type=jnp.float32)
    grad_w_gate = jnp.dot(normed.T, gate_low, preferred_element_type=jnp.float32)
    grad_w_xbc = jnp.dot(normed.T, conv_low, preferred_element_type=jnp.float32)
    grad_w_dt = jnp.dot(normed.T, dt_low, preferred_element_type=jnp.float32)
    _, pull_rms = jax.vjp(rms_scale, hidden, saved["norm_scale"])
    grad_hidden, grad_norm_gain = pull_rms(grad_normed)
    weight_grads = (
        grad_norm_gain,
        grad_w_gate,
        grad_w_xbc,
        grad_w_dt,
        grad_conv_weight,
        grad_conv_bias,
        grad_gate_gain,
        grad_w_out,
    )
    return (grad_in + grad_hidden, weight_grads, (grad_dt_bias, grad_a_log, grad_skip))


def shards(
    tokens,
    starts,
    valid,
    norm_gain,
    w_gate,
    w_xbc,
    w_dt,
    conv_weight,
    conv_bias,
    dt_bias,
    a_log,
    skip_weight,
    gate_gain,
    w_out,
    cotangent,
):
    layers = norm_gain.shape[0]
    grid = Grid()
    count = grid.count
    rows = w_gate.shape[1]
    outer = w_out.shape[1]
    taps, chans = conv_weight.shape[1:]
    width = w_xbc.shape[2]
    small = rows + (taps + 1) * chans + outer
    small_cols = -(-small // rows)
    pad = -(HEADS + small_cols) % 128
    packs = []
    for l in range(layers):
        extra = jnp.concatenate(
            [norm_gain[l], conv_weight[l].reshape(-1), conv_bias[l], gate_gain[l]]
        )
        extra = jnp.pad(extra, (0, rows * small_cols - small)).reshape(rows, small_cols)
        first = jnp.concatenate([w_xbc[l], w_dt[l], extra, jnp.zeros((rows, pad), extra.dtype)], 1)
        packs.extend([first, w_gate[l], w_out[l]])
    gathered = gather_weights(grid, packs)
    wholes = []
    for l in range(layers):
        first, gate_w, out_w = (jnp.concatenate(p, axis=1) for p in gathered[3 * l : 3 * l + 3])
        extra = first[:, width + HEADS : width + HEADS + small_cols].reshape(count, -1)
        at = rows + taps * chans
        wholes.append(
            (
                extra[:, :rows].reshape(-1),
                gate_w,
                first[:, :width],
                first[:, width : width + HEADS],
                jnp.moveaxis(extra[:, rows:at].reshape(count, taps, chans), 1, 0).reshape(taps, -1),
                extra[:, at : at + chans].reshape(-1),
                extra[:, at + chans : at + chans + outer].reshape(-1),
                out_w,
            )
        )
    hidden = tokens.astype(jnp.float32)
    saves = []
    for l in range(layers):
        heads = (dt_bias[l], a_log[l], skip_weight[l])
        hidden, saved = layer_forward(hidden, wholes[l], heads, starts, valid)
        saves.append(saved)
    grad = cotangent.astype(jnp.float32)
    owned_list = [None] * layers
    summed_list = [None] * layers
    for l in reversed(range(layers)):
        heads = (dt_bias[l], a_log[l], skip_weight[l])
        grad, weight_grads, head_grads = layer_backward(grad, saves[l], wholes[l], heads)
        (
            grad_norm_gain,
            grad_w_gate,
            grad_w_xbc,
            grad_w_dt,
            grad_conv_weight,
            grad_conv_bias,
            grad_gate_gain,
            grad_w_out,
        ) = weight_grads
        extra = jnp.concatenate(
            [
                grad_norm_gain.reshape(count, rows),
                jnp.moveaxis(grad_conv_weight.reshape(taps, count, chans), 0, 1).reshape(count, -1),
                grad_conv_bias.reshape(count, chans),
                grad_gate_gain.reshape(count, outer),
                jnp.zeros((count, rows * small_cols - small), jnp.float32),
            ],
            axis=1,
        ).reshape(count * rows, small_cols)
        first = jnp.concatenate(
            [grad_w_xbc, grad_w_dt, extra, jnp.zeros((count * rows, pad), jnp.float32)], axis=1
        ).astype(jnp.bfloat16)
        out_part = scatter_grads(grid, grad_w_out.astype(jnp.bfloat16))
        gate_part = scatter_grads(grid, grad_w_gate.astype(jnp.bfloat16))
        first_part = scatter_grads(grid, first)
        extra = first_part[:, width + HEADS : width + HEADS + small_cols].reshape(-1)
        at = rows + taps * chans
        owned_list[l] = (
            extra[:rows],
            gate_part,
            first_part[:, :width],
            first_part[:, width : width + HEADS],
            extra[rows:at].reshape(taps, chans),
            extra[at : at + chans],
            extra[at + chans : at + chans + outer],
            out_part,
        )
        summed_list[l] = head_grads
    sums = grid.sum_all(jnp.stack([jnp.stack(s) for s in summed_list]))
    summed_list = [tuple(sums[l, i] for i in range(3)) for l in range(layers)]

    def stacked(position, source):
        return jnp.stack([member[position] for member in source])

    return (
        hidden,
        grad,
        stacked(0, owned_list),
        stacked(1, owned_list),
        stacked(2, owned_list),
        stacked(3, owned_list),
        stacked(4, owned_list),
        stacked(5, owned_list),
        stacked(0, summed_list),
        stacked(1, summed_list),
        stacked(2, summed_list),
        stacked(6, owned_list),
        stacked(7, owned_list),
    )


def solution(mesh):
    return jax.shard_map(
        shards,
        mesh=mesh,
        in_specs=(
            P(("dp", "fsdp"), None),
            P(("dp", "fsdp")),
            P(("dp", "fsdp")),
            P(None, ("dp", "fsdp")),
            P(None, ("dp", "fsdp"), None),
            P(None, ("dp", "fsdp"), None),
            P(None, ("dp", "fsdp"), None),
            P(None, None, ("dp", "fsdp")),
            P(None, ("dp", "fsdp")),
            P(),
            P(),
            P(),
            P(None, ("dp", "fsdp")),
            P(None, ("dp", "fsdp"), None),
            P(("dp", "fsdp"), None),
        ),
        out_specs=(
            P(("dp", "fsdp"), None),
            P(("dp", "fsdp"), None),
            P(None, ("dp", "fsdp")),
            P(None, ("dp", "fsdp"), None),
            P(None, ("dp", "fsdp"), None),
            P(None, ("dp", "fsdp"), None),
            P(None, None, ("dp", "fsdp")),
            P(None, ("dp", "fsdp")),
            P(),
            P(),
            P(),
            P(None, ("dp", "fsdp")),
            P(None, ("dp", "fsdp"), None),
        ),
        check_vma=False,
    )
```

```python
import jax
import jax.numpy as jnp
from jax import lax
from jax.experimental import pallas as pl
from jax.experimental.pallas import tpu as pltpu
from jax.sharding import PartitionSpec as P

INNER = 1536
HEADS = 24
HEAD_DIM = 64
STATE = 128
KCONV = 4
SPAN = 256
XBC = INNER + 2 * STATE


epsilon = 1e-05


def shifted(block, axis, distance):
    devices = range(lax.axis_size(axis))
    route = [(i - distance, i) for i in devices if i - distance in devices]
    return lax.ppermute(block, axis, route)


AXES = ("dp", "fsdp")


def radices(count):
    factors = []
    radix = 2
    while count > 1:
        while count % radix:
            radix += 1
        factors.append(radix)
        count //= radix
    return factors


class Grid:
    def __init__(self):
        self.count = lax.axis_size("dp") * lax.axis_size("fsdp")
        self.factors = radices(self.count)
        self.place = lax.axis_index("dp") * lax.axis_size("fsdp") + lax.axis_index("fsdp")
        self.strides = []
        stride = 1
        for radix in self.factors:
            self.strides.append(stride)
            stride *= radix
        self.depth = len(self.factors)

    def digit(self, k):
        return (self.place // self.strides[k]) % self.factors[k]

    def dims(self):
        return tuple(reversed(self.factors))

    def axis(self, k):
        return self.depth - 1 - k

    def swap(self, block, k):
        stride = self.strides[k]
        route = []
        for i in range(self.count):
            up = (i // stride) % 2 == 0
            route.append((i, i + stride if up else i - stride))
        return lax.ppermute(block, AXES, route)

    def hop(self, block, k, way, keep):
        stride, radix = self.strides[k], self.factors[k]
        route = []
        for i in range(self.count):
            digit = (i // stride) % radix
            if 0 <= digit + way < radix and keep(digit):
                route.append((i, i + way * stride))
        return lax.ppermute(block, AXES, route)

    def gather_step(self, block, k):
        axis, radix = self.axis(k), self.factors[k]
        digit = self.digit(k)
        if radix == 2:
            other = self.swap(block, k)
            first = jnp.where(digit == 0, block, other)
            second = jnp.where(digit == 0, other, block)
            return jnp.concatenate([first, second], axis=axis)
        before, after = [], []
        left = right = block
        for d in range(1, radix):
            left = self.hop(left, k, 1, lambda digit: digit >= d - 1)
            right = self.hop(right, k, -1, lambda digit: digit + d - 1 < radix)
            before.insert(0, left)
            after.append(right)
        line = jnp.concatenate(before + [block] + after, axis=axis)
        return lax.dynamic_slice_in_dim(line, radix - 1 - digit, radix, axis)

    def scatter_step(self, block, k, kind):
        axis, radix = self.axis(k), self.factors[k]
        digit = self.digit(k)

        def pick(index):
            index = jnp.clip(index, 0, radix - 1)
            return lax.dynamic_slice_in_dim(block, index, 1, axis)

        wide = jnp.float32
        if radix == 2:
            got = self.swap(pick(1 - digit), k)
            return (pick(digit).astype(wide) + got.astype(wide)).astype(kind)
        total = pick(digit).astype(wide)
        for way in (1, -1):
            run = None
            for d in range(radix - 1, 0, -1):
                part = pick(digit + way * d)
                if run is not None:
                    part = (part.astype(wide) + run.astype(wide)).astype(block.dtype)
                run = self.hop(part, k, way, lambda digit: 0 <= digit + way * d < radix)
            total = total + run.astype(wide)
        return total.astype(kind)

    def orders(self):
        far = list(range(self.depth - 1, 2, -1))
        return far, ([1, 2], [2, 1])

    def sum_all(self, value):
        for k in range(self.depth):
            value = value + self.swap(value, k)
        return value


def tied(value, *others):
    others = [o for o in others if o is not None]
    if not others:
        return value
    return lax.optimization_barrier((value, *others))[0]


def gather_pack(grid, pieces, after_far, after_near):
    far, orders = grid.orders()
    rows = pieces[0].shape[0]
    block = jnp.concatenate(pieces, axis=1)
    block = tied(block.reshape((1,) * grid.depth + block.shape), after_far)
    for k in far:
        block = grid.gather_step(block, k)
    near = tied(block, after_near)
    cut = pieces[0].shape[1]
    parts = [near[..., :cut], near[..., cut:]]
    for at in range(2):
        parts = [grid.gather_step(p, order[at]) for p, order in zip(parts, orders)]
    wholes = [grid.gather_step(p, 0).reshape(-1, p.shape[-1]) for p in parts]
    return wholes, block, parts[0]


def scatter_pack(grid, wholes):
    far, orders = grid.orders()
    rows = wholes[0].shape[0] // grid.count
    parts = []
    for whole, order in zip(wholes, orders):
        part = whole.reshape(grid.dims() + (rows, whole.shape[1]))
        for k in (0, *order):
            part = grid.scatter_step(part, k, BF16)
        parts.append(part)
    cut = wholes[0].shape[1]
    block = jnp.concatenate(parts, axis=-1)
    near = list(reversed(far))
    for k in near:
        block = grid.scatter_step(block, k, F32 if k == near[-1] else BF16)
    block = block.reshape(rows, -1)
    return block[:, :cut], block[:, cut:]


def state_chain(growth, keep, fresh, axis, way):
    devices = lax.axis_size(axis)
    carry = jnp.zeros_like(fresh)
    for s in range(1, devices):
        leaving = (growth * carry + fresh) * keep
        at = s - 1 if way == 1 else devices - s
        got = lax.ppermute(leaving.astype(jnp.bfloat16), axis, [(at, at + way)])
        carry = carry + got.astype(jnp.float32)
    return carry


LANES = 128
PAIRS = INNER // LANES
F32 = jnp.float32
BF16 = jnp.bfloat16
FAR = -1e30


def dot(a, b):
    return jnp.dot(a, b, preferred_element_type=F32)


def dot_nt(a, b):
    return lax.dot_general(a, b, (((1,), (1,)), ((), ())), preferred_element_type=F32)


def flip(a):
    return a.astype(F32).T


def split3(value):
    high = value.astype(BF16)
    rest = value - high.astype(F32)
    mid = rest.astype(BF16)
    low = (rest - mid.astype(F32)).astype(BF16)
    return jnp.concatenate([high, mid, low], axis=1)


def head_sum(value, spread):
    high = value.astype(BF16)
    low = (value - high.astype(F32)).astype(BF16)
    return dot_nt(high, spread) + dot_nt(low, spread)


def lanes_of(p):
    return pl.ds(pl.multiple_of(p * LANES, LANES), LANES)


def sigmoid(v):
    return 1.0 / (1.0 + jnp.exp(-v))


def iota(shape, axis):
    return lax.broadcasted_iota(jnp.int32, shape, axis)


def call(body, outs, *args, scratch=(), flops=2e9):
    vm = pl.BlockSpec(memory_space=pltpu.VMEM)
    size = sum(a.size * a.dtype.itemsize for a in args)
    return pl.pallas_call(
        body,
        out_shape=[jax.ShapeDtypeStruct(s, d) for s, d in outs],
        in_specs=[vm] * len(args),
        out_specs=[vm] * len(outs),
        scratch_shapes=list(scratch),
        compiler_params=pltpu.CompilerParams(vmem_limit_bytes=52 * 2**20),
        cost_estimate=pl.CostEstimate(flops=int(flops), bytes_accessed=int(size), transcendentals=0),
    )(*args)


def project_body(hidden, gain, wa, wb, normed, conv_in, dt):
    h = hidden[...]
    scale = lax.rsqrt(jnp.mean(h * h, axis=-1, keepdims=True) + epsilon)
    low = (h * scale * gain[...]).astype(BF16)
    normed[...] = low
    cut = wa.shape[1]
    rest = XBC - cut
    conv_in[:, :cut] = dot(low, wa[...]).astype(BF16)
    second = dot(low, wb[...])
    conv_in[:, cut:] = second[:, :rest].astype(BF16)
    dt[...] = jnp.where(iota((SPAN, LANES), 1) < HEADS, second[:, rest : rest + LANES], 0.0)


def conv_pre(ext, weight, bias, lanes):
    total = bias[:, lanes] + weight[KCONV - 1 : KCONV, lanes] * ext[8 : 8 + SPAN, lanes]
    for s in range(1, KCONV):
        tap = weight[KCONV - 1 - s : KCONV - s, lanes]
        total = total + tap * ext[8 - s : 8 - s + SPAN, lanes]
    return total


def triangle(upper):
    i, j = iota((SPAN, SPAN), 0), iota((SPAN, SPAN), 1)
    return jnp.where((i <= j) if upper else (i >= j), 1.0, 0.0).astype(F32)


def running(mask, value):
    return jnp.dot(mask, value, precision=lax.Precision.HIGHEST, preferred_element_type=F32)


def states_body(
    conv_in, rim, weight, bias, dt, dt_bias, a_log, valid, spread,
    x, keys, queries, step, cum, fresh, growth, ext, wide,
):
    ext[:8] = rim[...].astype(F32)
    ext[8:] = conv_in[...].astype(F32)

    def act(lanes):
        pre = conv_pre(ext, weight, bias, lanes)
        return (pre * sigmoid(pre)).astype(BF16)

    keys[...] = act(pl.ds(INNER, LANES))
    queries[...] = act(pl.ds(INNER + LANES, LANES))
    raw = dt[...] + dt_bias[...]
    size = jnp.maximum(raw, 0.0) + jnp.log1p(jnp.exp(-jnp.abs(raw)))
    size = jnp.where(iota((SPAN, LANES), 1) < HEADS, size * valid[...], 0.0)
    step[...] = size
    total = running(triangle(False), -jnp.exp(a_log[...]) * size)
    cum[...] = total
    last = total[SPAN - 1 :]
    tail = jnp.exp(last - total) * size
    wide[...] = split3(tail)
    grow = split3(jnp.broadcast_to(jnp.exp(last), (8, LANES)))
    turned = flip(keys[...]).astype(BF16)

    def pair(p, carry):
        lanes = lanes_of(p)
        low = act(lanes)
        x[:, lanes] = low
        weighted = (low.astype(F32) * dot(wide[...], spread[:, lanes])).astype(BF16)
        fresh[:, lanes] = dot(turned, weighted)
        growth[:, lanes] = dot(grow, spread[:, lanes])
        return carry

    lax.fori_loop(0, PAIRS, pair, 0)


def diag_body(x, keys, queries, step, cum, skip, spread, y, scores, cum_t, step_t, wide):
    scores[...] = dot_nt(queries[...], keys[...])
    cum_t[...] = cum[...].T
    step_t[...] = step[...].T
    wide[...] = split3(cum[...])
    half = SPAN // 2

    def pair(p, carry):
        lanes = lanes_of(p)
        xp = x[:, lanes]
        col = dot(wide[...], spread[:, lanes])
        turned = pltpu.roll(col, HEAD_DIM, 1)
        first = iota((SPAN, LANES), 1) < HEAD_DIM
        both = []
        for k in range(2):
            c = jnp.where(first, col, turned) if k == 0 else jnp.where(first, turned, col)
            row = cum_t[pl.ds(2 * p + k, 1), :]
            steps = step_t[pl.ds(2 * p + k, 1), :]
            tri = iota((SPAN, half), 0) >= iota((SPAN, half), 1)
            f0 = jnp.exp(jnp.where(tri, c - row[:, :half], FAR))
            m0 = (scores[:, :half] * f0 * steps[:, :half]).astype(BF16)
            f1 = jnp.exp(jnp.where(tri[:half], c[half:] - row[:, half:], FAR))
            m1 = (scores[half:, half:] * f1 * steps[:, half:]).astype(BF16)
            d0 = dot(m0, xp[:half])
            d1 = dot(m1, xp[half:])
            both.append(jnp.concatenate([d0[:half], d0[half:] + d1], axis=0))
        y[:, lanes] = jnp.where(first, both[0], both[1]) + skip[:, lanes] * xp.astype(F32)
        return carry

    lax.fori_loop(0, PAIRS, pair, 0)


def finish_body(y, gate, queries, carried, cum, gain, w_out, hidden, spread, mixed, normed_out, result, wide, total, gated):
    wide[...] = split3(jnp.exp(cum[...]))
    total[...] = jnp.zeros_like(total)

    def mix(p, carry):
        lanes = lanes_of(p)
        rise = dot(wide[...], spread[:, lanes])
        m = y[:, lanes] + rise * dot(queries[...], carried[:, lanes])
        mixed[:, lanes] = m
        g = gate[:, lanes]
        v = m * (g * sigmoid(g))
        gated[:, lanes] = v
        total[...] += v * v
        return carry

    lax.fori_loop(0, PAIRS, mix, 0)
    mean = jnp.sum(total[...], axis=1, keepdims=True) * (1.0 / INNER)
    scale = lax.rsqrt(mean + epsilon)

    def norm(p, carry):
        lanes = lanes_of(p)
        normed_out[:, lanes] = (gated[:, lanes] * scale * gain[:, lanes]).astype(BF16)
        return carry

    lax.fori_loop(0, PAIRS, norm, 0)
    result[...] = hidden[...] + dot(normed_out[...], w_out[...])


def open_body(
    grad, w_out, mixed, gate, gain, queries, carried, cum, x, spread,
    gain_grad, gate_low, diag_low, entering_grad, query_grad, cum_grad, skip_grad, wide, square, cross, back,
):
    out_low = grad[...].astype(BF16)
    square[...] = jnp.zeros_like(square)
    cross[...] = jnp.zeros_like(cross)
    query_grad[...] = jnp.zeros_like(query_grad)
    cum_grad[...] = jnp.zeros_like(cum_grad)
    wide[...] = split3(jnp.exp(cum[...]))

    def first(p, carry):
        lanes = lanes_of(p)
        g = dot_nt(out_low, w_out[lanes, :])
        back[:, lanes] = g
        a = gate[:, lanes]
        v = mixed[:, lanes] * (a * sigmoid(a))
        square[...] += v * v
        cross[...] += v * (g * gain[:, lanes])
        return carry

    lax.fori_loop(0, PAIRS, first, 0)
    scale = lax.rsqrt(jnp.sum(square[...], axis=1, keepdims=True) * (1.0 / INNER) + epsilon)
    share = jnp.sum(cross[...], axis=1, keepdims=True) * (1.0 / INNER) * scale * scale * scale
    turned = flip(queries[...]).astype(BF16)

    def second(p, carry):
        lanes = lanes_of(p)
        g = back[:, lanes]
        a = gate[:, lanes]
        s = sigmoid(a)
        act = a * s
        m = mixed[:, lanes]
        v = m * act
        gain_grad[:, lanes] = jnp.sum(g * v * scale, axis=0, keepdims=True)
        dv = scale * (g * gain[:, lanes]) - v * share
        gate_low[:, lanes] = (dv * m * (s + act * (1.0 - s))).astype(BF16)
        gm = dv * act
        diag_low[:, lanes] = gm.astype(BF16)
        skip_grad[:, lanes] = jnp.sum(gm * x[:, lanes].astype(F32), axis=0, keepdims=True)
        risen = dot(wide[...], spread[:, lanes]) * gm
        low = risen.astype(BF16)
        kept = carried[:, lanes]
        heads = spread[:LANES, lanes]
        cum_grad[...] += head_sum(risen * dot(queries[...], kept), heads)
        entering_grad[:, lanes] = dot(turned, low)
        query_grad[...] += dot_nt(low, kept)
        return carry

    lax.fori_loop(0, PAIRS, second, 0)


def pairs_body(
    diag_low, x, keys, queries, step, cum, skip, spread, query_in,
    x_grad, key_grad, query_grad, step_grad, row_grad, scores, score_grad, cum_t, wide, wide_step,
):
    scores[...] = dot_nt(keys[...], queries[...])
    score_grad[...] = jnp.zeros_like(score_grad)
    step_grad[...] = jnp.zeros_like(step_grad)
    row_grad[...] = jnp.zeros_like(row_grad)
    cum_t[...] = cum[...].T
    wide[...] = split3(cum[...])
    wide_step[...] = split3(step[...])
    half = SPAN // 2

    def pair(p, carry):
        lanes = lanes_of(p)
        xp = x[:, lanes]
        dp = diag_low[:, lanes]
        first = iota((SPAN, LANES), 1) < HEAD_DIM
        col = dot(wide[...], spread[:, lanes])
        col_turned = pltpu.roll(col, HEAD_DIM, 1)
        stp = dot(wide_step[...], spread[:, lanes])
        stp_turned = pltpu.roll(stp, HEAD_DIM, 1)
        both = []
        for k in range(2):
            mine = first if k == 0 else jnp.logical_not(first)
            c = jnp.where(mine, col, col_turned)
            st = jnp.where(mine, stp, stp_turned)
            row = cum_t[pl.ds(2 * p + k, 1), :]
            tri = iota((SPAN, half), 0) <= iota((SPAN, half), 1) + half
            xk = jnp.where(mine, xp.astype(F32), 0.0).astype(BF16)
            g1 = dot_nt(xk, dp[half:])
            g0 = dot_nt(xk[:half], dp[:half])
            f1 = jnp.exp(jnp.where(tri, row[:, half:] - c, FAR))
            f0 = jnp.exp(jnp.where(tri[half:], row[:, :half] - c[:half], FAR))
            w1, w0 = g1 * f1, g0 * f0
            s1, s0 = scores[:, half:], scores[:half, :half]
            st0 = st[:half]
            score_grad[:, half:] += w1 * st
            score_grad[:half, :half] += w0 * st0
            q1, q0 = w1 * s1, w0 * s0
            each = jnp.sum(q1, axis=1, keepdims=True)
            each = jnp.concatenate(
                [each[:half] + jnp.sum(q0, axis=1, keepdims=True), each[half:]], axis=0
            )
            step_grad[...] += jnp.where(iota((SPAN, LANES), 1) == 2 * p + k, each, 0.0)
            across = jnp.concatenate(
                [
                    jnp.sum(q0 * st0, axis=0, keepdims=True),
                    jnp.sum(q1 * st, axis=0, keepdims=True),
                ],
                axis=1,
            )
            row_grad[pl.ds(2 * p + k, 1), :] = across
            m1 = (s1 * f1 * st).astype(BF16)
            m0 = (s0 * f0 * st0).astype(BF16)
            top = dot(m1, dp[half:])
            low = dot(m0, dp[:half])
            both.append(jnp.concatenate([top[:half] + low, top[half:]], axis=0))
        x_grad[:, lanes] = jnp.where(first, both[0], both[1]) + skip[:, lanes] * dp.astype(F32)
        return carry

    lax.fori_loop(0, PAIRS, pair, 0)
    low = score_grad[...].astype(BF16)
    key_grad[...] = dot(low, queries[...])
    query_grad[...] = query_in[...] + dot(score_grad[...].T.astype(BF16), keys[...])


def close_body(
    pending, carried, keys, x, step, cum, x_grad, key_in, query_grad, step_in, row_grad, cum_in,
    conv_in, rim, weight, bias, dt, dt_bias, a_log, valid, spread,
    act_grad, dt_low, dt_bias_grad, a_log_grad, bias_grad, weight_grad,
    ext, wide, tail_grad, grow_grad, key_grad,
):
    ext[:8] = rim[...].astype(F32)
    ext[8:] = conv_in[...].astype(F32)
    total = cum[...]
    size = step[...]
    last = total[SPAN - 1 :]
    fade = jnp.exp(last - total)
    tail = fade * size
    wide[...] = split3(tail)
    tail_grad[...] = jnp.zeros_like(tail_grad)
    grow_grad[...] = jnp.zeros_like(grow_grad)
    key_grad[...] = key_in[...]

    def through(lanes, grad):
        pre = conv_pre(ext, weight, bias, lanes)
        s = sigmoid(pre)
        ga = grad * (s * (1.0 + pre * (1.0 - s)))
        act_grad[:, lanes] = ga
        bias_grad[:, lanes] = jnp.sum(ga, axis=0, keepdims=True)
        for k in range(KCONV):
            at = 8 - (KCONV - 1 - k)
            weight_grad[k : k + 1, lanes] = jnp.sum(
                ga * ext[at : at + SPAN, lanes], axis=0, keepdims=True
            )

    def pair(p, carry):
        lanes = lanes_of(p)
        late = pending[:, lanes]
        low = late.astype(BF16)
        xp = x[:, lanes].astype(F32)
        heads = spread[:LANES, lanes]
        over = dot(wide[...], spread[:, lanes])
        gw = dot(keys[...], low)
        tail_grad[...] += head_sum(gw * xp, heads)
        key_grad[...] += dot_nt((xp * over).astype(BF16), low)
        column = jnp.sum(late * carried[:, lanes].astype(F32), axis=0, keepdims=True)
        grow_grad[...] += head_sum(jnp.broadcast_to(column, (8, LANES)), heads)
        through(lanes, x_grad[:, lanes] + gw * over)
        return carry

    lax.fori_loop(0, PAIRS, pair, 0)
    through(pl.ds(INNER, LANES), key_grad[...])
    through(pl.ds(INNER + LANES, LANES), query_grad[...])
    tg = tail_grad[...]
    run = tg * tail
    cg = cum_in[...] + row_grad[...].T - size * step_in[...] - run
    end = jnp.sum(run, axis=0, keepdims=True) + grow_grad[:1] * jnp.exp(last)
    cg = cg + jnp.where(iota((SPAN, LANES), 0) == SPAN - 1, end, 0.0)
    rate = jnp.exp(a_log[...])
    decay_grad = running(triangle(True), cg)
    sg = tg * fade + step_in[...] - rate * decay_grad
    a_log_grad[...] = jnp.sum(decay_grad * (-rate * size), axis=0, keepdims=True)
    pre_grad = sg * valid[...] * sigmoid(dt[...] + dt_bias[...])
    pre_grad = jnp.where(iota((SPAN, LANES), 1) < HEADS, pre_grad, 0.0)
    dt_bias_grad[...] = jnp.sum(pre_grad, axis=0, keepdims=True)
    dt_low[...] = pre_grad.astype(BF16)


def inward_body(act_grad, rim_grad, weight, dt_low, gate_part, wa, wb, hidden, gain, grad, first, grad_out, gain_grad, ext):
    ext[:SPAN] = act_grad[...]
    ext[SPAN:] = rim_grad[...]

    def conv(c, carry):
        lanes = lanes_of(c)
        total = weight[KCONV - 1 : KCONV, lanes] * ext[:SPAN, lanes]
        for s in range(1, KCONV):
            total = total + weight[KCONV - 1 - s : KCONV - s, lanes] * ext[s : s + SPAN, lanes]
        first[:, lanes] = total.astype(BF16)
        return carry

    lax.fori_loop(0, XBC // LANES, conv, 0)
    first[:, XBC:] = dt_low[...]
    cut = wa.shape[1]
    back = gate_part[...] + dot_nt(first[:, :cut], wa[...]) + dot_nt(first[:, cut:], wb[...])
    h = hidden[...]
    scale = lax.rsqrt(jnp.mean(h * h, axis=-1, keepdims=True) + epsilon)
    gain_grad[...] = jnp.sum(back * h * scale, axis=0, keepdims=True)
    back = back * gain[...]
    share = jnp.mean(back * h, axis=-1, keepdims=True) * scale * scale * scale
    grad_out[...] = grad[...] + back * scale - h * share


def padded(row):
    return jnp.pad(row.astype(F32), (0, LANES - row.shape[0]))[None]


def layer_forward(hidden, weights, heads, keep, valid, spread):
    norm_gain, wa, wb, w_gate, conv_weight, conv_bias, gate_gain, w_out = weights
    dt_bias, a_log, skip = heads
    count = hidden.shape[0]
    normed, conv_in, dt = call(
        project_body,
        [((count, hidden.shape[1]), BF16), ((count, XBC), BF16), ((count, LANES), F32)],
        hidden, norm_gain, wa, wb,
    )
    rim = (shifted(conv_in[count - 8 :], "fsdp", 1).astype(F32) * keep).astype(BF16)
    x, keys, queries, step, cum, fresh, growth = call(
        states_body,
        [
            ((count, INNER), BF16), ((count, STATE), BF16), ((count, STATE), BF16), ((count, LANES), F32),
            ((count, LANES), F32), ((STATE, INNER), F32), ((8, INNER), F32),
        ],
        conv_in, rim, conv_weight, conv_bias, dt, dt_bias, a_log, valid, spread,
        scratch=[pltpu.VMEM((count + 8, XBC), F32), pltpu.VMEM((count, 3 * LANES), BF16)],
        flops=5e8,
    )
    growth = growth[:1]
    carried = (keep * state_chain(keep * growth, 1.0, fresh, "fsdp", 1)).astype(BF16)
    (y,) = call(
        diag_body, [((count, INNER), F32)], x, keys, queries, step, cum, skip, spread,
        scratch=[
            pltpu.VMEM((SPAN, SPAN), F32), pltpu.VMEM((LANES, count), F32), pltpu.VMEM((LANES, count), F32),
            pltpu.VMEM((count, 3 * LANES), BF16),
        ],
        flops=4e9,
    )
    gate = dot(normed, w_gate)
    mixed, normed_out, result = call(
        finish_body,
        [((count, INNER), F32), ((count, INNER), BF16), (hidden.shape, F32)],
        y, gate, queries, carried, cum, gate_gain, w_out, hidden, spread,
        scratch=[
            pltpu.VMEM((count, 3 * LANES), BF16), pltpu.VMEM((count, LANES), F32), pltpu.VMEM((count, INNER), F32),
        ],
    )
    saved = (hidden, normed, conv_in, dt, rim, x, keys, queries, step, cum, growth, carried, gate, mixed, normed_out)
    return result, saved


def layer_backward(grad, saved, weights, heads, keep, valid, spread):
    norm_gain, wa, wb, w_gate, conv_weight, conv_bias, gate_gain, w_out = weights
    dt_bias, a_log, skip = heads
    hidden, normed, conv_in, dt, rim, x, keys, queries, step, cum, growth, carried, gate, mixed, normed_out = saved
    count = hidden.shape[0]
    row = (1, INNER)
    gain_grad, gate_low, diag_low, entering_grad, query_part, cum_part, skip_grad = call(
        open_body,
        [
            (row, F32), ((count, INNER), BF16), ((count, INNER), BF16), ((STATE, INNER), F32), ((count, STATE), F32),
            ((count, LANES), F32), (row, F32),
        ],
        grad, w_out, mixed, gate, gate_gain, queries, carried, cum, x, spread,
        scratch=[
            pltpu.VMEM((count, 3 * LANES), BF16), pltpu.VMEM((count, LANES), F32), pltpu.VMEM((count, LANES), F32),
            pltpu.VMEM((count, INNER), F32),
        ],
    )
    grad_w_out = dot(normed_out.T, grad.astype(BF16)).astype(BF16)
    pending = state_chain(growth, keep, entering_grad, "fsdp", -1)
    x_grad, key_grad, query_grad, step_grad, row_grad = call(
        pairs_body,
        [
            ((count, INNER), F32), ((count, STATE), F32), ((count, STATE), F32), ((count, LANES), F32),
            ((LANES, count), F32),
        ],
        diag_low, x, keys, queries, step, cum, skip, spread, query_part,
        scratch=[
            pltpu.VMEM((SPAN, SPAN), F32), pltpu.VMEM((SPAN, SPAN), F32), pltpu.VMEM((LANES, count), F32),
            pltpu.VMEM((count, 3 * LANES), BF16), pltpu.VMEM((count, 3 * LANES), BF16),
        ],
        flops=8e9,
    )
    grad_w_gate = dot(normed.T, gate_low).astype(BF16)
    gate_part = dot(gate_low, w_gate.T)
    act_grad, dt_low, dt_bias_grad, a_log_grad, bias_grad, weight_grad = call(
        close_body,
        [
            ((count, XBC), F32), ((count, LANES), BF16), ((1, LANES), F32), ((1, LANES), F32), ((1, XBC), F32),
            ((KCONV, XBC), F32),
        ],
        pending, carried, keys, x, step, cum, x_grad, key_grad, query_grad, step_grad, row_grad, cum_part,
        conv_in, rim, conv_weight, conv_bias, dt, dt_bias, a_log, valid, spread,
        scratch=[
            pltpu.VMEM((count + 8, XBC), F32), pltpu.VMEM((count, 3 * LANES), BF16), pltpu.VMEM((count, LANES), F32),
            pltpu.VMEM((8, LANES), F32), pltpu.VMEM((count, STATE), F32),
        ],
    )
    rim_grad = shifted(act_grad[:8] * keep, "fsdp", -1)
    first, grad_out, norm_grad = call(
        inward_body,
        [((count, XBC + LANES), BF16), (hidden.shape, F32), ((1, hidden.shape[1]), F32)],
        act_grad, rim_grad, conv_weight, dt_low, gate_part, wa, wb, hidden, norm_gain, grad,
        scratch=[pltpu.VMEM((count + 8, XBC), F32)],
    )
    grad_first = dot(normed.T, first).astype(BF16)
    skip_sum = jnp.sum(skip_grad.reshape(HEADS, HEAD_DIM), axis=1)
    rows = (norm_grad[0], weight_grad, bias_grad[0], gain_grad[0])
    head_grads = jnp.stack([dt_bias_grad[0, :HEADS], a_log_grad[0, :HEADS], skip_sum])
    return grad_out, (grad_w_out, grad_w_gate, grad_first), rows, head_grads


def shards(
    tokens,
    starts,
    valid,
    norm_gain,
    w_gate,
    w_xbc,
    w_dt,
    conv_weight,
    conv_bias,
    dt_bias,
    a_log,
    skip_weight,
    gate_gain,
    w_out,
    cotangent,
):
    layers = norm_gain.shape[0]
    grid = Grid()
    count = grid.count
    rows, outer = w_gate.shape[1], w_out.shape[1]
    taps, chans = conv_weight.shape[1:]
    small = rows + (taps + 1) * chans + outer
    small_cols = -(-small // rows)
    spare = rows * small_cols - small
    pad = LANES - HEADS - small_cols
    cut = XBC // 2 // LANES * LANES
    at_small = XBC + HEADS
    firsts, seconds = [], []
    last_far = last_near = None
    for l in range(layers):
        extra = jnp.concatenate([norm_gain[l], conv_weight[l].reshape(-1), conv_bias[l], gate_gain[l]])
        extra = jnp.pad(extra, (0, spare)).reshape(rows, small_cols)
        tail = jnp.concatenate([w_xbc[l][:, cut:], w_dt[l], extra, jnp.zeros((rows, pad), BF16)], 1)
        pair, last_far, last_near = gather_pack(grid, [w_xbc[l][:, :cut], tail], last_far, last_near)
        firsts.append(pair)
        outs = w_out[l].reshape(rows, -1)
        pair, last_far, last_near = gather_pack(grid, [w_gate[l], outs], last_far, last_near)
        seconds.append(pair)
    wholes, heads = [], []
    split = rows + taps * chans
    for l in range(layers):
        wa, wb = firsts[l]
        extra = wb[:, at_small - cut : at_small - cut + small_cols].reshape(count, -1).astype(F32)
        kernel = jnp.moveaxis(extra[:, rows:split].reshape(count, taps, chans), 1, 0)
        wholes.append(
            (
                extra[:, :rows].reshape(1, -1),
                wa,
                wb,
                seconds[l][0],
                kernel.reshape(taps, -1),
                extra[:, split : split + chans].reshape(1, -1),
                extra[:, split + chans : small].reshape(1, -1),
                seconds[l][1].reshape(INNER, -1),
            )
        )
        heads.append((padded(dt_bias[l]), padded(a_log[l]), jnp.repeat(skip_weight[l], HEAD_DIM)[None]))
    spread = (iota((3 * LANES, INNER), 0) % LANES == iota((3 * LANES, INNER), 1) // HEAD_DIM).astype(BF16)
    keep = 1.0 - starts[0].astype(F32)
    valid = valid.astype(F32)[:, None]
    hidden = tokens.astype(F32)
    saves = []
    for l in range(layers):
        hidden, saved = layer_forward(hidden, wholes[l], heads[l], keep, valid, spread)
        saves.append(saved)
    grad = cotangent.astype(F32)
    owned, summed = [None] * layers, [None] * layers
    for l in reversed(range(layers)):
        grad, mats, row_grads, summed[l] = layer_backward(
            grad, saves[l], wholes[l], heads[l], keep, valid, spread
        )
        grad_w_out, grad_w_gate, grad_first = mats
        grad_norm, grad_kernel, grad_bias, grad_gain = row_grads
        gate_sum, out_sum = scatter_pack(grid, [grad_w_gate, grad_w_out.reshape(count * rows, -1)])
        extra = jnp.concatenate(
            [
                grad_norm.reshape(count, rows),
                jnp.moveaxis(grad_kernel.reshape(taps, count, chans), 0, 1).reshape(count, -1),
                grad_bias.reshape(count, chans),
                grad_gain.reshape(count, outer),
                jnp.zeros((count, spare), F32),
            ],
            axis=1,
        ).reshape(count * rows, small_cols)
        grad_first = lax.dynamic_update_slice(grad_first, extra.astype(BF16), (0, at_small))
        left, right = scatter_pack(grid, [grad_first[:, :cut], grad_first[:, cut:]])
        extra = right[:, at_small - cut : at_small - cut + small_cols].reshape(-1)
        owned[l] = (
            extra[:rows],
            gate_sum,
            jnp.concatenate([left, right[:, : XBC - cut]], axis=1),
            right[:, XBC - cut : at_small - cut],
            extra[rows:split].reshape(taps, chans),
            extra[split : split + chans],
            extra[split + chans : small],
            out_sum.reshape(outer, -1),
        )
    sums = grid.sum_all(jnp.stack(summed))

    def stacked(position):
        return jnp.stack([member[position] for member in owned])

    return (
        hidden,
        grad,
        stacked(0),
        stacked(1),
        stacked(2),
        stacked(3),
        stacked(4),
        stacked(5),
        sums[:, 0],
        sums[:, 1],
        sums[:, 2],
        stacked(6),
        stacked(7),
    )


def solution(mesh):
    return jax.shard_map(
        shards,
        mesh=mesh,
        in_specs=(
            P(("dp", "fsdp"), None),
            P(("dp", "fsdp")),
            P(("dp", "fsdp")),
            P(None, ("dp", "fsdp")),
            P(None, ("dp", "fsdp"), None),
            P(None, ("dp", "fsdp"), None),
            P(None, ("dp", "fsdp"), None),
            P(None, None, ("dp", "fsdp")),
            P(None, ("dp", "fsdp")),
            P(),
            P(),
            P(),
            P(None, ("dp", "fsdp")),
            P(None, ("dp", "fsdp"), None),
            P(("dp", "fsdp"), None),
        ),
        out_specs=(
            P(("dp", "fsdp"), None),
            P(("dp", "fsdp"), None),
            P(None, ("dp", "fsdp")),
            P(None, ("dp", "fsdp"), None),
            P(None, ("dp", "fsdp"), None),
            P(None, ("dp", "fsdp"), None),
            P(None, None, ("dp", "fsdp")),
            P(None, ("dp", "fsdp")),
            P(),
            P(),
            P(),
            P(None, ("dp", "fsdp")),
            P(None, ("dp", "fsdp"), None),
        ),
        check_vma=False,
    )
```

```python
import jax
import jax.numpy as jnp
from jax import lax
from jax.experimental import pallas as pl
from jax.experimental.pallas import tpu as pltpu
from jax.sharding import PartitionSpec as P

INNER = 1536
HEADS = 24
HEAD_DIM = 64
STATE = 128
KCONV = 4
SPAN = 256
XBC = INNER + 2 * STATE


epsilon = 1e-05


def shifted(block, axis, distance):
    devices = range(lax.axis_size(axis))
    route = [(i - distance, i) for i in devices if i - distance in devices]
    return lax.ppermute(block, axis, route)


AXES = ("dp", "fsdp")


def radices(count):
    factors = []
    radix = 2
    while count > 1:
        while count % radix:
            radix += 1
        factors.append(radix)
        count //= radix
    return factors


class Grid:
    def __init__(self):
        self.count = lax.axis_size("dp") * lax.axis_size("fsdp")
        self.factors = radices(self.count)
        self.place = lax.axis_index("dp") * lax.axis_size("fsdp") + lax.axis_index("fsdp")
        self.strides = []
        stride = 1
        for radix in self.factors:
            self.strides.append(stride)
            stride *= radix
        self.depth = len(self.factors)

    def digit(self, k):
        return (self.place // self.strides[k]) % self.factors[k]

    def dims(self):
        return tuple(reversed(self.factors))

    def axis(self, k):
        return self.depth - 1 - k

    def swap(self, block, k):
        stride = self.strides[k]
        route = []
        for i in range(self.count):
            up = (i // stride) % 2 == 0
            route.append((i, i + stride if up else i - stride))
        return lax.ppermute(block, AXES, route)

    def hop(self, block, k, way, keep):
        stride, radix = self.strides[k], self.factors[k]
        route = []
        for i in range(self.count):
            digit = (i // stride) % radix
            if 0 <= digit + way < radix and keep(digit):
                route.append((i, i + way * stride))
        return lax.ppermute(block, AXES, route)

    def gather_step(self, block, k):
        axis, radix = self.axis(k), self.factors[k]
        digit = self.digit(k)
        if radix == 2:
            other = self.swap(block, k)
            shape = block.shape[:axis] + (2,) + block.shape[axis + 1 :]
            mine = lax.broadcasted_iota(jnp.int32, shape, axis) == digit
            return jnp.where(mine, jnp.broadcast_to(block, shape), jnp.broadcast_to(other, shape))
        before, after = [], []
        left = right = block
        for d in range(1, radix):
            left = self.hop(left, k, 1, lambda digit: digit >= d - 1)
            right = self.hop(right, k, -1, lambda digit: digit + d - 1 < radix)
            before.insert(0, left)
            after.append(right)
        line = jnp.concatenate(before + [block] + after, axis=axis)
        return lax.dynamic_slice_in_dim(line, radix - 1 - digit, radix, axis)

    def scatter_step(self, block, k, kind):
        axis, radix = self.axis(k), self.factors[k]
        digit = self.digit(k)

        def pick(index):
            index = jnp.clip(index, 0, radix - 1)
            return lax.dynamic_slice_in_dim(block, index, 1, axis)

        wide = jnp.float32
        if radix == 2:
            got = self.swap(pick(1 - digit), k)
            return (pick(digit).astype(wide) + got.astype(wide)).astype(kind)
        total = pick(digit).astype(wide)
        for way in (1, -1):
            run = None
            for d in range(radix - 1, 0, -1):
                part = pick(digit + way * d)
                if run is not None:
                    part = (part.astype(wide) + run.astype(wide)).astype(block.dtype)
                run = self.hop(part, k, way, lambda digit: 0 <= digit + way * d < radix)
            total = total + run.astype(wide)
        return total.astype(kind)

    def orders(self):
        far = list(range(self.depth - 1, 2, -1))
        return far, ([1, 2], [2, 1])

    def sum_all(self, value):
        for k in range(self.depth):
            value = value + self.swap(value, k)
        return value


def tied(value, *others):
    others = [o for o in others if o is not None]
    if not others:
        return value
    return lax.optimization_barrier((value, *others))[0]


def gather_pack(grid, pieces, after_far, after_near):
    far, orders = grid.orders()
    rows = pieces[0].shape[0]
    block = jnp.concatenate([pieces[0], pieces[1].reshape(rows, -1)], axis=1)
    block = tied(block.reshape((1,) * grid.depth + block.shape), after_far)
    for k in far:
        block = grid.gather_step(block, k)
    near = tied(block, after_near)
    cut = pieces[0].shape[1]
    parts = [near[..., :cut], near[..., cut:].reshape(near.shape[:-2] + pieces[1].shape)]
    for at in range(2):
        parts = [grid.gather_step(p, order[at]) for p, order in zip(parts, orders)]
    wholes = [grid.gather_step(p, 0).reshape(-1, p.shape[-1]) for p in parts]
    return wholes, block, parts[0]


def scatter_pack(grid, wholes):
    far, orders = grid.orders()
    shapes = [(w.shape[0] // grid.count, w.shape[1]) for w in wholes]
    parts = []
    for whole, order, shape in zip(wholes, orders, shapes):
        part = whole.reshape(grid.dims() + shape)
        for k in (0, *order):
            part = grid.scatter_step(part, k, BF16)
        parts.append(part)
    rows, cut = shapes[0]
    parts[1] = parts[1].reshape(parts[1].shape[:-2] + (rows, -1))
    block = jnp.concatenate(parts, axis=-1)
    near = list(reversed(far))
    for k in near:
        block = grid.scatter_step(block, k, F32 if k == near[-1] else BF16)
    block = block.reshape(rows, -1)
    return block[:, :cut], block[:, cut:].reshape(shapes[1])


def scan_states(decay, fresh, axis, way):
    devices = lax.axis_size(axis)
    place = lax.axis_index(axis)
    if way < 0:
        place = devices - 1 - place
    rows = fresh.shape[0]
    total, lead = decay, jnp.ones_like(decay)
    carry = jnp.zeros_like(fresh)
    step = 1
    while step < devices:
        final = 2 * step >= devices
        high = (place // step) % 2 == 1
        spans = [i if way > 0 else devices - 1 - i for i in range(devices)]
        route = [(spans[i], spans[i ^ step]) for i in range(devices) if not final or not i & step]
        packed = jnp.concatenate([fresh, jnp.broadcast_to(total, (8,) + total.shape[1:])]).astype(BF16)
        got = lax.ppermute(packed, axis, route).astype(F32)
        other, other_total = got[:rows], got[rows : rows + 1]
        carry = jnp.where(high, lead * other + carry, carry)
        if not final:
            fresh = jnp.where(high, total * other + fresh, other_total * fresh + other)
            lead = jnp.where(high, lead * other_total, lead)
            total = total * other_total
        step *= 2
    return carry


LANES = 128
PAIRS = INNER // LANES
F32 = jnp.float32
BF16 = jnp.bfloat16
FAR = -1e30
UNROLL = 2


def dot(a, b):
    return jnp.dot(a, b, preferred_element_type=F32)


def dot_nt(a, b):
    return lax.dot_general(a, b, (((1,), (1,)), ((), ())), preferred_element_type=F32)


def flip(a):
    return a.astype(F32).T


def split3(value):
    high = value.astype(BF16)
    rest = value - high.astype(F32)
    mid = rest.astype(BF16)
    low = (rest - mid.astype(F32)).astype(BF16)
    return jnp.concatenate([high, mid, low], axis=1)


def head_sum(high, low, spread):
    return dot_nt(high, spread[:LANES]) + dot_nt(low, spread[:LANES])


def lanes_of(p):
    return pl.ds(pl.multiple_of(p * LANES, LANES), LANES)


def sigmoid(v):
    return 0.5 + 0.5 * jnp.tanh(0.5 * v)


def each_pair(body, group=UNROLL):
    def some(i, carry):
        for k in range(group):
            body(i * group + k)
        return carry

    lax.fori_loop(0, PAIRS // group, some, 0)


def put_split(high, low, lanes, value):
    top = value.astype(BF16)
    high[:, lanes] = top
    low[:, lanes] = (value - top.astype(F32)).astype(BF16)


def iota(shape, axis):
    return lax.broadcasted_iota(jnp.int32, shape, axis)


def call(body, outs, *args, scratch=(), flops=2e9):
    vm = pl.BlockSpec(memory_space=pltpu.VMEM)
    size = sum(a.size * a.dtype.itemsize for a in args)
    return pl.pallas_call(
        body,
        out_shape=[jax.ShapeDtypeStruct(s, d) for s, d in outs],
        in_specs=[vm] * len(args),
        out_specs=[vm] * len(outs),
        scratch_shapes=list(scratch),
        compiler_params=pltpu.CompilerParams(vmem_limit_bytes=52 * 2**20),
        cost_estimate=pl.CostEstimate(flops=int(flops), bytes_accessed=int(size), transcendentals=0),
    )(*args)


def project_body(hidden, gain, wa, wb, normed, conv_in, dt):
    h = hidden[...]
    scale = lax.rsqrt(jnp.mean(h * h, axis=-1, keepdims=True) + epsilon)
    low = (h * scale * gain[...]).astype(BF16)
    normed[...] = low
    cut = wa.shape[1]
    rest = XBC - cut
    conv_in[:, :cut] = dot(low, wa[...]).astype(BF16)
    second = dot(low, wb[...])
    conv_in[:, cut:] = second[:, :rest].astype(BF16)
    dt[...] = jnp.where(iota((SPAN, LANES), 1) < HEADS, second[:, rest : rest + LANES], 0.0)


def conv_pre(ext, weight, bias, lanes):
    total = bias[:, lanes] + weight[KCONV - 1 : KCONV, lanes] * ext[8 : 8 + SPAN, lanes]
    for s in range(1, KCONV):
        tap = weight[KCONV - 1 - s : KCONV - s, lanes]
        total = total + tap * ext[8 - s : 8 - s + SPAN, lanes]
    return total


def triangle(upper):
    i, j = iota((SPAN, SPAN), 0), iota((SPAN, SPAN), 1)
    return jnp.where((i <= j) if upper else (i >= j), 1.0, 0.0).astype(F32)


def running(mask, value):
    return jnp.dot(mask, value, precision=lax.Precision.HIGHEST, preferred_element_type=F32)


def states_body(
    conv_in, rim, weight, bias, dt, dt_bias, a_log, valid, spread,
    x, keys, queries, step, cum, fresh, growth, ext, wide, weighted,
):
    ext[:8] = rim[...].astype(F32)
    ext[8:] = conv_in[...].astype(F32)

    def act(lanes):
        pre = conv_pre(ext, weight, bias, lanes)
        return (pre * sigmoid(pre)).astype(BF16)

    keys[...] = act(pl.ds(INNER, LANES))
    queries[...] = act(pl.ds(INNER + LANES, LANES))
    raw = dt[...] + dt_bias[...]
    size = jnp.maximum(raw, 0.0) + jnp.log1p(jnp.exp(-jnp.abs(raw)))
    size = jnp.where(iota((SPAN, LANES), 1) < HEADS, size * valid[...], 0.0)
    step[...] = size
    total = running(triangle(False), -jnp.exp(a_log[...]) * size)
    cum[...] = total
    last = total[SPAN - 1 :]
    tail = jnp.exp(last - total) * size
    wide[...] = dot(split3(tail), spread[...])
    growth[...] = dot(split3(jnp.broadcast_to(jnp.exp(last), (8, LANES))), spread[...])

    def pair(p):
        lanes = lanes_of(p)
        low = act(lanes)
        x[:, lanes] = low
        weighted[:, lanes] = (low.astype(F32) * wide[:, lanes]).astype(BF16)

    each_pair(pair)
    fresh[...] = dot(flip(keys[...]).astype(BF16), weighted[...])


def diag_body(x, keys, queries, step, cum, skip, spread, y, scores, cum_t, step_t, wide):
    scores[...] = dot_nt(queries[...], keys[...])
    cum_t[...] = cum[...].T
    step_t[...] = step[...].T
    wide[...] = dot(split3(cum[...]), spread[...])
    half = SPAN // 2

    def pair(p):
        lanes = lanes_of(p)
        xp = x[:, lanes]
        col = wide[:, lanes]
        turned = pltpu.roll(col, HEAD_DIM, 1)
        first = iota((SPAN, LANES), 1) < HEAD_DIM
        both = []
        for k in range(2):
            c = jnp.where(first, col, turned) if k == 0 else jnp.where(first, turned, col)
            row = cum_t[pl.ds(2 * p + k, 1), :]
            steps = step_t[pl.ds(2 * p + k, 1), :]
            tri = iota((SPAN, half), 0) >= iota((SPAN, half), 1)
            f0 = jnp.exp(jnp.where(tri, c - row[:, :half], FAR))
            m0 = (scores[:, :half] * f0 * steps[:, :half]).astype(BF16)
            f1 = jnp.exp(jnp.where(tri[:half], c[half:] - row[:, half:], FAR))
            m1 = (scores[half:, half:] * f1 * steps[:, half:]).astype(BF16)
            d0 = dot(m0, xp[:half])
            d1 = dot(m1, xp[half:])
            both.append(jnp.concatenate([d0[:half], d0[half:] + d1], axis=0))
        y[:, lanes] = jnp.where(first, both[0], both[1]) + skip[:, lanes] * xp.astype(F32)

    each_pair(pair)


def finish_body(
    y, gate, queries, carried, cum, gain, w_out, hidden, spread, mixed, normed_out, result, wide, states, total, gated
):
    wide[...] = dot(split3(jnp.exp(cum[...])), spread[...])
    states[...] = dot(queries[...], carried[...])
    total[...] = jnp.zeros_like(total)

    def mix(p):
        lanes = lanes_of(p)
        m = y[:, lanes] + wide[:, lanes] * states[:, lanes]
        mixed[:, lanes] = m
        g = gate[:, lanes]
        v = m * (g * sigmoid(g))
        gated[:, lanes] = v
        total[...] += v * v

    each_pair(mix)
    mean = jnp.sum(total[...], axis=1, keepdims=True) * (1.0 / INNER)
    scale = lax.rsqrt(mean + epsilon)

    def norm(p):
        lanes = lanes_of(p)
        normed_out[:, lanes] = (gated[:, lanes] * scale * gain[:, lanes]).astype(BF16)

    each_pair(norm)
    result[...] = hidden[...] + dot(normed_out[...], w_out[...])


def open_body(
    grad, w_out, mixed, gate, gain, queries, carried, cum, x, spread,
    gain_grad, gate_low, diag_low, entering_grad, query_grad, cum_grad, skip_grad,
    wide, states, square, cross, back, state_low, high, low,
):
    out_low = grad[...].astype(BF16)
    square[...] = jnp.zeros_like(square)
    cross[...] = jnp.zeros_like(cross)
    wide[...] = dot(split3(jnp.exp(cum[...])), spread[...])
    states[...] = dot(queries[...], carried[...])
    back[...] = dot_nt(out_low, w_out[...])

    def first(p):
        lanes = lanes_of(p)
        a = gate[:, lanes]
        v = mixed[:, lanes] * (a * sigmoid(a))
        square[...] += v * v
        cross[...] += v * (back[:, lanes] * gain[:, lanes])

    each_pair(first)
    scale = lax.rsqrt(jnp.sum(square[...], axis=1, keepdims=True) * (1.0 / INNER) + epsilon)
    share = jnp.sum(cross[...], axis=1, keepdims=True) * (1.0 / INNER) * scale * scale * scale

    def second(p):
        lanes = lanes_of(p)
        g = back[:, lanes]
        a = gate[:, lanes]
        s = sigmoid(a)
        act = a * s
        m = mixed[:, lanes]
        v = m * act
        gain_grad[:, lanes] = jnp.sum(g * v * scale, axis=0, keepdims=True)
        dv = scale * (g * gain[:, lanes]) - v * share
        gate_low[:, lanes] = (dv * m * (s + act * (1.0 - s))).astype(BF16)
        gm = dv * act
        diag_low[:, lanes] = gm.astype(BF16)
        skip_grad[:, lanes] = jnp.sum(gm * x[:, lanes].astype(F32), axis=0, keepdims=True)
        risen = wide[:, lanes] * gm
        state_low[:, lanes] = risen.astype(BF16)
        put_split(high, low, lanes, risen * states[:, lanes])

    each_pair(second)
    cum_grad[...] = head_sum(high[...], low[...], spread)
    entering_grad[...] = dot(flip(queries[...]).astype(BF16), state_low[...])
    query_grad[...] = dot_nt(state_low[...], carried[...])


def pairs_body(
    diag_low, x, keys, queries, step, cum, skip, spread, query_in,
    x_grad, key_grad, query_grad, step_grad, row_grad, scores, score_grad, cum_t, wide, wide_step,
):
    scores[...] = dot_nt(keys[...], queries[...])
    score_grad[...] = jnp.zeros_like(score_grad)
    step_grad[...] = jnp.zeros_like(step_grad)
    row_grad[...] = jnp.zeros_like(row_grad)
    cum_t[...] = cum[...].T
    wide[...] = dot(split3(cum[...]), spread[...])
    wide_step[...] = dot(split3(step[...]), spread[...])
    half = SPAN // 2

    def pair(p):
        lanes = lanes_of(p)
        xp = x[:, lanes]
        dp = diag_low[:, lanes]
        first = iota((SPAN, LANES), 1) < HEAD_DIM
        col = wide[:, lanes]
        col_turned = pltpu.roll(col, HEAD_DIM, 1)
        stp = wide_step[:, lanes]
        stp_turned = pltpu.roll(stp, HEAD_DIM, 1)
        both = []
        for k in range(2):
            mine = first if k == 0 else jnp.logical_not(first)
            c = jnp.where(mine, col, col_turned)
            st = jnp.where(mine, stp, stp_turned)
            row = cum_t[pl.ds(2 * p + k, 1), :]
            tri = iota((SPAN, half), 0) <= iota((SPAN, half), 1) + half
            xk = jnp.where(mine, xp.astype(F32), 0.0).astype(BF16)
            g1 = dot_nt(xk, dp[half:])
            g0 = dot_nt(xk[:half], dp[:half])
            f1 = jnp.exp(jnp.where(tri, row[:, half:] - c, FAR))
            f0 = jnp.exp(jnp.where(tri[half:], row[:, :half] - c[:half], FAR))
            w1, w0 = g1 * f1, g0 * f0
            s1, s0 = scores[:, half:], scores[:half, :half]
            st0 = st[:half]
            score_grad[:, half:] += w1 * st
            score_grad[:half, :half] += w0 * st0
            q1, q0 = w1 * s1, w0 * s0
            each = jnp.sum(q1, axis=1, keepdims=True)
            each = jnp.concatenate(
                [each[:half] + jnp.sum(q0, axis=1, keepdims=True), each[half:]], axis=0
            )
            step_grad[...] += jnp.where(iota((SPAN, LANES), 1) == 2 * p + k, each, 0.0)
            across = jnp.concatenate(
                [
                    jnp.sum(q0 * st0, axis=0, keepdims=True),
                    jnp.sum(q1 * st, axis=0, keepdims=True),
                ],
                axis=1,
            )
            row_grad[pl.ds(2 * p + k, 1), :] = across
            m1 = (s1 * f1 * st).astype(BF16)
            m0 = (s0 * f0 * st0).astype(BF16)
            top = dot(m1, dp[half:])
            low = dot(m0, dp[:half])
            both.append(jnp.concatenate([top[:half] + low, top[half:]], axis=0))
        x_grad[:, lanes] = jnp.where(first, both[0], both[1]) + skip[:, lanes] * dp.astype(F32)

    each_pair(pair)
    low = score_grad[...].astype(BF16)
    key_grad[...] = dot(low, queries[...])
    query_grad[...] = query_in[...] + dot(score_grad[...].T.astype(BF16), keys[...])


def close_body(
    pending, carried, keys, x, step, cum, x_grad, key_in, query_grad, step_in, row_grad, cum_in,
    conv_in, rim, weight, bias, dt, dt_bias, a_log, valid, spread,
    act_grad, dt_low, dt_bias_grad, a_log_grad, bias_grad, weight_grad,
    ext, wide, back, weighted, column, high, low,
):
    ext[:8] = rim[...].astype(F32)
    ext[8:] = conv_in[...].astype(F32)
    total = cum[...]
    size = step[...]
    last = total[SPAN - 1 :]
    fade = jnp.exp(last - total)
    tail = fade * size
    late = pending[...].astype(BF16)
    wide[...] = dot(split3(tail), spread[...])
    back[...] = dot(keys[...], late)

    def through(lanes, grad):
        pre = conv_pre(ext, weight, bias, lanes)
        s = sigmoid(pre)
        ga = grad * (s * (1.0 + pre * (1.0 - s)))
        act_grad[:, lanes] = ga
        bias_grad[:, lanes] = jnp.sum(ga, axis=0, keepdims=True)
        for k in range(KCONV):
            at = 8 - (KCONV - 1 - k)
            weight_grad[k : k + 1, lanes] = jnp.sum(
                ga * ext[at : at + SPAN, lanes], axis=0, keepdims=True
            )

    def pair(p):
        lanes = lanes_of(p)
        xp = x[:, lanes].astype(F32)
        over = wide[:, lanes]
        gw = back[:, lanes]
        put_split(high, low, lanes, gw * xp)
        weighted[:, lanes] = (xp * over).astype(BF16)
        kept = pending[:, lanes] * carried[:, lanes].astype(F32)
        column[:, lanes] = jnp.broadcast_to(jnp.sum(kept, axis=0, keepdims=True), (8, LANES))
        through(lanes, x_grad[:, lanes] + gw * over)

    each_pair(pair)
    through(pl.ds(INNER, LANES), key_in[...] + dot_nt(weighted[...], late))
    through(pl.ds(INNER + LANES, LANES), query_grad[...])
    tg = head_sum(high[...], low[...], spread)
    top = column[...].astype(BF16)
    grow_grad = head_sum(top, (column[...] - top.astype(F32)).astype(BF16), spread)
    run = tg * tail
    cg = cum_in[...] + row_grad[...].T - size * step_in[...] - run
    end = jnp.sum(run, axis=0, keepdims=True) + grow_grad[:1] * jnp.exp(last)
    cg = cg + jnp.where(iota((SPAN, LANES), 0) == SPAN - 1, end, 0.0)
    rate = jnp.exp(a_log[...])
    decay_grad = running(triangle(True), cg)
    sg = tg * fade + step_in[...] - rate * decay_grad
    a_log_grad[...] = jnp.sum(decay_grad * (-rate * size), axis=0, keepdims=True)
    pre_grad = sg * valid[...] * sigmoid(dt[...] + dt_bias[...])
    pre_grad = jnp.where(iota((SPAN, LANES), 1) < HEADS, pre_grad, 0.0)
    dt_bias_grad[...] = jnp.sum(pre_grad, axis=0, keepdims=True)
    dt_low[...] = pre_grad.astype(BF16)


def inward_body(act_grad, rim_grad, weight, dt_low, gate_part, wa, wb, hidden, gain, grad, first, grad_out, gain_grad, ext):
    ext[:SPAN] = act_grad[...]
    ext[SPAN:] = rim_grad[...]

    def conv(c, carry):
        for k in range(2):
            lanes = lanes_of(2 * c + k)
            total = weight[KCONV - 1 : KCONV, lanes] * ext[:SPAN, lanes]
            for s in range(1, KCONV):
                total = total + weight[KCONV - 1 - s : KCONV - s, lanes] * ext[s : s + SPAN, lanes]
            first[:, lanes] = total.astype(BF16)
        return carry

    lax.fori_loop(0, XBC // LANES // 2, conv, 0)
    first[:, XBC:] = dt_low[...]
    cut = wa.shape[1]
    back = gate_part[...] + dot_nt(first[:, :cut], wa[...]) + dot_nt(first[:, cut:], wb[...])
    h = hidden[...]
    scale = lax.rsqrt(jnp.mean(h * h, axis=-1, keepdims=True) + epsilon)
    gain_grad[...] = jnp.sum(back * h * scale, axis=0, keepdims=True)
    back = back * gain[...]
    share = jnp.mean(back * h, axis=-1, keepdims=True) * scale * scale * scale
    grad_out[...] = grad[...] + back * scale - h * share


def padded(row):
    return jnp.pad(row.astype(F32), (0, LANES - row.shape[0]))[None]


def layer_forward(hidden, weights, heads, keep, valid, spread):
    norm_gain, wa, wb, w_gate, conv_weight, conv_bias, gate_gain, w_out = weights
    dt_bias, a_log, skip = heads
    count = hidden.shape[0]
    normed, conv_in, dt = call(
        project_body,
        [((count, hidden.shape[1]), BF16), ((count, XBC), BF16), ((count, LANES), F32)],
        hidden, norm_gain, wa, wb,
    )
    rim = (shifted(conv_in[count - 8 :], "fsdp", 1).astype(F32) * keep).astype(BF16)
    x, keys, queries, step, cum, fresh, growth = call(
        states_body,
        [
            ((count, INNER), BF16), ((count, STATE), BF16), ((count, STATE), BF16), ((count, LANES), F32),
            ((count, LANES), F32), ((STATE, INNER), F32), ((8, INNER), F32),
        ],
        conv_in, rim, conv_weight, conv_bias, dt, dt_bias, a_log, valid, spread,
        scratch=[
            pltpu.VMEM((count + 8, XBC), F32), pltpu.VMEM((count, INNER), F32), pltpu.VMEM((count, INNER), BF16),
        ],
        flops=5e8,
    )
    growth = growth[:1]
    carried = (keep * scan_states(keep * growth, fresh, "fsdp", 1)).astype(BF16)
    (y,) = call(
        diag_body, [((count, INNER), F32)], x, keys, queries, step, cum, skip, spread,
        scratch=[
            pltpu.VMEM((SPAN, SPAN), F32), pltpu.VMEM((LANES, count), F32), pltpu.VMEM((LANES, count), F32),
            pltpu.VMEM((count, INNER), F32),
        ],
        flops=4e9,
    )
    gate = dot(normed, w_gate)
    mixed, normed_out, result = call(
        finish_body,
        [((count, INNER), F32), ((count, INNER), BF16), (hidden.shape, F32)],
        y, gate, queries, carried, cum, gate_gain, w_out, hidden, spread,
        scratch=[
            pltpu.VMEM((count, INNER), F32), pltpu.VMEM((count, INNER), F32), pltpu.VMEM((count, LANES), F32),
            pltpu.VMEM((count, INNER), F32),
        ],
    )
    saved = (hidden, normed, conv_in, dt, rim, x, keys, queries, step, cum, growth, carried, gate, mixed, normed_out)
    return result, saved


def layer_backward(grad, saved, weights, heads, keep, valid, spread):
    norm_gain, wa, wb, w_gate, conv_weight, conv_bias, gate_gain, w_out = weights
    dt_bias, a_log, skip = heads
    hidden, normed, conv_in, dt, rim, x, keys, queries, step, cum, growth, carried, gate, mixed, normed_out = saved
    count = hidden.shape[0]
    row = (1, INNER)
    gain_grad, gate_low, diag_low, entering_grad, query_part, cum_part, skip_grad = call(
        open_body,
        [
            (row, F32), ((count, INNER), BF16), ((count, INNER), BF16), ((STATE, INNER), F32), ((count, STATE), F32),
            ((count, LANES), F32), (row, F32),
        ],
        grad, w_out, mixed, gate, gate_gain, queries, carried, cum, x, spread,
        scratch=[
            pltpu.VMEM((count, INNER), F32), pltpu.VMEM((count, INNER), F32), pltpu.VMEM((count, LANES), F32),
            pltpu.VMEM((count, LANES), F32), pltpu.VMEM((count, INNER), F32), pltpu.VMEM((count, INNER), BF16),
            pltpu.VMEM((count, INNER), BF16), pltpu.VMEM((count, INNER), BF16),
        ],
    )
    grad_w_out = dot(normed_out.T, grad.astype(BF16)).astype(BF16)
    pending = scan_states(keep * growth, keep * entering_grad, "fsdp", -1)
    x_grad, key_grad, query_grad, step_grad, row_grad = call(
        pairs_body,
        [
            ((count, INNER), F32), ((count, STATE), F32), ((count, STATE), F32), ((count, LANES), F32),
            ((LANES, count), F32),
        ],
        diag_low, x, keys, queries, step, cum, skip, spread, query_part,
        scratch=[
            pltpu.VMEM((SPAN, SPAN), F32), pltpu.VMEM((SPAN, SPAN), F32), pltpu.VMEM((LANES, count), F32),
            pltpu.VMEM((count, INNER), F32), pltpu.VMEM((count, INNER), F32),
        ],
        flops=8e9,
    )
    grad_w_gate = dot(normed.T, gate_low).astype(BF16)
    gate_part = dot(gate_low, w_gate.T)
    act_grad, dt_low, dt_bias_grad, a_log_grad, bias_grad, weight_grad = call(
        close_body,
        [
            ((count, XBC), F32), ((count, LANES), BF16), ((1, LANES), F32), ((1, LANES), F32), ((1, XBC), F32),
            ((KCONV, XBC), F32),
        ],
        pending, carried, keys, x, step, cum, x_grad, key_grad, query_grad, step_grad, row_grad, cum_part,
        conv_in, rim, conv_weight, conv_bias, dt, dt_bias, a_log, valid, spread,
        scratch=[
            pltpu.VMEM((count + 8, XBC), F32), pltpu.VMEM((count, INNER), F32), pltpu.VMEM((count, INNER), F32),
            pltpu.VMEM((count, INNER), BF16), pltpu.VMEM((8, INNER), F32), pltpu.VMEM((count, INNER), BF16),
            pltpu.VMEM((count, INNER), BF16),
        ],
    )
    rim_grad = shifted(act_grad[:8] * keep, "fsdp", -1)
    first, grad_out, norm_grad = call(
        inward_body,
        [((count, XBC + LANES), BF16), (hidden.shape, F32), ((1, hidden.shape[1]), F32)],
        act_grad, rim_grad, conv_weight, dt_low, gate_part, wa, wb, hidden, norm_gain, grad,
        scratch=[pltpu.VMEM((count + 8, XBC), F32)],
    )
    cut = wa.shape[1]
    grad_a = dot(normed.T, first[:, :cut]).astype(BF16)
    grad_b = dot(normed.T, first[:, cut:]).astype(BF16)
    skip_sum = jnp.sum(skip_grad.reshape(HEADS, HEAD_DIM), axis=1)
    rows = jnp.concatenate(
        [
            norm_grad[0],
            weight_grad.reshape(-1),
            bias_grad[0],
            gain_grad[0],
            dt_bias_grad[0],
            a_log_grad[0],
            padded(skip_sum)[0],
        ]
    )
    return grad_out, (grad_w_out, grad_w_gate, grad_a, grad_b), rows


def shards(
    tokens,
    starts,
    valid,
    norm_gain,
    w_gate,
    w_xbc,
    w_dt,
    conv_weight,
    conv_bias,
    dt_bias,
    a_log,
    skip_weight,
    gate_gain,
    w_out,
    cotangent,
):
    layers = norm_gain.shape[0]
    grid = Grid()
    count = grid.count
    rows, outer = w_gate.shape[1], w_out.shape[1]
    taps, chans = conv_weight.shape[1:]
    small = rows + (taps + 1) * chans + outer
    small_cols = -(-small // rows)
    spare = rows * small_cols - small
    pad = LANES - HEADS - small_cols
    cut = XBC // 2 // LANES * LANES
    at_small = XBC + HEADS
    firsts, seconds = [], []
    last_far = last_near = None
    for l in range(layers):
        extra = jnp.concatenate([norm_gain[l], conv_weight[l].reshape(-1), conv_bias[l], gate_gain[l]])
        extra = jnp.pad(extra, (0, spare)).reshape(rows, small_cols)
        tail = jnp.concatenate([w_xbc[l][:, cut:], w_dt[l], extra, jnp.zeros((rows, pad), BF16)], 1)
        if l == 0:
            pair, last_far, last_near = gather_pack(grid, [w_xbc[l][:, :cut], tail], last_far, last_near)
            firsts.append(pair)
            pair, last_far, last_near = gather_pack(grid, [w_gate[l], w_out[l]], last_far, last_near)
            seconds.append(pair)
            continue
        first = jnp.concatenate([w_xbc[l][:, :cut], tail], axis=1)
        outs = jnp.moveaxis(w_out[l].reshape(2, rows, -1), 0, 1).reshape(rows, -1)
        second = jnp.concatenate([w_gate[l], outs], axis=1)
        first, second = (lax.all_gather(p, AXES, axis=0, tiled=True) for p in (first, second))
        firsts.append([first[:, :cut], first[:, cut:]])
        width = w_gate.shape[2]
        outs = jnp.moveaxis(second[:, width:].reshape(count, rows, 2, -1), 2, 1)
        seconds.append([second[:, :width], outs.reshape(INNER, -1)])
    wholes, heads = [], []
    split = rows + taps * chans
    for l in range(layers):
        wa, wb = firsts[l]
        extra = wb[:, at_small - cut : at_small - cut + small_cols].reshape(count, -1).astype(F32)
        kernel = jnp.moveaxis(extra[:, rows:split].reshape(count, taps, chans), 1, 0)
        wholes.append(
            (
                extra[:, :rows].reshape(1, -1),
                wa,
                wb,
                seconds[l][0],
                kernel.reshape(taps, -1),
                extra[:, split : split + chans].reshape(1, -1),
                extra[:, split + chans : small].reshape(1, -1),
                seconds[l][1].reshape(INNER, -1),
            )
        )
        heads.append((padded(dt_bias[l]), padded(a_log[l]), jnp.repeat(skip_weight[l], HEAD_DIM)[None]))
    spread = (iota((3 * LANES, INNER), 0) % LANES == iota((3 * LANES, INNER), 1) // HEAD_DIM).astype(BF16)
    keep = 1.0 - starts[0].astype(F32)
    valid = valid.astype(F32)[:, None]
    hidden = tokens.astype(F32)
    saves = []
    for l in range(layers):
        hidden, saved = layer_forward(hidden, wholes[l], heads[l], keep, valid, spread)
        saves.append(saved)
    grad = cotangent.astype(F32)
    owned, summed = [None] * layers, [None] * layers
    for l in reversed(range(layers)):
        grad, mats, summed[l] = layer_backward(grad, saves[l], wholes[l], heads[l], keep, valid, spread)
        grad_w_out, grad_w_gate, grad_a, grad_b = mats
        if l == 0:
            gate_sum, out_sum = scatter_pack(grid, [grad_w_gate, grad_w_out])
            left, right = scatter_pack(grid, [grad_a, grad_b])
        else:
            outs = jnp.moveaxis(grad_w_out.reshape(count, 2, rows, -1), 1, 2).reshape(count * rows, -1)
            packed = jnp.concatenate([grad_a, grad_b, grad_w_gate, outs], axis=1)
            packed = lax.psum_scatter(packed, AXES, scatter_dimension=0, tiled=True).astype(F32)
            at = cut + grad_b.shape[1]
            width = grad_w_gate.shape[1]
            left, right = packed[:, :cut], packed[:, cut:at]
            gate_sum = packed[:, at : at + width]
            out_sum = jnp.moveaxis(packed[:, at + width :].reshape(rows, 2, -1), 1, 0).reshape(outer, -1)
        owned[l] = (
            gate_sum,
            jnp.concatenate([left, right[:, : XBC - cut]], axis=1),
            right[:, XBC - cut : at_small - cut],
            out_sum,
        )
    sums = grid.sum_all(jnp.stack(summed))
    at_kernel = rows * count
    at_bias = at_kernel + taps * chans * count
    at_gain = at_bias + chans * count
    at_heads = at_gain + outer * count

    def own(first, size):
        return lax.dynamic_slice_in_dim(sums, first + grid.place * size, size, 1)

    kernel_sums = sums[:, at_kernel:at_bias].reshape(layers, taps, count * chans)
    kernel_sums = lax.dynamic_slice_in_dim(kernel_sums, grid.place * chans, chans, 2)
    head_sums = sums[:, at_heads:].reshape(layers, 3, LANES)[:, :, :HEADS]

    def stacked(position):
        return jnp.stack([member[position] for member in owned])

    return (
        hidden,
        grad,
        own(0, rows),
        stacked(0),
        stacked(1),
        stacked(2),
        kernel_sums,
        own(at_bias, chans),
        head_sums[:, 0],
        head_sums[:, 1],
        head_sums[:, 2],
        own(at_gain, outer),
        stacked(3),
    )


def solution(mesh):
    return jax.shard_map(
        shards,
        mesh=mesh,
        in_specs=(
            P(("dp", "fsdp"), None),
            P(("dp", "fsdp")),
            P(("dp", "fsdp")),
            P(None, ("dp", "fsdp")),
            P(None, ("dp", "fsdp"), None),
            P(None, ("dp", "fsdp"), None),
            P(None, ("dp", "fsdp"), None),
            P(None, None, ("dp", "fsdp")),
            P(None, ("dp", "fsdp")),
            P(),
            P(),
            P(),
            P(None, ("dp", "fsdp")),
            P(None, ("dp", "fsdp"), None),
            P(("dp", "fsdp"), None),
        ),
        out_specs=(
            P(("dp", "fsdp"), None),
            P(("dp", "fsdp"), None),
            P(None, ("dp", "fsdp")),
            P(None, ("dp", "fsdp"), None),
            P(None, ("dp", "fsdp"), None),
            P(None, ("dp", "fsdp"), None),
            P(None, None, ("dp", "fsdp")),
            P(None, ("dp", "fsdp")),
            P(),
            P(),
            P(),
            P(None, ("dp", "fsdp")),
            P(None, ("dp", "fsdp"), None),
        ),
        check_vma=False,
    )
```

```python
import math

import jax
import jax.numpy as jnp
from jax import lax
from jax.experimental import pallas as pl
from jax.experimental.pallas import tpu as pltpu
from jax.sharding import PartitionSpec as P

INNER = 1536
HEADS = 24
HEAD_DIM = 64
STATE = 128
KCONV = 4
SPAN = 256
XBC = INNER + 2 * STATE


epsilon = 1e-05


def shifted(block, axis, distance):
    devices = range(lax.axis_size(axis))
    route = [(i - distance, i) for i in devices if i - distance in devices]
    return lax.ppermute(block, axis, route)


AXES = ("dp", "fsdp")


def radices(count):
    factors = []
    radix = 2
    while count > 1:
        while count % radix:
            radix += 1
        factors.append(radix)
        count //= radix
    return factors


class Grid:
    def __init__(self):
        self.count = lax.axis_size("dp") * lax.axis_size("fsdp")
        self.factors = radices(self.count)
        self.place = lax.axis_index("dp") * lax.axis_size("fsdp") + lax.axis_index("fsdp")
        self.strides = []
        stride = 1
        for radix in self.factors:
            self.strides.append(stride)
            stride *= radix
        self.depth = len(self.factors)

    def digit(self, k):
        return (self.place // self.strides[k]) % self.factors[k]

    def dims(self):
        return tuple(reversed(self.factors))

    def axis(self, k):
        return self.depth - 1 - k

    def swap(self, block, k):
        stride = self.strides[k]
        route = []
        for i in range(self.count):
            up = (i // stride) % 2 == 0
            route.append((i, i + stride if up else i - stride))
        return lax.ppermute(block, AXES, route)

    def hop(self, block, k, way, keep):
        stride, radix = self.strides[k], self.factors[k]
        route = []
        for i in range(self.count):
            digit = (i // stride) % radix
            if 0 <= digit + way < radix and keep(digit):
                route.append((i, i + way * stride))
        return lax.ppermute(block, AXES, route)

    def gather_step(self, block, k):
        axis, radix = self.axis(k), self.factors[k]
        digit = self.digit(k)
        if radix == 2:
            other = self.swap(block, k)
            shape = block.shape[:axis] + (2,) + block.shape[axis + 1 :]
            mine = lax.broadcasted_iota(jnp.int32, shape, axis) == digit
            return jnp.where(mine, jnp.broadcast_to(block, shape), jnp.broadcast_to(other, shape))
        before, after = [], []
        left = right = block
        for d in range(1, radix):
            left = self.hop(left, k, 1, lambda digit: digit >= d - 1)
            right = self.hop(right, k, -1, lambda digit: digit + d - 1 < radix)
            before.insert(0, left)
            after.append(right)
        line = jnp.concatenate(before + [block] + after, axis=axis)
        return lax.dynamic_slice_in_dim(line, radix - 1 - digit, radix, axis)

    def scatter_step(self, block, k, kind):
        axis, radix = self.axis(k), self.factors[k]
        digit = self.digit(k)

        def pick(index):
            index = jnp.clip(index, 0, radix - 1)
            return lax.dynamic_slice_in_dim(block, index, 1, axis)

        wide = jnp.float32
        if radix == 2:
            got = self.swap(pick(1 - digit), k)
            return (pick(digit).astype(wide) + got.astype(wide)).astype(kind)
        total = pick(digit).astype(wide)
        for way in (1, -1):
            run = None
            for d in range(radix - 1, 0, -1):
                part = pick(digit + way * d)
                if run is not None:
                    part = (part.astype(wide) + run.astype(wide)).astype(block.dtype)
                run = self.hop(part, k, way, lambda digit: 0 <= digit + way * d < radix)
            total = total + run.astype(wide)
        return total.astype(kind)

    def orders(self):
        far = list(range(self.depth - 1, 2, -1))
        return far, ([1, 2], [2, 1])

    def sum_all(self, value):
        for k in range(self.depth):
            value = value + self.swap(value, k)
        return value


def tied(value, *others):
    others = [o for o in others if o is not None]
    if not others:
        return value
    return lax.optimization_barrier((value, *others))[0]


def gather_pack(grid, pieces, after_far, after_near, extra=None):
    far, orders = grid.orders()
    rows = pieces[0].shape[0]
    block = jnp.concatenate([pieces[0], pieces[1].reshape(rows, -1)], axis=1)
    block = tied(block.reshape((1,) * grid.depth + block.shape), after_far)

    def along(k):
        nonlocal extra
        if extra is not None:
            extra = grid.gather_step(extra, k)

    for k in far:
        if extra is not None:
            block, extra = lax.optimization_barrier((block, extra))
        block = grid.gather_step(block, k)
        along(k)
    near = tied(block, after_near)
    cut = pieces[0].shape[1]
    parts = [near[..., :cut], near[..., cut:].reshape(near.shape[:-2] + pieces[1].shape)]
    for at in range(2):
        parts = [grid.gather_step(p, order[at]) for p, order in zip(parts, orders)]
        along(orders[0][at])
    wholes = [grid.gather_step(p, 0).reshape(-1, p.shape[-1]) for p in parts]
    along(0)
    return wholes, block, parts[0], extra


def scatter_near_step(grid, parts, at):
    _, orders = grid.orders()
    if at == 0:
        parts = [w.reshape(grid.dims() + (w.shape[0] // grid.count, w.shape[1])) for w in parts]
    return [grid.scatter_step(part, (0, *order)[at], BF16) for part, order in zip(parts, orders)]


def scatter_near(grid, parts):
    for at in range(3):
        parts = scatter_near_step(grid, parts, at)
        yield parts


def join_parts(parts):
    rows = parts[0].shape[-2]
    return jnp.concatenate([parts[0], parts[1].reshape(parts[1].shape[:-2] + (rows, -1))], axis=-1)


def split_far(block, shapes):
    rows, cut = shapes[0]
    block = block.reshape(rows, -1)
    return block[:, :cut], block[:, cut:].reshape(shapes[1])


def scatter_last(grid, wholes, ending, sums):
    far, _ = grid.orders()
    near = list(reversed(far))
    shapes = [(w.shape[0] // grid.count, w.shape[1]) for w in wholes]
    parts = list(wholes)
    rest = list(ending)

    def onward(blocks, at):
        if at < 3:
            return scatter_near_step(grid, blocks, at)
        if at > grid.depth - 1:
            return blocks
        block = join_parts(blocks) if at == 3 else blocks[0]
        k = near[at - 3]
        return [grid.scatter_step(block, k, F32 if k == near[-1] else BF16)]

    for at in range(grid.depth):
        count = len(parts)
        values = lax.optimization_barrier((*parts, *rest, sums))
        parts, rest, sums = values[:count], values[count:-1], values[-1]
        parts = onward(parts, at)
        rest = onward(rest, at + 2)
        sums = sums + grid.swap(sums, at)
    return split_far(parts[0], shapes), split_far(rest[0], [p.shape[-2:] for p in ending]), sums


def scan_states(decay, fresh, axis, way):
    devices = lax.axis_size(axis)
    place = lax.axis_index(axis)
    if way < 0:
        place = devices - 1 - place
    rows = fresh.shape[0]
    total, lead = decay, jnp.ones_like(decay)
    carry = jnp.zeros_like(fresh)
    step = 1
    while step < devices:
        final = 2 * step >= devices
        high = (place // step) % 2 == 1
        spans = [i if way > 0 else devices - 1 - i for i in range(devices)]
        route = [(spans[i], spans[i ^ step]) for i in range(devices) if not final or not i & step]
        packed = jnp.concatenate([fresh, jnp.broadcast_to(total, (8,) + total.shape[1:])]).astype(BF16)
        if final:
            yield packed
        got = lax.ppermute(packed, axis, route).astype(F32)
        other, other_total = got[:rows], got[rows : rows + 1]
        carry = jnp.where(high, lead * other + carry, carry)
        if not final:
            fresh = jnp.where(high, total * other + fresh, other_total * fresh + other)
            lead = jnp.where(high, lead * other_total, lead)
            total = total * other_total
        step *= 2
    yield carry


LANES = 128
PAIRS = INNER // LANES
F32 = jnp.float32
BF16 = jnp.bfloat16
FAR = -1e30
UNROLL = 2
VMEM_LIMIT = 52 * 2**20
VMEM_SLACK = 8 * 2**20


def dot(a, b):
    return jnp.dot(a, b, preferred_element_type=F32)


def dot_nt(a, b):
    return lax.dot_general(a, b, (((1,), (1,)), ((), ())), preferred_element_type=F32)


def flip(a):
    return a.astype(F32).T


def split3(value):
    high = value.astype(BF16)
    rest = value - high.astype(F32)
    mid = rest.astype(BF16)
    low = (rest - mid.astype(F32)).astype(BF16)
    return jnp.concatenate([high, mid, low], axis=1)


def head_sum(high, low, spread):
    return dot_nt(high, spread[:LANES]) + dot_nt(low, spread[:LANES])


def lanes_of(p):
    return pl.ds(pl.multiple_of(p * LANES, LANES), LANES)


def sigmoid(v):
    return 0.5 + 0.5 * jnp.tanh(0.5 * v)


def each_pair(body, group=UNROLL):
    def some(i, carry):
        for k in range(group):
            body(i * group + k)
        return carry

    lax.fori_loop(0, PAIRS // group, some, 0)


def put_split(high, low, lanes, value):
    top = value.astype(BF16)
    high[:, lanes] = top
    low[:, lanes] = (value - top.astype(F32)).astype(BF16)


def iota(shape, axis):
    return lax.broadcasted_iota(jnp.int32, shape, axis)


def call(body, outs, *args, scratch=(), flops=2e9):
    vm = pl.BlockSpec(memory_space=pltpu.VMEM)
    size = sum(a.size * a.dtype.itemsize for a in args)
    held = size + sum(math.prod(m) * jnp.dtype(d).itemsize for m, d in outs)
    held += sum(math.prod(m.shape) * jnp.dtype(m.dtype).itemsize for m in scratch)
    return pl.pallas_call(
        body,
        out_shape=[jax.ShapeDtypeStruct(s, d) for s, d in outs],
        in_specs=[vm] * len(args),
        out_specs=[vm] * len(outs),
        scratch_shapes=list(scratch),
        compiler_params=pltpu.CompilerParams(vmem_limit_bytes=max(VMEM_LIMIT, held + VMEM_SLACK)),
        cost_estimate=pl.CostEstimate(flops=int(flops), bytes_accessed=int(size), transcendentals=0),
    )(*args)


def project_body(hidden, gain, wa, wb, normed, conv_in, dt):
    h = hidden[...]
    scale = lax.rsqrt(jnp.mean(h * h, axis=-1, keepdims=True) + epsilon)
    low = (h * scale * gain[...]).astype(BF16)
    normed[...] = low
    cut = wa.shape[1]
    rest = XBC - cut
    conv_in[:, :cut] = dot(low, wa[...]).astype(BF16)
    second = dot(low, wb[...])
    conv_in[:, cut:] = second[:, :rest].astype(BF16)
    dt[...] = jnp.where(iota((SPAN, LANES), 1) < HEADS, second[:, rest : rest + LANES], 0.0)


def project_all_body(hidden, gain, weight, normed, conv_in, dt):
    h = hidden[...]
    scale = lax.rsqrt(jnp.mean(h * h, axis=-1, keepdims=True) + epsilon)
    low = (h * scale * gain[...]).astype(BF16)
    normed[...] = low
    conv_in[...] = dot(low, weight[:, :XBC]).astype(BF16)
    steps = dot(low, weight[:, XBC:])
    dt[...] = jnp.where(iota((SPAN, LANES), 1) < HEADS, steps, 0.0)


def conv_pre(ext, weight, bias, lanes):
    total = bias[:, lanes] + weight[KCONV - 1 : KCONV, lanes] * ext[8 : 8 + SPAN, lanes]
    for s in range(1, KCONV):
        tap = weight[KCONV - 1 - s : KCONV - s, lanes]
        total = total + tap * ext[8 - s : 8 - s + SPAN, lanes]
    return total


def triangle(upper):
    i, j = iota((SPAN, SPAN), 0), iota((SPAN, SPAN), 1)
    return jnp.where((i <= j) if upper else (i >= j), 1.0, 0.0).astype(F32)


def running(mask, value):
    return jnp.dot(mask, value, precision=lax.Precision.HIGHEST, preferred_element_type=F32)


def states_body(
    conv_in, rim, weight, bias, dt, dt_bias, a_log, valid, spread,
    x, stepped, keys, queries, step, cum, fresh, growth, ext, wide, wide_step, weighted,
):
    ext[:8] = rim[...].astype(F32)
    ext[8:] = conv_in[...].astype(F32)

    def act(lanes):
        pre = conv_pre(ext, weight, bias, lanes)
        return (pre * sigmoid(pre)).astype(BF16)

    keys[...] = act(pl.ds(INNER, LANES))
    queries[...] = act(pl.ds(INNER + LANES, LANES))
    raw = dt[...] + dt_bias[...]
    size = jnp.maximum(raw, 0.0) + jnp.log1p(jnp.exp(-jnp.abs(raw)))
    size = jnp.where(iota((SPAN, LANES), 1) < HEADS, size * valid[...], 0.0)
    step[...] = size
    total = running(triangle(False), -jnp.exp(a_log[...]) * size)
    cum[...] = total
    last = total[SPAN - 1 :]
    tail = jnp.exp(last - total) * size
    wide[...] = dot(split3(tail), spread[...])
    wide_step[...] = dot(split3(size), spread[...])
    growth[...] = dot(split3(jnp.broadcast_to(jnp.exp(last), (8, LANES))), spread[...])

    def pair(p):
        lanes = lanes_of(p)
        low = act(lanes)
        x[:, lanes] = low
        wider = low.astype(F32)
        weighted[:, lanes] = (wider * wide[:, lanes]).astype(BF16)
        stepped[:, lanes] = (wider * wide_step[:, lanes]).astype(BF16)

    each_pair(pair)
    fresh[...] = dot(flip(keys[...]).astype(BF16), weighted[...])


def diag_body(x, stepped, keys, queries, cum, skip, spread, y, scores, cum_t, wide):
    scores[...] = dot_nt(queries[...], keys[...])
    cum_t[...] = cum[...].T
    wide[...] = dot(split3(cum[...]), spread[...])
    half = SPAN // 2

    def pair(p):
        lanes = lanes_of(p)
        xp = stepped[:, lanes]
        col = wide[:, lanes]
        turned = pltpu.roll(col, HEAD_DIM, 1)
        first = iota((SPAN, LANES), 1) < HEAD_DIM
        both = []
        for k in range(2):
            c = jnp.where(first, col, turned) if k == 0 else jnp.where(first, turned, col)
            row = cum_t[pl.ds(2 * p + k, 1), :]
            tri = iota((SPAN, half), 0) >= iota((SPAN, half), 1)
            f0 = jnp.exp(jnp.where(tri, c - row[:, :half], FAR))
            f1 = jnp.exp(jnp.where(tri[:half], c[half:] - row[:, half:], FAR))
            d0 = dot((scores[:, :half] * f0).astype(BF16), xp[:half])
            d1 = dot((scores[half:, half:] * f1).astype(BF16), xp[half:])
            both.append(jnp.concatenate([d0[:half], d0[half:] + d1], axis=0))
        y[:, lanes] = jnp.where(first, both[0], both[1]) + skip[:, lanes] * x[:, lanes].astype(F32)

    each_pair(pair)


def finish_body(
    y, gate, queries, carried, cum, gain, w_out, hidden, spread, mixed, normed_out, result, wide, states, total, gated
):
    wide[...] = dot(split3(jnp.exp(cum[...])), spread[...])
    states[...] = dot(queries[...], carried[...])
    total[...] = jnp.zeros_like(total)

    def mix(p):
        lanes = lanes_of(p)
        m = y[:, lanes] + wide[:, lanes] * states[:, lanes]
        mixed[:, lanes] = m
        g = gate[:, lanes]
        v = m * (g * sigmoid(g))
        gated[:, lanes] = v
        total[...] += v * v

    each_pair(mix)
    mean = jnp.sum(total[...], axis=1, keepdims=True) * (1.0 / INNER)
    scale = lax.rsqrt(mean + epsilon)

    def norm(p):
        lanes = lanes_of(p)
        normed_out[:, lanes] = (gated[:, lanes] * scale * gain[:, lanes]).astype(BF16)

    each_pair(norm)
    result[...] = hidden[...] + dot(normed_out[...], w_out[...])


def open_body(
    grad, w_out, mixed, gate, gain, queries, carried, cum, x, skip, spread,
    gain_grad, gate_low, diag_low, entering_grad, query_grad, cum_grad, skip_grad,
    wide, square, cross, back, state_low, high, low,
):
    out_low = grad[...].astype(BF16)
    square[...] = jnp.zeros_like(square)
    cross[...] = jnp.zeros_like(cross)
    wide[...] = dot(split3(jnp.exp(cum[...])), spread[...])
    back[...] = dot_nt(out_low, w_out[...])

    def first(p):
        lanes = lanes_of(p)
        a = gate[:, lanes]
        v = mixed[:, lanes] * (a * sigmoid(a))
        square[...] += v * v
        cross[...] += v * (back[:, lanes] * gain[:, lanes])

    each_pair(first)
    scale = lax.rsqrt(jnp.sum(square[...], axis=1, keepdims=True) * (1.0 / INNER) + epsilon)
    share = jnp.sum(cross[...], axis=1, keepdims=True) * (1.0 / INNER) * scale * scale * scale

    def second(p):
        lanes = lanes_of(p)
        g = back[:, lanes]
        a = gate[:, lanes]
        s = sigmoid(a)
        act = a * s
        m = mixed[:, lanes]
        v = m * act
        gain_grad[:, lanes] = jnp.sum(g * v * scale, axis=0, keepdims=True)
        dv = scale * (g * gain[:, lanes]) - v * share
        gate_low[:, lanes] = (dv * m * (s + act * (1.0 - s))).astype(BF16)
        gm = dv * act
        rounded = gm.astype(BF16)
        diag_low[:, lanes] = rounded
        xp = x[:, lanes].astype(F32)
        skip_grad[:, lanes] = jnp.sum(gm * xp, axis=0, keepdims=True)
        state_low[:, lanes] = (wide[:, lanes] * gm).astype(BF16)
        put_split(high, low, lanes, rounded.astype(F32) * (m - skip[:, lanes] * xp))

    each_pair(second)
    cum_grad[...] = head_sum(high[...], low[...], spread)
    entering_grad[...] = dot(flip(queries[...]).astype(BF16), state_low[...])
    query_grad[...] = dot_nt(state_low[...], carried[...])


def pairs_body(
    diag_low, x, stepped, keys, queries, step, cum, skip, spread, query_in,
    x_grad, key_grad, query_grad, step_grad, col_grad,
    scores, score_grad, cum_t, wide, wide_step, high, low, col_high, col_low,
):
    scores[...] = dot_nt(keys[...], queries[...])
    score_grad[...] = jnp.zeros_like(score_grad)
    cum_t[...] = cum[...].T
    wide[...] = dot(split3(cum[...]), spread[...])
    wide_step[...] = dot(split3(step[...]), spread[...])
    half = SPAN // 2

    def pair(p):
        lanes = lanes_of(p)
        xp = stepped[:, lanes]
        dp = diag_low[:, lanes]
        first = iota((SPAN, LANES), 1) < HEAD_DIM
        col = wide[:, lanes]
        turned = pltpu.roll(col, HEAD_DIM, 1)
        both = []
        for k in range(2):
            mine = first if k == 0 else jnp.logical_not(first)
            c = jnp.where(mine, col, turned)
            row = cum_t[pl.ds(2 * p + k, 1), :]
            tri = iota((SPAN, half), 0) <= iota((SPAN, half), 1) + half
            xk = jnp.where(mine, xp.astype(F32), 0.0).astype(BF16)
            f1 = jnp.exp(jnp.where(tri, row[:, half:] - c, FAR))
            f0 = jnp.exp(jnp.where(tri[half:], row[:, :half] - c[:half], FAR))
            score_grad[:, half:] += dot_nt(xk, dp[half:]) * f1
            score_grad[:half, :half] += dot_nt(xk[:half], dp[:half]) * f0
            top = dot((scores[:, half:] * f1).astype(BF16), dp[half:])
            bottom = dot((scores[:half, :half] * f0).astype(BF16), dp[:half])
            both.append(jnp.concatenate([top[:half] + bottom, top[half:]], axis=0))
        through = jnp.where(first, both[0], both[1])
        x_grad[:, lanes] = wide_step[:, lanes] * through + skip[:, lanes] * dp.astype(F32)
        put_split(high, low, lanes, x[:, lanes].astype(F32) * through)
        put_split(col_high, col_low, lanes, xp.astype(F32) * through)

    each_pair(pair)
    step_grad[...] = head_sum(high[...], low[...], spread)
    col_grad[...] = head_sum(col_high[...], col_low[...], spread)
    key_grad[...] = dot(score_grad[...].astype(BF16), queries[...])
    query_grad[...] = query_in[...] + dot(score_grad[...].T.astype(BF16), keys[...])


def close_body(
    pending, carried, keys, x, step, cum, x_grad, key_in, query_grad, step_in, col_in, cum_in,
    conv_in, rim, weight, bias, dt, dt_bias, a_log, valid, spread,
    act_grad, dt_low, dt_bias_grad, a_log_grad, bias_grad, weight_grad,
    ext, wide, back, weighted, column, high, low,
):
    ext[:8] = rim[...].astype(F32)
    ext[8:] = conv_in[...].astype(F32)
    total = cum[...]
    size = step[...]
    last = total[SPAN - 1 :]
    fade = jnp.exp(last - total)
    tail = fade * size
    late = pending[...].astype(BF16)
    wide[...] = dot(split3(tail), spread[...])
    back[...] = dot(keys[...], late)

    def through(lanes, grad):
        pre = conv_pre(ext, weight, bias, lanes)
        s = sigmoid(pre)
        ga = grad * (s * (1.0 + pre * (1.0 - s)))
        act_grad[:, lanes] = ga
        bias_grad[:, lanes] = jnp.sum(ga, axis=0, keepdims=True)
        for k in range(KCONV):
            at = 8 - (KCONV - 1 - k)
            weight_grad[k : k + 1, lanes] = jnp.sum(
                ga * ext[at : at + SPAN, lanes], axis=0, keepdims=True
            )

    def pair(p):
        lanes = lanes_of(p)
        xp = x[:, lanes].astype(F32)
        over = wide[:, lanes]
        gw = back[:, lanes]
        put_split(high, low, lanes, gw * xp)
        weighted[:, lanes] = (xp * over).astype(BF16)
        kept = pending[:, lanes] * carried[:, lanes].astype(F32)
        column[:, lanes] = jnp.broadcast_to(jnp.sum(kept, axis=0, keepdims=True), (8, LANES))
        through(lanes, x_grad[:, lanes] + gw * over)

    each_pair(pair)
    through(pl.ds(INNER, LANES), key_in[...] + dot_nt(weighted[...], late))
    through(pl.ds(INNER + LANES, LANES), query_grad[...])
    tg = head_sum(high[...], low[...], spread)
    top = column[...].astype(BF16)
    grow_grad = head_sum(top, (column[...] - top.astype(F32)).astype(BF16), spread)
    run = tg * tail
    cg = cum_in[...] - col_in[...] - run
    end = jnp.sum(run, axis=0, keepdims=True) + grow_grad[:1] * jnp.exp(last)
    cg = cg + jnp.where(iota((SPAN, LANES), 0) == SPAN - 1, end, 0.0)
    rate = jnp.exp(a_log[...])
    decay_grad = running(triangle(True), cg)
    sg = tg * fade + step_in[...] - rate * decay_grad
    a_log_grad[...] = jnp.sum(decay_grad * (-rate * size), axis=0, keepdims=True)
    pre_grad = sg * valid[...] * sigmoid(dt[...] + dt_bias[...])
    pre_grad = jnp.where(iota((SPAN, LANES), 1) < HEADS, pre_grad, 0.0)
    dt_bias_grad[...] = jnp.sum(pre_grad, axis=0, keepdims=True)
    dt_low[...] = pre_grad.astype(BF16)


def conv_back(act_grad, rim_grad, weight, dt_low, first, ext):
    ext[:SPAN] = act_grad[...]
    ext[SPAN:] = rim_grad[...]

    def conv(c, carry):
        for k in range(2):
            lanes = lanes_of(2 * c + k)
            total = weight[KCONV - 1 : KCONV, lanes] * ext[:SPAN, lanes]
            for s in range(1, KCONV):
                total = total + weight[KCONV - 1 - s : KCONV - s, lanes] * ext[s : s + SPAN, lanes]
            first[:, lanes] = total.astype(BF16)
        return carry

    lax.fori_loop(0, XBC // LANES // 2, conv, 0)
    first[:, XBC : XBC + LANES] = dt_low[...]


def norm_back(back, hidden, gain, grad, grad_out, gain_grad):
    h = hidden[...]
    scale = lax.rsqrt(jnp.mean(h * h, axis=-1, keepdims=True) + epsilon)
    gain_grad[...] = jnp.sum(back * h * scale, axis=0, keepdims=True)
    back = back * gain[...]
    share = jnp.mean(back * h, axis=-1, keepdims=True) * scale * scale * scale
    grad_out[...] = grad[...] + back * scale - h * share


def inward_body(act_grad, rim_grad, weight, dt_low, gate_part, wa, wb, hidden, gain, grad, first, grad_out, gain_grad, ext):
    conv_back(act_grad, rim_grad, weight, dt_low, first, ext)
    cut = wa.shape[1]
    back = gate_part[...] + dot_nt(first[:, :cut], wa[...]) + dot_nt(first[:, cut:], wb[...])
    norm_back(back, hidden, gain, grad, grad_out, gain_grad)


def inward_all_body(act_grad, rim_grad, weight, dt_low, gate_part, whole, hidden, gain, grad, first, grad_out, gain_grad, ext):
    conv_back(act_grad, rim_grad, weight, dt_low, first, ext)
    norm_back(gate_part[...] + dot_nt(first[...], whole[...]), hidden, gain, grad, grad_out, gain_grad)


def padded(row):
    return jnp.pad(row.astype(F32), (0, LANES - row.shape[0]))[None]


def layer_forward(hidden, weights, heads, keep, valid, spread):
    norm_gain, w_in, conv_weight, conv_bias, gate_gain, w_out = weights
    dt_bias, a_log, skip = heads
    count = hidden.shape[0]
    outs = [((count, hidden.shape[1]), BF16), ((count, XBC), BF16), ((count, LANES), F32)]
    body = project_body if len(w_in) == 3 else project_all_body
    normed, conv_in, dt = call(body, outs, hidden, norm_gain, *w_in[:-1])
    gate = dot(normed, w_in[-1])
    rim = (shifted(conv_in[count - 8 :], "fsdp", 1).astype(F32) * keep).astype(BF16)
    x, stepped, keys, queries, step, cum, fresh, growth = call(
        states_body,
        [
            ((count, INNER), BF16), ((count, INNER), BF16), ((count, STATE), BF16), ((count, STATE), BF16), ((count, LANES), F32),
            ((count, LANES), F32), ((STATE, INNER), F32), ((8, INNER), F32),
        ],
        conv_in, rim, conv_weight, conv_bias, dt, dt_bias, a_log, valid, spread,
        scratch=[
            pltpu.VMEM((count + 8, XBC), F32), pltpu.VMEM((count, INNER), F32), pltpu.VMEM((count, INNER), F32),
            pltpu.VMEM((count, INNER), BF16),
        ],
        flops=5e8,
    )
    growth = growth[:1]
    scan = scan_states(keep * growth, fresh, "fsdp", 1)
    stepped = tied(stepped, next(scan))
    (y,) = call(
        diag_body, [((count, INNER), F32)], x, stepped, keys, queries, cum, skip, spread,
        scratch=[
            pltpu.VMEM((SPAN, SPAN), F32), pltpu.VMEM((LANES, count), F32),
            pltpu.VMEM((count, INNER), F32),
        ],
        flops=4e9,
    )
    carried = (keep * next(scan)).astype(BF16)
    mixed, normed_out, result = call(
        finish_body,
        [((count, INNER), F32), ((count, INNER), BF16), (hidden.shape, F32)],
        y, gate, queries, carried, cum, gate_gain, w_out, hidden, spread,
        scratch=[
            pltpu.VMEM((count, INNER), F32), pltpu.VMEM((count, INNER), F32), pltpu.VMEM((count, LANES), F32),
            pltpu.VMEM((count, INNER), F32),
        ],
    )
    saved = (hidden, normed, conv_in, dt, rim, x, stepped, keys, queries, step, cum, growth, carried, gate, mixed, normed_out)
    return result, saved


def layer_backward(grad, saved, weights, heads, keep, valid, spread, grid):
    norm_gain, w_in, conv_weight, conv_bias, gate_gain, w_out = weights
    dt_bias, a_log, skip = heads
    hidden, normed, conv_in, dt, rim, x, stepped, keys, queries, step, cum, growth, carried, gate, mixed, normed_out = saved
    count = hidden.shape[0]
    row = (1, INNER)
    gain_grad, gate_low, diag_low, entering_grad, query_part, cum_part, skip_grad = call(
        open_body,
        [
            (row, F32), ((count, INNER), BF16), ((count, INNER), BF16), ((STATE, INNER), F32), ((count, STATE), F32),
            ((count, LANES), F32), (row, F32),
        ],
        grad, w_out, mixed, gate, gate_gain, queries, carried, cum, x, skip, spread,
        scratch=[
            pltpu.VMEM((count, INNER), F32), pltpu.VMEM((count, LANES), F32),
            pltpu.VMEM((count, LANES), F32), pltpu.VMEM((count, INNER), F32), pltpu.VMEM((count, INNER), BF16),
            pltpu.VMEM((count, INNER), BF16), pltpu.VMEM((count, INNER), BF16),
        ],
    )
    grad_w_out = dot(normed_out.T, grad.astype(BF16)).astype(BF16)
    scan = scan_states(keep * growth, keep * entering_grad, "fsdp", -1)
    diag_low = tied(diag_low, next(scan))
    x_grad, key_grad, query_grad, step_grad, col_grad = call(
        pairs_body,
        [
            ((count, INNER), F32), ((count, STATE), F32), ((count, STATE), F32), ((count, LANES), F32),
            ((count, LANES), F32),
        ],
        diag_low, x, stepped, keys, queries, step, cum, skip, spread, query_part,
        scratch=[
            pltpu.VMEM((SPAN, SPAN), F32), pltpu.VMEM((SPAN, SPAN), F32), pltpu.VMEM((LANES, count), F32),
            pltpu.VMEM((count, INNER), F32), pltpu.VMEM((count, INNER), F32),
            *[pltpu.VMEM((count, INNER), BF16)] * 4,
        ],
        flops=8e9,
    )
    split = len(w_in) == 3
    ready, moved = None, None
    grad_w_gate = dot(normed.T, gate_low).astype(BF16)
    gate_part = dot(gate_low, w_in[-1].T)
    if split:
        steps = scatter_near(grid, [grad_w_gate, grad_w_out])
        ready = next(steps)
        x_grad = tied(x_grad, *ready)
    pending = next(scan)
    act_grad, dt_low, dt_bias_grad, a_log_grad, bias_grad, weight_grad = call(
        close_body,
        [
            ((count, XBC), F32), ((count, LANES), BF16), ((1, LANES), F32), ((1, LANES), F32), ((1, XBC), F32),
            ((KCONV, XBC), F32),
        ],
        pending, carried, keys, x, step, cum, x_grad, key_grad, query_grad, step_grad, col_grad, cum_part,
        conv_in, rim, conv_weight, conv_bias, dt, dt_bias, a_log, valid, spread,
        scratch=[
            pltpu.VMEM((count + 8, XBC), F32), pltpu.VMEM((count, INNER), F32), pltpu.VMEM((count, INNER), F32),
            pltpu.VMEM((count, INNER), BF16), pltpu.VMEM((8, INNER), F32), pltpu.VMEM((count, INNER), BF16),
            pltpu.VMEM((count, INNER), BF16),
        ],
    )
    rim_grad = shifted(act_grad[:8] * keep, "fsdp", -1)
    outs = [((count, XBC + LANES), BF16), (hidden.shape, F32), ((1, hidden.shape[1]), F32)]
    scratch = [pltpu.VMEM((count + 8, XBC), F32)]
    if split:
        ready = next(steps)
        first, grad_out, norm_grad = call(
            inward_body, outs, act_grad, rim_grad, conv_weight, dt_low, gate_part, *w_in[:2], hidden, norm_gain, grad,
            scratch=scratch,
        )
        cut = w_in[0].shape[1]
        first_grads = [dot(normed.T, first[:, :cut]).astype(BF16), dot(normed.T, first[:, cut:]).astype(BF16)]
        mats = (ready, first_grads)
    else:
        first, grad_out, norm_grad = call(
            inward_all_body, outs, act_grad, rim_grad, conv_weight, dt_low, gate_part, w_in[0], hidden, norm_gain, grad,
            scratch=scratch,
        )
        mats = (dot(normed.T, first).astype(BF16), grad_w_gate, grad_w_out)
    skip_sum = jnp.sum(skip_grad.reshape(HEADS, HEAD_DIM), axis=1)
    rows = jnp.concatenate(
        [
            norm_grad[0],
            weight_grad.reshape(-1),
            bias_grad[0],
            gain_grad[0],
            dt_bias_grad[0],
            a_log_grad[0],
            padded(skip_sum)[0],
        ]
    )
    return grad_out, mats, rows


def shards(
    tokens,
    starts,
    valid,
    norm_gain,
    w_gate,
    w_xbc,
    w_dt,
    conv_weight,
    conv_bias,
    dt_bias,
    a_log,
    skip_weight,
    gate_gain,
    w_out,
    cotangent,
):
    layers = norm_gain.shape[0]
    grid = Grid()
    count = grid.count
    rows, outer = w_gate.shape[1], w_out.shape[1]
    taps, chans = conv_weight.shape[1:]
    pad = LANES - HEADS
    cut = XBC // 2 // LANES * LANES
    small = jnp.concatenate(
        [
            v.reshape(-1)
            for l in range(layers)
            for v in (norm_gain[l], conv_weight[l], conv_bias[l], gate_gain[l])
        ]
    )
    length = small.size
    small = jnp.pad(small, (0, -length % (8 * LANES))).reshape((1,) * grid.depth + (-1, LANES))
    firsts, seconds = [], []
    hidden_width = tokens.shape[1]
    for l in range(layers):
        tail = jnp.concatenate([w_xbc[l][:, cut:], w_dt[l], jnp.zeros((rows, pad), BF16)], 1)
        if l == 0:
            pair, last_far, last_near, small = gather_pack(grid, [w_xbc[l][:, :cut], tail], None, None, small)
            firsts.append(pair)
            pair, *_ = gather_pack(grid, [w_gate[l], w_out[l]], last_far, last_near)
            seconds.append(pair)
            continue
        first = jnp.concatenate([w_xbc[l][:, :cut], tail], axis=1)
        firsts.append([lax.all_gather(first, AXES, axis=0, tiled=True)])
        second = jnp.concatenate([w_out[l], w_gate[l].reshape(outer, -1)], axis=1)
        second = lax.all_gather(second, AXES, axis=0, tiled=True)
        seconds.append([second[:, hidden_width:].reshape(hidden_width, INNER), second[:, :hidden_width]])
    small = small.reshape(count, -1)[:, :length].astype(F32)
    wholes, heads = [], []
    at = 0
    for l in range(layers):
        rest = []
        for size in (rows, taps * chans, chans, outer):
            rest.append(small[:, at : at + size])
            at += size
        w_in = firsts[l]
        kernel = jnp.moveaxis(rest[1].reshape(count, taps, chans), 1, 0)
        wholes.append(
            (
                rest[0].reshape(1, -1),
                [*w_in, seconds[l][0]],
                kernel.reshape(taps, -1),
                rest[2].reshape(1, -1),
                rest[3].reshape(1, -1),
                seconds[l][1],
            )
        )
        heads.append((padded(dt_bias[l]), padded(a_log[l]), jnp.repeat(skip_weight[l], HEAD_DIM)[None]))
    spread = (iota((3 * LANES, INNER), 0) % LANES == iota((3 * LANES, INNER), 1) // HEAD_DIM).astype(BF16)
    keep = 1.0 - starts[0].astype(F32)
    valid = valid.astype(F32)[:, None]
    hidden = tokens.astype(F32)
    saves = []
    for l in range(layers):
        hidden, saved = layer_forward(hidden, wholes[l], heads[l], keep, valid, spread)
        saves.append(saved)
    grad = cotangent.astype(F32)
    owned, summed = [None] * layers, [None] * layers
    for l in reversed(range(layers)):
        grad, mats, summed[l] = layer_backward(grad, saves[l], wholes[l], heads[l], keep, valid, spread, grid)
        if l == 0:
            sums = jnp.stack(summed)
            (left, right), (gate_sum, out_sum), sums = scatter_last(grid, mats[1], mats[0], sums)
        else:
            outs = jnp.moveaxis(mats[2].reshape(count, 2, rows, -1), 1, 2).reshape(count * rows, -1)
            packed = jnp.concatenate([mats[0], mats[1], outs], axis=1)
            packed = lax.psum_scatter(packed, AXES, scatter_dimension=0, tiled=True).astype(F32)
            at = XBC + LANES
            left, right = packed[:, :cut], packed[:, cut:at]
            gate_sum = packed[:, at : at + INNER]
            out_sum = jnp.moveaxis(packed[:, at + INNER :].reshape(rows, 2, -1), 1, 0).reshape(outer, -1)
        owned[l] = (
            gate_sum,
            jnp.concatenate([left, right[:, : XBC - cut]], axis=1),
            right[:, XBC - cut : XBC - cut + HEADS],
            out_sum,
        )
    at_kernel = rows * count
    at_bias = at_kernel + taps * chans * count
    at_gain = at_bias + chans * count
    at_heads = at_gain + outer * count

    def own(first, size):
        return lax.dynamic_slice_in_dim(sums, first + grid.place * size, size, 1)

    kernel_sums = sums[:, at_kernel:at_bias].reshape(layers, taps, count * chans)
    kernel_sums = lax.dynamic_slice_in_dim(kernel_sums, grid.place * chans, chans, 2)
    head_sums = sums[:, at_heads:].reshape(layers, 3, LANES)[:, :, :HEADS]

    def stacked(position):
        return jnp.stack([member[position] for member in owned])

    return (
        hidden,
        grad,
        own(0, rows),
        stacked(0),
        stacked(1),
        stacked(2),
        kernel_sums,
        own(at_bias, chans),
        head_sums[:, 0],
        head_sums[:, 1],
        head_sums[:, 2],
        own(at_gain, outer),
        stacked(3),
    )


def solution(mesh):
    return jax.shard_map(
        shards,
        mesh=mesh,
        in_specs=(
            P(("dp", "fsdp"), None),
            P(("dp", "fsdp")),
            P(("dp", "fsdp")),
            P(None, ("dp", "fsdp")),
            P(None, ("dp", "fsdp"), None),
            P(None, ("dp", "fsdp"), None),
            P(None, ("dp", "fsdp"), None),
            P(None, None, ("dp", "fsdp")),
            P(None, ("dp", "fsdp")),
            P(),
            P(),
            P(),
            P(None, ("dp", "fsdp")),
            P(None, ("dp", "fsdp"), None),
            P(("dp", "fsdp"), None),
        ),
        out_specs=(
            P(("dp", "fsdp"), None),
            P(("dp", "fsdp"), None),
            P(None, ("dp", "fsdp")),
            P(None, ("dp", "fsdp"), None),
            P(None, ("dp", "fsdp"), None),
            P(None, ("dp", "fsdp"), None),
            P(None, None, ("dp", "fsdp")),
            P(None, ("dp", "fsdp")),
            P(),
            P(),
            P(),
            P(None, ("dp", "fsdp")),
            P(None, ("dp", "fsdp"), None),
        ),
        check_vma=False,
    )
```

```python
import math

import jax
import jax.numpy as jnp
from jax import lax
from jax.experimental import pallas as pl
from jax.experimental.pallas import tpu as pltpu
from jax.sharding import PartitionSpec as P

INNER = 1536
HEADS = 24
HEAD_DIM = 64
STATE = 128
KCONV = 4
SPAN = 256
XBC = INNER + 2 * STATE


epsilon = 1e-05


def shifted(block, axis, distance):
    devices = range(lax.axis_size(axis))
    route = [(i - distance, i) for i in devices if i - distance in devices]
    return lax.ppermute(block, axis, route)


AXES = ("dp", "fsdp")


def radices(count):
    factors = []
    radix = 2
    while count > 1:
        while count % radix:
            radix += 1
        factors.append(radix)
        count //= radix
    return factors


class Grid:
    def __init__(self):
        self.count = lax.axis_size("dp") * lax.axis_size("fsdp")
        self.factors = radices(self.count)
        self.place = lax.axis_index("dp") * lax.axis_size("fsdp") + lax.axis_index("fsdp")
        self.strides = []
        stride = 1
        for radix in self.factors:
            self.strides.append(stride)
            stride *= radix
        self.depth = len(self.factors)

    def digit(self, k):
        return (self.place // self.strides[k]) % self.factors[k]

    def dims(self):
        return tuple(reversed(self.factors))

    def axis(self, k):
        return self.depth - 1 - k

    def swap(self, block, k):
        stride = self.strides[k]
        route = []
        for i in range(self.count):
            up = (i // stride) % 2 == 0
            route.append((i, i + stride if up else i - stride))
        return lax.ppermute(block, AXES, route)

    def hop(self, block, k, way, keep):
        stride, radix = self.strides[k], self.factors[k]
        route = []
        for i in range(self.count):
            digit = (i // stride) % radix
            if 0 <= digit + way < radix and keep(digit):
                route.append((i, i + way * stride))
        return lax.ppermute(block, AXES, route)

    def gather_step(self, block, k):
        axis, radix = self.axis(k), self.factors[k]
        digit = self.digit(k)
        if radix == 2:
            other = self.swap(block, k)
            shape = block.shape[:axis] + (2,) + block.shape[axis + 1 :]
            mine = lax.broadcasted_iota(jnp.int32, shape, axis) == digit
            return jnp.where(mine, jnp.broadcast_to(block, shape), jnp.broadcast_to(other, shape))
        before, after = [], []
        left = right = block
        for d in range(1, radix):
            left = self.hop(left, k, 1, lambda digit: digit >= d - 1)
            right = self.hop(right, k, -1, lambda digit: digit + d - 1 < radix)
            before.insert(0, left)
            after.append(right)
        line = jnp.concatenate(before + [block] + after, axis=axis)
        return lax.dynamic_slice_in_dim(line, radix - 1 - digit, radix, axis)

    def scatter_step(self, terms, k):
        axis, radix = self.axis(k), self.factors[k]
        digit = self.digit(k)

        def pick(index):
            index = jnp.clip(index, 0, radix - 1)
            return [lax.dynamic_slice_in_dim(t, index, 1, axis) for t in terms]

        if radix == 2:
            return [self.swap(total(pick(1 - digit), BF16), k), *pick(digit)]
        kept = pick(digit)
        for way in (1, -1):
            run = []
            for d in range(radix - 1, 0, -1):
                part = total(pick(digit + way * d) + run, BF16)
                run = [self.hop(part, k, way, lambda digit: 0 <= digit + way * d < radix)]
            kept.extend(run)
        return kept

    def orders(self):
        far = list(range(self.depth - 1, 2, -1))
        return far, ([1, 2], [2, 1])

    def sum_all(self, value):
        for k in range(self.depth):
            value = value + self.swap(value, k)
        return value


def total(terms, kind):
    if len(terms) == 1:
        return terms[0].astype(kind)
    return sum(t.astype(F32) for t in terms).astype(kind)


def tied(value, *others):
    others = [o for o in others if o is not None]
    if not others:
        return value
    return lax.optimization_barrier((value, *others))[0]


def gather_pack(grid, pieces, after_far, after_near, extra=None):
    far, orders = grid.orders()
    rows = pieces[0].shape[0]
    block = jnp.concatenate([pieces[0], pieces[1].reshape(rows, -1)], axis=1)
    block = tied(block.reshape((1,) * grid.depth + block.shape), after_far)

    def along(k):
        nonlocal extra
        if extra is not None:
            extra = grid.gather_step(extra, k)

    for k in far:
        block = grid.gather_step(block, k)
    extra = extra if extra is None else tied(extra, block)
    for k in far:
        along(k)
    near = tied(block, after_near)
    cut = pieces[0].shape[1]
    parts = [near[..., :cut], near[..., cut:].reshape(near.shape[:-2] + pieces[1].shape)]
    for at in range(2):
        parts = [grid.gather_step(p, order[at]) for p, order in zip(parts, orders)]
        along(orders[0][at])
    wholes = [grid.gather_step(p, 0).reshape(-1, p.shape[-1]) for p in parts]
    along(0)
    return wholes, block, parts[0], extra


def scatter_near_step(grid, parts, at):
    _, orders = grid.orders()
    return [grid.scatter_step(part, (0, *order)[at]) for part, order in zip(parts, orders)]


def opened(grid, wholes):
    return [[w.reshape(grid.dims() + (w.shape[0] // grid.count, w.shape[1]))] for w in wholes]


def join_parts(parts):
    parts = [total(p, BF16) for p in parts]
    rows = parts[0].shape[-2]
    return jnp.concatenate([parts[0], parts[1].reshape(parts[1].shape[:-2] + (rows, -1))], axis=-1)


def split_far(terms, shapes):
    rows, cut = shapes[0]
    block = total(terms, F32).reshape(rows, -1)
    return block[:, :cut], block[:, cut:].reshape(shapes[1])


def held(values):
    flat, tree = jax.tree.flatten(values)
    return jax.tree.unflatten(tree, lax.optimization_barrier(tuple(flat)))


def scatter_last(grid, wholes, ending, sums):
    far, _ = grid.orders()
    near = list(reversed(far))
    shapes = [(w.shape[0] // grid.count, w.shape[1]) for w in wholes]
    last_shapes = [p[0].shape[-2:] for p in ending]
    parts, rest = opened(grid, wholes), ending

    def onward(blocks, at):
        if at < 3:
            return scatter_near_step(grid, blocks, at)
        if at > grid.depth - 1:
            return blocks
        terms = [join_parts(blocks)] if at == 3 else blocks[0]
        return [grid.scatter_step(terms, near[at - 3])]

    for at in range(grid.depth):
        parts, rest, sums = held((parts, rest, sums))
        parts = onward(parts, at)
        rest = onward(rest, at + 2)
        sums = sums + grid.swap(sums, at)
    return split_far(parts[0], shapes), split_far(rest[0], last_shapes), sums


def scan_states(packed, axis, way):
    devices = lax.axis_size(axis)
    place = lax.axis_index(axis)
    if way < 0:
        place = devices - 1 - place
    rows = packed.shape[0] - 8
    fresh, decay = packed[:rows].astype(F32), packed[rows : rows + 1].astype(F32)
    lead, carry = jnp.ones_like(decay), jnp.zeros_like(fresh)
    message = packed
    step = 1
    while step < devices:
        final = 2 * step >= devices
        high = (place // step) % 2 == 1
        spans = [i if way > 0 else devices - 1 - i for i in range(devices)]
        route = [(spans[i], spans[i ^ step]) for i in range(devices) if not final or not i & step]
        if final:
            message = message[:rows]
            yield message
        got = lax.ppermute(message, axis, route).astype(F32)
        carry = jnp.where(high, lead * got[:rows] + carry, carry)
        if not final:
            other, other_decay = got[:rows], got[rows : rows + 1]
            fresh = jnp.where(high, decay * other + fresh, other_decay * fresh + other)
            lead = jnp.where(high, lead * other_decay, lead)
            decay = decay * other_decay
            message = fresh.astype(BF16)
            if 4 * step < devices:
                message = jnp.concatenate([message, jnp.broadcast_to(decay, (8, decay.shape[1])).astype(BF16)])
        step *= 2
    yield carry


LANES = 128
PAIRS = INNER // LANES
F32 = jnp.float32
BF16 = jnp.bfloat16
FAR = -1e30
UNROLL = 2
VMEM_LIMIT = 52 * 2**20
VMEM_SLACK = 8 * 2**20


def dot(a, b):
    return jnp.dot(a, b, preferred_element_type=F32)


def dot_nt(a, b):
    return lax.dot_general(a, b, (((1,), (1,)), ((), ())), preferred_element_type=F32)


def flip(a):
    return a.astype(F32).T


def split3(value):
    high = value.astype(BF16)
    rest = value - high.astype(F32)
    mid = rest.astype(BF16)
    low = (rest - mid.astype(F32)).astype(BF16)
    return jnp.concatenate([high, mid, low], axis=1)


def head_sum(high, low, spread):
    return dot_nt(high, spread[:LANES]) + dot_nt(low, spread[:LANES])


def lanes_of(p):
    return pl.ds(pl.multiple_of(p * LANES, LANES), LANES)


def sigmoid(v):
    return 0.5 + 0.5 * jnp.tanh(0.5 * v)


def each_pair(body, group=UNROLL):
    def some(i, carry):
        for k in range(group):
            body(i * group + k)
        return carry

    lax.fori_loop(0, PAIRS // group, some, 0)


def put_split(high, low, lanes, value):
    top = value.astype(BF16)
    high[:, lanes] = top
    low[:, lanes] = (value - top.astype(F32)).astype(BF16)


def iota(shape, axis):
    return lax.broadcasted_iota(jnp.int32, shape, axis)


def call(body, outs, *args, scratch=(), flops=2e9):
    vm = pl.BlockSpec(memory_space=pltpu.VMEM)
    size = sum(a.size * a.dtype.itemsize for a in args)
    held = size + sum(math.prod(m) * jnp.dtype(d).itemsize for m, d in outs)
    held += sum(math.prod(m.shape) * jnp.dtype(m.dtype).itemsize for m in scratch)
    return pl.pallas_call(
        body,
        out_shape=[jax.ShapeDtypeStruct(s, d) for s, d in outs],
        in_specs=[vm] * len(args),
        out_specs=[vm] * len(outs),
        scratch_shapes=list(scratch),
        compiler_params=pltpu.CompilerParams(vmem_limit_bytes=max(VMEM_LIMIT, held + VMEM_SLACK)),
        cost_estimate=pl.CostEstimate(flops=int(flops), bytes_accessed=int(size), transcendentals=0),
    )(*args)


def project_body(hidden, gain, wa, wb, normed, conv_in, dt):
    h = hidden[...]
    scale = lax.rsqrt(jnp.mean(h * h, axis=-1, keepdims=True) + epsilon)
    low = (h * scale * gain[...]).astype(BF16)
    normed[...] = low
    cut = wa.shape[1]
    rest = XBC - cut
    conv_in[:, :cut] = dot(low, wa[...]).astype(BF16)
    second = dot(low, wb[...])
    conv_in[:, cut:] = second[:, :rest].astype(BF16)
    dt[...] = jnp.where(iota((SPAN, LANES), 1) < HEADS, second[:, rest : rest + LANES], 0.0)


def project_all_body(hidden, gain, weight, normed, conv_in, dt, gate):
    h = hidden[...]
    scale = lax.rsqrt(jnp.mean(h * h, axis=-1, keepdims=True) + epsilon)
    low = (h * scale * gain[...]).astype(BF16)
    normed[...] = low
    conv_in[...] = dot(low, weight[:, :XBC]).astype(BF16)
    steps = dot(low, weight[:, XBC : XBC + LANES])
    dt[...] = jnp.where(iota((SPAN, LANES), 1) < HEADS, steps, 0.0)
    gate[...] = dot(low, weight[:, XBC + LANES :]).astype(BF16)


def conv_pre(ext, weight, bias, lanes):
    total = bias[:, lanes] + weight[KCONV - 1 : KCONV, lanes] * ext[8 : 8 + SPAN, lanes]
    for s in range(1, KCONV):
        tap = weight[KCONV - 1 - s : KCONV - s, lanes]
        total = total + tap * ext[8 - s : 8 - s + SPAN, lanes]
    return total


def triangle(upper):
    i, j = iota((SPAN, SPAN), 0), iota((SPAN, SPAN), 1)
    return jnp.where((i <= j) if upper else (i >= j), 1.0, 0.0).astype(F32)


def running(mask, value):
    return jnp.dot(mask, value, precision=lax.Precision.HIGHEST, preferred_element_type=F32)


def states_body(
    conv_in, rim, weight, bias, dt, dt_bias, a_log, valid, keep, spread,
    x, stepped, keys, queries, step, cum, packed, ext, wide, wide_step, weighted,
):
    ext[:8] = rim[...].astype(F32)
    ext[8:] = conv_in[...].astype(F32)

    def act(lanes):
        pre = conv_pre(ext, weight, bias, lanes)
        return (pre * sigmoid(pre)).astype(BF16)

    keys[...] = act(pl.ds(INNER, LANES))
    queries[...] = act(pl.ds(INNER + LANES, LANES))
    raw = dt[...] + dt_bias[...]
    size = jnp.maximum(raw, 0.0) + jnp.log1p(jnp.exp(-jnp.abs(raw)))
    size = jnp.where(iota((SPAN, LANES), 1) < HEADS, size * valid[...], 0.0)
    step[...] = size
    total = running(triangle(False), -jnp.exp(a_log[...]) * size)
    cum[...] = total
    last = total[SPAN - 1 :]
    tail = jnp.exp(last - total) * size
    wide[...] = dot(split3(tail), spread[...])
    wide_step[...] = dot(split3(size), spread[...])
    growth = jnp.broadcast_to(jnp.exp(last) * keep[...], (8, LANES))
    packed[STATE:] = dot(split3(growth), spread[...]).astype(BF16)

    def pair(p):
        lanes = lanes_of(p)
        low = act(lanes)
        x[:, lanes] = low
        wider = low.astype(F32)
        weighted[:, lanes] = (wider * wide[:, lanes]).astype(BF16)
        stepped[:, lanes] = (wider * wide_step[:, lanes]).astype(BF16)

    each_pair(pair)
    packed[:STATE] = dot(flip(keys[...]).astype(BF16), weighted[...]).astype(BF16)


def diag_body(x, stepped, keys, queries, cum, skip, spread, y, scores, cum_t, wide):
    scores[...] = dot_nt(queries[...], keys[...])
    cum_t[...] = cum[...].T
    wide[...] = dot(split3(cum[...]), spread[...])
    half = SPAN // 2

    def pair(p):
        lanes = lanes_of(p)
        xp = stepped[:, lanes]
        col = wide[:, lanes]
        turned = pltpu.roll(col, HEAD_DIM, 1)
        first = iota((SPAN, LANES), 1) < HEAD_DIM
        both = []
        for k in range(2):
            c = jnp.where(first, col, turned) if k == 0 else jnp.where(first, turned, col)
            row = cum_t[pl.ds(2 * p + k, 1), :]
            tri = iota((SPAN, half), 0) >= iota((SPAN, half), 1)
            f0 = jnp.exp(jnp.where(tri, c - row[:, :half], FAR))
            f1 = jnp.exp(jnp.where(tri[:half], c[half:] - row[:, half:], FAR))
            d0 = dot((scores[:, :half] * f0).astype(BF16), xp[:half])
            d1 = dot((scores[half:, half:] * f1).astype(BF16), xp[half:])
            both.append(jnp.concatenate([d0[:half], d0[half:] + d1], axis=0))
        out = jnp.where(first, both[0], both[1]) + skip[:, lanes] * x[:, lanes].astype(F32)
        y[:, lanes] = out

    each_pair(pair)


def finish_body(
    y, gate, queries, carried, cum, gain, w_out, hidden, spread, mixed, normed_out, result, wide, states, total, gated
):
    wide[...] = dot(split3(jnp.exp(cum[...])), spread[...])
    states[...] = dot(queries[...], carried[...])
    total[...] = jnp.zeros_like(total)

    def mix(p):
        lanes = lanes_of(p)
        m = y[:, lanes] + wide[:, lanes] * states[:, lanes]
        mixed[:, lanes] = m
        g = gate[:, lanes].astype(F32)
        v = m * (g * sigmoid(g))
        gated[:, lanes] = v
        total[...] += v * v

    each_pair(mix)
    mean = jnp.sum(total[...], axis=1, keepdims=True) * (1.0 / INNER)
    scale = lax.rsqrt(mean + epsilon)

    def norm(p):
        lanes = lanes_of(p)
        normed_out[:, lanes] = (gated[:, lanes] * scale * gain[:, lanes]).astype(BF16)

    each_pair(norm)
    result[...] = hidden[...] + dot(normed_out[...], w_out[...])


def open_body(
    grad, w_out, mixed, gate, gain, queries, carried, cum, x, skip, keep, decay, spread,
    gain_grad, gate_low, diag_low, packed, query_grad, cum_grad, skip_grad,
    wide, square, cross, back, state_low, high, low,
):
    out_low = grad[...].astype(BF16)
    square[...] = jnp.zeros_like(square)
    cross[...] = jnp.zeros_like(cross)
    wide[...] = dot(split3(jnp.exp(cum[...])), spread[...])
    back[...] = dot_nt(out_low, w_out[...])

    def first(p):
        lanes = lanes_of(p)
        a = gate[:, lanes].astype(F32)
        v = mixed[:, lanes] * (a * sigmoid(a))
        square[...] += v * v
        cross[...] += v * (back[:, lanes] * gain[:, lanes])

    each_pair(first)
    scale = lax.rsqrt(jnp.sum(square[...], axis=1, keepdims=True) * (1.0 / INNER) + epsilon)
    share = jnp.sum(cross[...], axis=1, keepdims=True) * (1.0 / INNER) * scale * scale * scale

    def second(p):
        lanes = lanes_of(p)
        g = back[:, lanes]
        a = gate[:, lanes].astype(F32)
        s = sigmoid(a)
        act = a * s
        m = mixed[:, lanes]
        v = m * act
        gain_grad[:, lanes] = jnp.sum(g * v * scale, axis=0, keepdims=True)
        dv = scale * (g * gain[:, lanes]) - v * share
        gate_low[:, lanes] = (dv * m * (s + act * (1.0 - s))).astype(BF16)
        gm = dv * act
        rounded = gm.astype(BF16)
        diag_low[:, lanes] = rounded
        xp = x[:, lanes].astype(F32)
        skip_grad[:, lanes] = jnp.sum(gm * xp, axis=0, keepdims=True)
        state_low[:, lanes] = (wide[:, lanes] * gm).astype(BF16)
        put_split(high, low, lanes, rounded.astype(F32) * (m - skip[:, lanes] * xp))

    each_pair(second)
    cum_grad[...] = head_sum(high[...], low[...], spread)
    packed[:STATE] = (dot(flip(queries[...]).astype(BF16), state_low[...]) * keep[:, :1]).astype(BF16)
    packed[STATE:] = decay[...]
    query_grad[...] = dot_nt(state_low[...], carried[...])


def pairs_body(
    diag_low, x, stepped, keys, queries, step, cum, skip, spread, query_in,
    x_grad, key_grad, query_grad, step_grad, col_grad,
    scores, score_grad, cum_t, wide, wide_step, high, low, col_high, col_low,
):
    scores[...] = dot_nt(keys[...], queries[...])
    score_grad[...] = jnp.zeros_like(score_grad)
    cum_t[...] = cum[...].T
    wide[...] = dot(split3(cum[...]), spread[...])
    wide_step[...] = dot(split3(step[...]), spread[...])
    half = SPAN // 2

    def pair(p):
        lanes = lanes_of(p)
        xp = stepped[:, lanes]
        dp = diag_low[:, lanes]
        first = iota((SPAN, LANES), 1) < HEAD_DIM
        col = wide[:, lanes]
        turned = pltpu.roll(col, HEAD_DIM, 1)
        both = []
        for k in range(2):
            mine = first if k == 0 else jnp.logical_not(first)
            c = jnp.where(mine, col, turned)
            row = cum_t[pl.ds(2 * p + k, 1), :]
            tri = iota((SPAN, half), 0) <= iota((SPAN, half), 1) + half
            xk = jnp.where(mine, xp.astype(F32), 0.0).astype(BF16)
            f1 = jnp.exp(jnp.where(tri, row[:, half:] - c, FAR))
            f0 = jnp.exp(jnp.where(tri[half:], row[:, :half] - c[:half], FAR))
            score_grad[:, half:] += dot_nt(xk, dp[half:]) * f1
            score_grad[:half, :half] += dot_nt(xk[:half], dp[:half]) * f0
            top = dot((scores[:, half:] * f1).astype(BF16), dp[half:])
            bottom = dot((scores[:half, :half] * f0).astype(BF16), dp[:half])
            both.append(jnp.concatenate([top[:half] + bottom, top[half:]], axis=0))
        through = jnp.where(first, both[0], both[1])
        x_grad[:, lanes] = wide_step[:, lanes] * through + skip[:, lanes] * dp.astype(F32)
        put_split(high, low, lanes, x[:, lanes].astype(F32) * through)
        put_split(col_high, col_low, lanes, xp.astype(F32) * through)

    each_pair(pair)
    step_grad[...] = head_sum(high[...], low[...], spread)
    col_grad[...] = head_sum(col_high[...], col_low[...], spread)
    key_grad[...] = dot(score_grad[...].astype(BF16), queries[...])
    query_grad[...] = query_in[...] + dot(score_grad[...].T.astype(BF16), keys[...])


def close_body(
    pending, carried, keys, x, step, cum, x_grad, key_in, query_grad, step_in, col_in, cum_in,
    conv_in, rim, weight, bias, dt, dt_bias, a_log, valid, spread,
    act_grad, dt_low, dt_bias_grad, a_log_grad, bias_grad, weight_grad,
    ext, wide, back, weighted, column, high, low,
):
    ext[:8] = rim[...].astype(F32)
    ext[8:] = conv_in[...].astype(F32)
    total = cum[...]
    size = step[...]
    last = total[SPAN - 1 :]
    fade = jnp.exp(last - total)
    tail = fade * size
    late = pending[...].astype(BF16)
    wide[...] = dot(split3(tail), spread[...])
    back[...] = dot(keys[...], late)

    def through(lanes, grad):
        pre = conv_pre(ext, weight, bias, lanes)
        s = sigmoid(pre)
        ga = grad * (s * (1.0 + pre * (1.0 - s)))
        act_grad[:, lanes] = ga.astype(BF16)
        bias_grad[:, lanes] = jnp.sum(ga, axis=0, keepdims=True)
        for k in range(KCONV):
            at = 8 - (KCONV - 1 - k)
            weight_grad[k : k + 1, lanes] = jnp.sum(
                ga * ext[at : at + SPAN, lanes], axis=0, keepdims=True
            )

    def pair(p):
        lanes = lanes_of(p)
        xp = x[:, lanes].astype(F32)
        over = wide[:, lanes]
        gw = back[:, lanes]
        put_split(high, low, lanes, gw * xp)
        weighted[:, lanes] = (xp * over).astype(BF16)
        kept = pending[:, lanes] * carried[:, lanes].astype(F32)
        column[:, lanes] = jnp.broadcast_to(jnp.sum(kept, axis=0, keepdims=True), (8, LANES))
        through(lanes, x_grad[:, lanes] + gw * over)

    each_pair(pair)
    through(pl.ds(INNER, LANES), key_in[...] + dot_nt(weighted[...], late))
    through(pl.ds(INNER + LANES, LANES), query_grad[...])
    tg = head_sum(high[...], low[...], spread)
    top = column[...].astype(BF16)
    grow_grad = head_sum(top, (column[...] - top.astype(F32)).astype(BF16), spread)
    run = tg * tail
    cg = cum_in[...] - col_in[...] - run
    end = jnp.sum(run, axis=0, keepdims=True) + grow_grad[:1] * jnp.exp(last)
    cg = cg + jnp.where(iota((SPAN, LANES), 0) == SPAN - 1, end, 0.0)
    rate = jnp.exp(a_log[...])
    decay_grad = running(triangle(True), cg)
    sg = tg * fade + step_in[...] - rate * decay_grad
    a_log_grad[...] = jnp.sum(decay_grad * (-rate * size), axis=0, keepdims=True)
    pre_grad = sg * valid[...] * sigmoid(dt[...] + dt_bias[...])
    pre_grad = jnp.where(iota((SPAN, LANES), 1) < HEADS, pre_grad, 0.0)
    dt_bias_grad[...] = jnp.sum(pre_grad, axis=0, keepdims=True)
    dt_low[...] = pre_grad.astype(BF16)


def conv_back(act_grad, rim_grad, weight, dt_low, first, ext):
    ext[:SPAN] = act_grad[...].astype(F32)
    ext[SPAN:] = rim_grad[...].astype(F32)

    def conv(c, carry):
        for k in range(2):
            lanes = lanes_of(2 * c + k)
            total = weight[KCONV - 1 : KCONV, lanes] * ext[:SPAN, lanes]
            for s in range(1, KCONV):
                total = total + weight[KCONV - 1 - s : KCONV - s, lanes] * ext[s : s + SPAN, lanes]
            first[:, lanes] = total.astype(BF16)
        return carry

    lax.fori_loop(0, XBC // LANES // 2, conv, 0)
    first[:, XBC : XBC + LANES] = dt_low[...]


def norm_back(back, hidden, gain, grad, grad_out, gain_grad):
    h = hidden[...]
    scale = lax.rsqrt(jnp.mean(h * h, axis=-1, keepdims=True) + epsilon)
    gain_grad[...] = jnp.sum(back * h * scale, axis=0, keepdims=True)
    back = back * gain[...]
    share = jnp.mean(back * h, axis=-1, keepdims=True) * scale * scale * scale
    grad_out[...] = grad[...] + back * scale - h * share


def inward_body(act_grad, rim_grad, weight, dt_low, gate_part, wa, wb, hidden, gain, grad, first, grad_out, gain_grad, ext):
    conv_back(act_grad, rim_grad, weight, dt_low, first, ext)
    cut = wa.shape[1]
    back = gate_part[...] + dot_nt(first[:, :cut], wa[...]) + dot_nt(first[:, cut:], wb[...])
    norm_back(back, hidden, gain, grad, grad_out, gain_grad)


def inward_all_body(act_grad, rim_grad, weight, dt_low, gate_low, whole, hidden, gain, grad, first, grad_out, gain_grad, ext):
    conv_back(act_grad, rim_grad, weight, dt_low, first, ext)
    back = dot_nt(first[...], whole[:, : XBC + LANES]) + dot_nt(gate_low[...], whole[:, XBC + LANES :])
    norm_back(back, hidden, gain, grad, grad_out, gain_grad)


def padded(row):
    return jnp.pad(row.astype(F32), (0, LANES - row.shape[0]))[None]


def layer_forward(hidden, weights, heads, keep, valid, spread):
    norm_gain, w_in, conv_weight, conv_bias, gate_gain, w_out = weights
    dt_bias, a_log, skip = heads
    count = hidden.shape[0]
    outs = [((count, hidden.shape[1]), BF16), ((count, XBC), BF16), ((count, LANES), F32)]
    if len(w_in) == 3:
        normed, conv_in, dt = call(project_body, outs, hidden, norm_gain, *w_in[:2])
        gate = dot(normed, w_in[2]).astype(BF16)
    else:
        outs.append(((count, INNER), BF16))
        normed, conv_in, dt, gate = call(project_all_body, outs, hidden, norm_gain, *w_in)
    rim = (shifted(conv_in[count - 8 :], "fsdp", 1).astype(F32) * keep).astype(BF16)
    x, stepped, keys, queries, step, cum, packed = call(
        states_body,
        [
            ((count, INNER), BF16), ((count, INNER), BF16), ((count, STATE), BF16), ((count, STATE), BF16), ((count, LANES), F32),
            ((count, LANES), F32), ((STATE + 8, INNER), BF16),
        ],
        conv_in, rim, conv_weight, conv_bias, dt, dt_bias, a_log, valid, jnp.full((1, LANES), keep), spread,
        scratch=[
            pltpu.VMEM((count + 8, XBC), F32), pltpu.VMEM((count, INNER), F32), pltpu.VMEM((count, INNER), F32),
            pltpu.VMEM((count, INNER), BF16),
        ],
        flops=5e8,
    )
    scan = scan_states(packed, "fsdp", 1)
    stepped = tied(stepped, next(scan))
    (y,) = call(
        diag_body, [((count, INNER), F32)], x, stepped, keys, queries, cum, skip, spread,
        scratch=[
            pltpu.VMEM((SPAN, SPAN), F32), pltpu.VMEM((LANES, count), F32),
            pltpu.VMEM((count, INNER), F32),
        ],
        flops=4e9,
    )
    carried = (keep * next(scan)).astype(BF16)
    mixed, normed_out, result = call(
        finish_body,
        [((count, INNER), F32), ((count, INNER), BF16), (hidden.shape, F32)],
        y, gate, queries, carried, cum, gate_gain, w_out, hidden, spread,
        scratch=[
            pltpu.VMEM((count, INNER), F32), pltpu.VMEM((count, INNER), F32), pltpu.VMEM((count, LANES), F32),
            pltpu.VMEM((count, INNER), F32),
        ],
    )
    saved = (hidden, normed, conv_in, dt, rim, x, stepped, keys, queries, step, cum, packed[STATE:], carried, gate, mixed, normed_out)
    return result, saved


def layer_backward(grad, saved, weights, heads, keep, valid, spread, grid):
    norm_gain, w_in, conv_weight, conv_bias, gate_gain, w_out = weights
    dt_bias, a_log, skip = heads
    hidden, normed, conv_in, dt, rim, x, stepped, keys, queries, step, cum, decay, carried, gate, mixed, normed_out = saved
    count = hidden.shape[0]
    row = (1, INNER)
    gain_grad, gate_low, diag_low, packed, query_part, cum_part, skip_grad = call(
        open_body,
        [
            (row, F32), ((count, INNER), BF16), ((count, INNER), BF16), ((STATE + 8, INNER), BF16), ((count, STATE), F32),
            ((count, LANES), F32), (row, F32),
        ],
        grad, w_out, mixed, gate, gate_gain, queries, carried, cum, x, skip, jnp.full((1, LANES), keep), decay, spread,
        scratch=[
            pltpu.VMEM((count, INNER), F32), pltpu.VMEM((count, LANES), F32),
            pltpu.VMEM((count, LANES), F32), pltpu.VMEM((count, INNER), F32), pltpu.VMEM((count, INNER), BF16),
            pltpu.VMEM((count, INNER), BF16), pltpu.VMEM((count, INNER), BF16),
        ],
    )
    grad_w_out = dot(normed_out.T, grad.astype(BF16)).astype(BF16)
    scan = scan_states(packed, "fsdp", -1)
    diag_low = tied(diag_low, next(scan))
    x_grad, key_grad, query_grad, step_grad, col_grad = call(
        pairs_body,
        [
            ((count, INNER), F32), ((count, STATE), F32), ((count, STATE), F32), ((count, LANES), F32),
            ((count, LANES), F32),
        ],
        diag_low, x, stepped, keys, queries, step, cum, skip, spread, query_part,
        scratch=[
            pltpu.VMEM((SPAN, SPAN), F32), pltpu.VMEM((SPAN, SPAN), F32), pltpu.VMEM((LANES, count), F32),
            pltpu.VMEM((count, INNER), F32), pltpu.VMEM((count, INNER), F32),
            *[pltpu.VMEM((count, INNER), BF16)] * 4,
        ],
        flops=8e9,
    )
    split = len(w_in) == 3
    ready, moved = None, None
    grad_w_gate = dot(normed.T, gate_low).astype(BF16)
    if split:
        gate_part = dot(gate_low, w_in[2].T)
        ready = scatter_near_step(grid, opened(grid, [grad_w_gate, grad_w_out]), 0)
        x_grad = tied(x_grad, *[part[0] for part in ready])
    pending = next(scan)
    act_grad, dt_low, dt_bias_grad, a_log_grad, bias_grad, weight_grad = call(
        close_body,
        [
            ((count, XBC), BF16), ((count, LANES), BF16), ((1, LANES), F32), ((1, LANES), F32), ((1, XBC), F32),
            ((KCONV, XBC), F32),
        ],
        pending, carried, keys, x, step, cum, x_grad, key_grad, query_grad, step_grad, col_grad, cum_part,
        conv_in, rim, conv_weight, conv_bias, dt, dt_bias, a_log, valid, spread,
        scratch=[
            pltpu.VMEM((count + 8, XBC), F32), pltpu.VMEM((count, INNER), F32), pltpu.VMEM((count, INNER), F32),
            pltpu.VMEM((count, INNER), BF16), pltpu.VMEM((8, INNER), F32), pltpu.VMEM((count, INNER), BF16),
            pltpu.VMEM((count, INNER), BF16),
        ],
    )
    rim_grad = shifted((act_grad[:8].astype(F32) * keep).astype(BF16), "fsdp", -1)
    outs = [((count, XBC + LANES), BF16), (hidden.shape, F32), ((1, hidden.shape[1]), F32)]
    scratch = [pltpu.VMEM((count + 8, XBC), F32)]
    if split:
        ready = scatter_near_step(grid, ready, 1)
        first, grad_out, norm_grad = call(
            inward_body, outs, act_grad, rim_grad, conv_weight, dt_low, gate_part, *w_in[:2], hidden, norm_gain, grad,
            scratch=scratch,
        )
        cut = w_in[0].shape[1]
        first_grads = [dot(normed.T, first[:, :cut]).astype(BF16), dot(normed.T, first[:, cut:]).astype(BF16)]
        mats = (ready, first_grads)
    else:
        first, grad_out, norm_grad = call(
            inward_all_body, outs, act_grad, rim_grad, conv_weight, dt_low, gate_low, *w_in, hidden, norm_gain, grad,
            scratch=scratch,
        )
        mats = (dot(normed.T, first).astype(BF16), grad_w_gate, grad_w_out)
    skip_sum = jnp.sum(skip_grad.reshape(HEADS, HEAD_DIM), axis=1)
    rows = jnp.concatenate(
        [
            norm_grad[0],
            weight_grad.reshape(-1),
            bias_grad[0],
            gain_grad[0],
            dt_bias_grad[0],
            a_log_grad[0],
            padded(skip_sum)[0],
        ]
    )
    return grad_out, mats, rows


def shards(
    tokens,
    starts,
    valid,
    norm_gain,
    w_gate,
    w_xbc,
    w_dt,
    conv_weight,
    conv_bias,
    dt_bias,
    a_log,
    skip_weight,
    gate_gain,
    w_out,
    cotangent,
):
    layers = norm_gain.shape[0]
    grid = Grid()
    count = grid.count
    rows, outer = w_gate.shape[1], w_out.shape[1]
    taps, chans = conv_weight.shape[1:]
    pad = LANES - HEADS
    cut = XBC // 2 // LANES * LANES
    small = jnp.concatenate(
        [
            v.reshape(-1)
            for l in range(layers)
            for v in (norm_gain[l], conv_weight[l], conv_bias[l], gate_gain[l])
        ]
    )
    length = small.size
    small = jnp.pad(small, (0, -length % (8 * LANES))).reshape((1,) * grid.depth + (-1, LANES))
    firsts, seconds = [], []
    for l in range(layers):
        tail = jnp.concatenate([w_xbc[l][:, cut:], w_dt[l], jnp.zeros((rows, pad), BF16)], 1)
        if l == 0:
            pair, last_far, last_near, small = gather_pack(grid, [w_xbc[l][:, :cut], tail], None, None, small)
            firsts.append(pair)
            pair, *_ = gather_pack(grid, [w_gate[l], w_out[l]], last_far, last_near)
            seconds.append(pair)
            continue
        first = jnp.concatenate([w_xbc[l][:, :cut], tail, w_gate[l]], axis=1)
        firsts.append([lax.all_gather(first, AXES, axis=0, tiled=True)])
        seconds.append([None, lax.all_gather(w_out[l], AXES, axis=0, tiled=True)])
    small = small.reshape(count, -1)[:, :length].astype(F32)
    wholes, heads = [], []
    at = 0
    for l in range(layers):
        rest = []
        for size in (rows, taps * chans, chans, outer):
            rest.append(small[:, at : at + size])
            at += size
        w_in = firsts[l]
        kernel = jnp.moveaxis(rest[1].reshape(count, taps, chans), 1, 0)
        wholes.append(
            (
                rest[0].reshape(1, -1),
                w_in if l else [*w_in, seconds[l][0]],
                kernel.reshape(taps, -1),
                rest[2].reshape(1, -1),
                rest[3].reshape(1, -1),
                seconds[l][1],
            )
        )
        heads.append((padded(dt_bias[l]), padded(a_log[l]), jnp.repeat(skip_weight[l], HEAD_DIM)[None]))
    spread = (iota((3 * LANES, INNER), 0) % LANES == iota((3 * LANES, INNER), 1) // HEAD_DIM).astype(BF16)
    keep = 1.0 - starts[0].astype(F32)
    valid = valid.astype(F32)[:, None]
    hidden = tokens.astype(F32)
    saves = []
    for l in range(layers):
        hidden, saved = layer_forward(hidden, wholes[l], heads[l], keep, valid, spread)
        saves.append(saved)
    grad = cotangent.astype(F32)
    owned, summed = [None] * layers, [None] * layers
    for l in reversed(range(layers)):
        grad, mats, summed[l] = layer_backward(grad, saves[l], wholes[l], heads[l], keep, valid, spread, grid)
        if l == 0:
            sums = jnp.stack(summed)
            (left, right), (gate_sum, out_sum), sums = scatter_last(grid, mats[1], mats[0], sums)
        else:
            outs = jnp.moveaxis(mats[2].reshape(count, 2, rows, -1), 1, 2).reshape(count * rows, -1)
            packed = jnp.concatenate([mats[0], mats[1], outs], axis=1)
            packed = lax.psum_scatter(packed, AXES, scatter_dimension=0, tiled=True).astype(F32)
            at = XBC + LANES
            left, right = packed[:, :cut], packed[:, cut:at]
            gate_sum = packed[:, at : at + INNER]
            out_sum = jnp.moveaxis(packed[:, at + INNER :].reshape(rows, 2, -1), 1, 0).reshape(outer, -1)
        owned[l] = (
            gate_sum,
            jnp.concatenate([left, right[:, : XBC - cut]], axis=1),
            right[:, XBC - cut : XBC - cut + HEADS],
            out_sum,
        )
    at_kernel = rows * count
    at_bias = at_kernel + taps * chans * count
    at_gain = at_bias + chans * count
    at_heads = at_gain + outer * count

    def own(first, size):
        return lax.dynamic_slice_in_dim(sums, first + grid.place * size, size, 1)

    kernel_sums = sums[:, at_kernel:at_bias].reshape(layers, taps, count * chans)
    kernel_sums = lax.dynamic_slice_in_dim(kernel_sums, grid.place * chans, chans, 2)
    head_sums = sums[:, at_heads:].reshape(layers, 3, LANES)[:, :, :HEADS]

    def stacked(position):
        return jnp.stack([member[position] for member in owned])

    return (
        hidden,
        grad,
        own(0, rows),
        stacked(0),
        stacked(1),
        stacked(2),
        kernel_sums,
        own(at_bias, chans),
        head_sums[:, 0],
        head_sums[:, 1],
        head_sums[:, 2],
        own(at_gain, outer),
        stacked(3),
    )


def solution(mesh):
    return jax.shard_map(
        shards,
        mesh=mesh,
        in_specs=(
            P(("dp", "fsdp"), None),
            P(("dp", "fsdp")),
            P(("dp", "fsdp")),
            P(None, ("dp", "fsdp")),
            P(None, ("dp", "fsdp"), None),
            P(None, ("dp", "fsdp"), None),
            P(None, ("dp", "fsdp"), None),
            P(None, None, ("dp", "fsdp")),
            P(None, ("dp", "fsdp")),
            P(),
            P(),
            P(),
            P(None, ("dp", "fsdp")),
            P(None, ("dp", "fsdp"), None),
            P(("dp", "fsdp"), None),
        ),
        out_specs=(
            P(("dp", "fsdp"), None),
            P(("dp", "fsdp"), None),
            P(None, ("dp", "fsdp")),
            P(None, ("dp", "fsdp"), None),
            P(None, ("dp", "fsdp"), None),
            P(None, ("dp", "fsdp"), None),
            P(None, None, ("dp", "fsdp")),
            P(None, ("dp", "fsdp")),
            P(),
            P(),
            P(),
            P(None, ("dp", "fsdp")),
            P(None, ("dp", "fsdp"), None),
        ),
        check_vma=False,
    )
```

```python
import math

import jax
import jax.numpy as jnp
from jax import lax
from jax.experimental import pallas as pl
from jax.experimental.pallas import tpu as pltpu
from jax.sharding import PartitionSpec as P

INNER = 1536
HEADS = 24
HEAD_DIM = 64
STATE = 128
KCONV = 4
SPAN = 256
XBC = INNER + 2 * STATE


epsilon = 1e-05


def shifted(block, axis, distance):
    devices = range(lax.axis_size(axis))
    route = [(i - distance, i) for i in devices if i - distance in devices]
    return lax.ppermute(block, axis, route)


AXES = ("dp", "fsdp")


def radices(count):
    factors = []
    radix = 2
    while count > 1:
        while count % radix:
            radix += 1
        factors.append(radix)
        count //= radix
    return factors


class Grid:
    def __init__(self):
        self.count = lax.axis_size("dp") * lax.axis_size("fsdp")
        self.factors = radices(self.count)
        self.place = lax.axis_index("dp") * lax.axis_size("fsdp") + lax.axis_index("fsdp")
        self.strides = []
        stride = 1
        for radix in self.factors:
            self.strides.append(stride)
            stride *= radix
        self.depth = len(self.factors)

    def digit(self, k):
        return (self.place // self.strides[k]) % self.factors[k]

    def dims(self):
        return tuple(reversed(self.factors))

    def axis(self, k):
        return self.depth - 1 - k

    def swap(self, block, k):
        stride = self.strides[k]
        route = []
        for i in range(self.count):
            up = (i // stride) % 2 == 0
            route.append((i, i + stride if up else i - stride))
        return lax.ppermute(block, AXES, route)

    def hop(self, block, k, way, keep):
        stride, radix = self.strides[k], self.factors[k]
        route = []
        for i in range(self.count):
            digit = (i // stride) % radix
            if 0 <= digit + way < radix and keep(digit):
                route.append((i, i + way * stride))
        return lax.ppermute(block, AXES, route)

    def gather_step(self, block, k):
        axis, radix = self.axis(k), self.factors[k]
        digit = self.digit(k)
        if radix == 2:
            other = self.swap(block, k)
            shape = block.shape[:axis] + (2,) + block.shape[axis + 1 :]
            mine = lax.broadcasted_iota(jnp.int32, shape, axis) == digit
            return jnp.where(mine, jnp.broadcast_to(block, shape), jnp.broadcast_to(other, shape))
        before, after = [], []
        left = right = block
        for d in range(1, radix):
            left = self.hop(left, k, 1, lambda digit: digit >= d - 1)
            right = self.hop(right, k, -1, lambda digit: digit + d - 1 < radix)
            before.insert(0, left)
            after.append(right)
        line = jnp.concatenate(before + [block] + after, axis=axis)
        return lax.dynamic_slice_in_dim(line, radix - 1 - digit, radix, axis)

    def scatter_step(self, block, k, kind):
        axis, radix = self.axis(k), self.factors[k]
        digit = self.digit(k)

        def pick(index):
            index = jnp.clip(index, 0, radix - 1)
            return lax.dynamic_slice_in_dim(block, index, 1, axis)

        wide = jnp.float32
        if radix == 2:
            got = self.swap(pick(1 - digit), k)
            return (pick(digit).astype(wide) + got.astype(wide)).astype(kind)
        total = pick(digit).astype(wide)
        for way in (1, -1):
            run = None
            for d in range(radix - 1, 0, -1):
                part = pick(digit + way * d)
                if run is not None:
                    part = (part.astype(wide) + run.astype(wide)).astype(block.dtype)
                run = self.hop(part, k, way, lambda digit: 0 <= digit + way * d < radix)
            total = total + run.astype(wide)
        return total.astype(kind)

    def orders(self):
        far = list(range(self.depth - 1, 2, -1))
        return far, ([1, 2], [2, 1])

    def sum_all(self, value):
        for k in range(self.depth):
            value = value + self.swap(value, k)
        return value


def tied(value, *others):
    others = [o for o in others if o is not None]
    if not others:
        return value
    return lax.optimization_barrier((value, *others))[0]


def gather_pack(grid, pieces, after_far, after_near, extra=None):
    far, orders = grid.orders()
    rows = pieces[0].shape[0]
    block = jnp.concatenate([pieces[0], pieces[1].reshape(rows, -1)], axis=1)
    block = tied(block.reshape((1,) * grid.depth + block.shape), after_far)

    def along(k):
        nonlocal extra
        if extra is not None:
            extra = grid.gather_step(extra, k)

    for k in far:
        if extra is not None:
            block, extra = lax.optimization_barrier((block, extra))
        block = grid.gather_step(block, k)
        along(k)
    near = tied(block, after_near)
    cut = pieces[0].shape[1]
    parts = [near[..., :cut], near[..., cut:].reshape(near.shape[:-2] + pieces[1].shape)]
    for at in range(2):
        parts = [grid.gather_step(p, order[at]) for p, order in zip(parts, orders)]
        along(orders[0][at])
    wholes = [grid.gather_step(p, 0).reshape(-1, p.shape[-1]) for p in parts]
    along(0)
    return wholes, block, parts[0], extra


def scatter_near_step(grid, parts, at):
    _, orders = grid.orders()
    if at == 0:
        parts = [w.reshape(grid.dims() + (w.shape[0] // grid.count, w.shape[1])) for w in parts]
    return [grid.scatter_step(part, (0, *order)[at], BF16) for part, order in zip(parts, orders)]


def scatter_near(grid, parts):
    for at in range(3):
        parts = scatter_near_step(grid, parts, at)
        yield parts


def join_parts(parts):
    rows = parts[0].shape[-2]
    return jnp.concatenate([parts[0], parts[1].reshape(parts[1].shape[:-2] + (rows, -1))], axis=-1)


def split_far(block, shapes):
    rows, cut = shapes[0]
    block = block.reshape(rows, -1)
    return block[:, :cut], block[:, cut:].reshape(shapes[1])


def scatter_last(grid, wholes, ending, sums):
    far, _ = grid.orders()
    near = list(reversed(far))
    shapes = [(w.shape[0] // grid.count, w.shape[1]) for w in wholes]
    parts = list(wholes)
    rest = list(ending)

    def onward(blocks, at):
        if at < 3:
            return scatter_near_step(grid, blocks, at)
        if at > grid.depth - 1:
            return blocks
        block = join_parts(blocks) if at == 3 else blocks[0]
        k = near[at - 3]
        return [grid.scatter_step(block, k, F32 if k == near[-1] else BF16)]

    for at in range(grid.depth):
        count = len(parts)
        values = lax.optimization_barrier((*parts, *rest, sums))
        parts, rest, sums = values[:count], values[count:-1], values[-1]
        parts = onward(parts, at)
        rest = onward(rest, at + 2)
        sums = sums + grid.swap(sums, at)
    return split_far(parts[0], shapes), split_far(rest[0], [p.shape[-2:] for p in ending]), sums


def scan_states(decay, fresh, axis, way):
    devices = lax.axis_size(axis)
    place = lax.axis_index(axis)
    if way < 0:
        place = devices - 1 - place
    rows = fresh.shape[0]
    total, lead = decay, jnp.ones_like(decay)
    carry = jnp.zeros_like(fresh)
    step = 1
    while step < devices:
        final = 2 * step >= devices
        high = (place // step) % 2 == 1
        spans = [i if way > 0 else devices - 1 - i for i in range(devices)]
        route = [(spans[i], spans[i ^ step]) for i in range(devices) if not final or not i & step]
        packed = jnp.concatenate([fresh, jnp.broadcast_to(total, (8,) + total.shape[1:])]).astype(BF16)
        if final:
            yield packed
        got = lax.ppermute(packed, axis, route).astype(F32)
        other, other_total = got[:rows], got[rows : rows + 1]
        carry = jnp.where(high, lead * other + carry, carry)
        if not final:
            fresh = jnp.where(high, total * other + fresh, other_total * fresh + other)
            lead = jnp.where(high, lead * other_total, lead)
            total = total * other_total
        step *= 2
    yield carry


LANES = 128
PAIRS = INNER // LANES
F32 = jnp.float32
BF16 = jnp.bfloat16
FAR = -1e30
UNROLL = 2
VMEM_LIMIT = 52 * 2**20
VMEM_SLACK = 8 * 2**20


def dot(a, b):
    return jnp.dot(a, b, preferred_element_type=F32)


def dot_nt(a, b):
    return lax.dot_general(a, b, (((1,), (1,)), ((), ())), preferred_element_type=F32)


def flip(a):
    return a.astype(F32).T


def split3(value):
    high = value.astype(BF16)
    rest = value - high.astype(F32)
    mid = rest.astype(BF16)
    low = (rest - mid.astype(F32)).astype(BF16)
    return jnp.concatenate([high, mid, low], axis=1)


def head_sum(high, low, spread):
    return dot_nt(high, spread[:LANES]) + dot_nt(low, spread[:LANES])


def lanes_of(p):
    return pl.ds(pl.multiple_of(p * LANES, LANES), LANES)


def sigmoid(v):
    return 0.5 + 0.5 * jnp.tanh(0.5 * v)


def each_pair(body, group=UNROLL):
    def some(i, carry):
        for k in range(group):
            body(i * group + k)
        return carry

    lax.fori_loop(0, PAIRS // group, some, 0)


def put_split(high, low, lanes, value):
    top = value.astype(BF16)
    high[:, lanes] = top
    low[:, lanes] = (value - top.astype(F32)).astype(BF16)


def iota(shape, axis):
    return lax.broadcasted_iota(jnp.int32, shape, axis)


def call(body, outs, *args, scratch=(), flops=2e9):
    vm = pl.BlockSpec(memory_space=pltpu.VMEM)
    size = sum(a.size * a.dtype.itemsize for a in args)
    held = size + sum(math.prod(m) * jnp.dtype(d).itemsize for m, d in outs)
    held += sum(math.prod(m.shape) * jnp.dtype(m.dtype).itemsize for m in scratch)
    return pl.pallas_call(
        body,
        out_shape=[jax.ShapeDtypeStruct(s, d) for s, d in outs],
        in_specs=[vm] * len(args),
        out_specs=[vm] * len(outs),
        scratch_shapes=list(scratch),
        compiler_params=pltpu.CompilerParams(vmem_limit_bytes=max(VMEM_LIMIT, held + VMEM_SLACK)),
        cost_estimate=pl.CostEstimate(flops=int(flops), bytes_accessed=int(size), transcendentals=0),
    )(*args)


def project_body(hidden, gain, wa, wb, normed, conv_in, dt):
    h = hidden[...]
    scale = lax.rsqrt(jnp.mean(h * h, axis=-1, keepdims=True) + epsilon)
    low = (h * scale * gain[...]).astype(BF16)
    normed[...] = low
    cut = wa.shape[1]
    rest = XBC - cut
    conv_in[:, :cut] = dot(low, wa[...]).astype(BF16)
    second = dot(low, wb[...])
    conv_in[:, cut:] = second[:, :rest].astype(BF16)
    dt[...] = jnp.where(iota((SPAN, LANES), 1) < HEADS, second[:, rest : rest + LANES], 0.0)


def project_all_body(hidden, gain, weight, normed, conv_in, dt):
    h = hidden[...]
    scale = lax.rsqrt(jnp.mean(h * h, axis=-1, keepdims=True) + epsilon)
    low = (h * scale * gain[...]).astype(BF16)
    normed[...] = low
    conv_in[...] = dot(low, weight[:, :XBC]).astype(BF16)
    steps = dot(low, weight[:, XBC:])
    dt[...] = jnp.where(iota((SPAN, LANES), 1) < HEADS, steps, 0.0)


def conv_pre(ext, weight, bias, lanes):
    total = bias[:, lanes] + weight[KCONV - 1 : KCONV, lanes] * ext[8 : 8 + SPAN, lanes]
    for s in range(1, KCONV):
        tap = weight[KCONV - 1 - s : KCONV - s, lanes]
        total = total + tap * ext[8 - s : 8 - s + SPAN, lanes]
    return total


def triangle(upper):
    i, j = iota((SPAN, SPAN), 0), iota((SPAN, SPAN), 1)
    return jnp.where((i <= j) if upper else (i >= j), 1.0, 0.0).astype(F32)


def running(mask, value):
    return jnp.dot(mask, value, precision=lax.Precision.HIGHEST, preferred_element_type=F32)


def states_body(
    conv_in, rim, weight, bias, dt, dt_bias, a_log, valid, spread,
    x, stepped, keys, queries, step, cum, fresh, growth, ext, wide, wide_step, weighted,
):
    ext[:8] = rim[...].astype(F32)
    ext[8:] = conv_in[...].astype(F32)

    def act(lanes):
        pre = conv_pre(ext, weight, bias, lanes)
        return (pre * sigmoid(pre)).astype(BF16)

    keys[...] = act(pl.ds(INNER, LANES))
    queries[...] = act(pl.ds(INNER + LANES, LANES))
    raw = dt[...] + dt_bias[...]
    size = jnp.maximum(raw, 0.0) + jnp.log1p(jnp.exp(-jnp.abs(raw)))
    size = jnp.where(iota((SPAN, LANES), 1) < HEADS, size * valid[...], 0.0)
    step[...] = size
    total = running(triangle(False), -jnp.exp(a_log[...]) * size)
    cum[...] = total
    last = total[SPAN - 1 :]
    tail = jnp.exp(last - total) * size
    wide[...] = dot(split3(tail), spread[...])
    wide_step[...] = dot(split3(size), spread[...])
    growth[...] = dot(split3(jnp.broadcast_to(jnp.exp(last), (8, LANES))), spread[...])

    def pair(p):
        lanes = lanes_of(p)
        low = act(lanes)
        x[:, lanes] = low
        wider = low.astype(F32)
        weighted[:, lanes] = (wider * wide[:, lanes]).astype(BF16)
        stepped[:, lanes] = (wider * wide_step[:, lanes]).astype(BF16)

    each_pair(pair)
    fresh[...] = dot(flip(keys[...]).astype(BF16), weighted[...])


def diag_body(x, stepped, keys, queries, cum, skip, spread, y, scores, cum_t, wide):
    scores[...] = dot_nt(queries[...], keys[...])
    cum_t[...] = cum[...].T
    wide[...] = dot(split3(cum[...]), spread[...])
    half = SPAN // 2

    def pair(p):
        lanes = lanes_of(p)
        xp = stepped[:, lanes]
        col = wide[:, lanes]
        turned = pltpu.roll(col, HEAD_DIM, 1)
        first = iota((SPAN, LANES), 1) < HEAD_DIM
        both = []
        for k in range(2):
            c = jnp.where(first, col, turned) if k == 0 else jnp.where(first, turned, col)
            row = cum_t[pl.ds(2 * p + k, 1), :]
            tri = iota((SPAN, half), 0) >= iota((SPAN, half), 1)
            f0 = jnp.exp(jnp.where(tri, c - row[:, :half], FAR))
            f1 = jnp.exp(jnp.where(tri[:half], c[half:] - row[:, half:], FAR))
            d0 = dot((scores[:, :half] * f0).astype(BF16), xp[:half])
            d1 = dot((scores[half:, half:] * f1).astype(BF16), xp[half:])
            both.append(jnp.concatenate([d0[:half], d0[half:] + d1], axis=0))
        y[:, lanes] = jnp.where(first, both[0], both[1]) + skip[:, lanes] * x[:, lanes].astype(F32)

    each_pair(pair)


def finish_body(
    y, gate, queries, carried, cum, gain, w_out, hidden, spread, mixed, normed_out, result, wide, states, total, gated
):
    wide[...] = dot(split3(jnp.exp(cum[...])), spread[...])
    states[...] = dot(queries[...], carried[...])
    total[...] = jnp.zeros_like(total)

    def mix(p):
        lanes = lanes_of(p)
        m = y[:, lanes] + wide[:, lanes] * states[:, lanes]
        mixed[:, lanes] = m
        g = gate[:, lanes].astype(F32)
        v = m * (g * sigmoid(g))
        gated[:, lanes] = v
        total[...] += v * v

    each_pair(mix)
    mean = jnp.sum(total[...], axis=1, keepdims=True) * (1.0 / INNER)
    scale = lax.rsqrt(mean + epsilon)

    def norm(p):
        lanes = lanes_of(p)
        normed_out[:, lanes] = (gated[:, lanes] * scale * gain[:, lanes]).astype(BF16)

    each_pair(norm)
    result[...] = hidden[...] + dot(normed_out[...], w_out[...])


def open_body(
    grad, w_out, mixed, gate, gain, queries, carried, cum, x, skip, spread,
    gain_grad, gate_low, diag_low, entering_grad, query_grad, cum_grad, skip_grad,
    wide, square, cross, back, state_low, high, low,
):
    out_low = grad[...].astype(BF16)
    square[...] = jnp.zeros_like(square)
    cross[...] = jnp.zeros_like(cross)
    wide[...] = dot(split3(jnp.exp(cum[...])), spread[...])
    back[...] = dot_nt(out_low, w_out[...])

    def first(p):
        lanes = lanes_of(p)
        a = gate[:, lanes].astype(F32)
        v = mixed[:, lanes] * (a * sigmoid(a))
        square[...] += v * v
        cross[...] += v * (back[:, lanes] * gain[:, lanes])

    each_pair(first)
    scale = lax.rsqrt(jnp.sum(square[...], axis=1, keepdims=True) * (1.0 / INNER) + epsilon)
    share = jnp.sum(cross[...], axis=1, keepdims=True) * (1.0 / INNER) * scale * scale * scale

    def second(p):
        lanes = lanes_of(p)
        g = back[:, lanes]
        a = gate[:, lanes].astype(F32)
        s = sigmoid(a)
        act = a * s
        m = mixed[:, lanes]
        v = m * act
        gain_grad[:, lanes] = jnp.sum(g * v * scale, axis=0, keepdims=True)
        dv = scale * (g * gain[:, lanes]) - v * share
        gate_low[:, lanes] = (dv * m * (s + act * (1.0 - s))).astype(BF16)
        gm = dv * act
        rounded = gm.astype(BF16)
        diag_low[:, lanes] = rounded
        xp = x[:, lanes].astype(F32)
        skip_grad[:, lanes] = jnp.sum(gm * xp, axis=0, keepdims=True)
        state_low[:, lanes] = (wide[:, lanes] * gm).astype(BF16)
        put_split(high, low, lanes, rounded.astype(F32) * (m - skip[:, lanes] * xp))

    each_pair(second)
    cum_grad[...] = head_sum(high[...], low[...], spread)
    entering_grad[...] = dot(flip(queries[...]).astype(BF16), state_low[...])
    query_grad[...] = dot_nt(state_low[...], carried[...])


def pairs_body(
    diag_low, x, stepped, keys, queries, step, cum, skip, spread, query_in,
    x_grad, key_grad, query_grad, step_grad, col_grad,
    scores, score_grad, cum_t, wide, wide_step, high, low, col_high, col_low,
):
    scores[...] = dot_nt(keys[...], queries[...])
    score_grad[...] = jnp.zeros_like(score_grad)
    cum_t[...] = cum[...].T
    wide[...] = dot(split3(cum[...]), spread[...])
    wide_step[...] = dot(split3(step[...]), spread[...])
    half = SPAN // 2

    def pair(p):
        lanes = lanes_of(p)
        xp = stepped[:, lanes]
        dp = diag_low[:, lanes]
        first = iota((SPAN, LANES), 1) < HEAD_DIM
        col = wide[:, lanes]
        turned = pltpu.roll(col, HEAD_DIM, 1)
        both = []
        for k in range(2):
            mine = first if k == 0 else jnp.logical_not(first)
            c = jnp.where(mine, col, turned)
            row = cum_t[pl.ds(2 * p + k, 1), :]
            tri = iota((SPAN, half), 0) <= iota((SPAN, half), 1) + half
            xk = jnp.where(mine, xp.astype(F32), 0.0).astype(BF16)
            f1 = jnp.exp(jnp.where(tri, row[:, half:] - c, FAR))
            f0 = jnp.exp(jnp.where(tri[half:], row[:, :half] - c[:half], FAR))
            score_grad[:, half:] += dot_nt(xk, dp[half:]) * f1
            score_grad[:half, :half] += dot_nt(xk[:half], dp[:half]) * f0
            top = dot((scores[:, half:] * f1).astype(BF16), dp[half:])
            bottom = dot((scores[:half, :half] * f0).astype(BF16), dp[:half])
            both.append(jnp.concatenate([top[:half] + bottom, top[half:]], axis=0))
        through = jnp.where(first, both[0], both[1])
        x_grad[:, lanes] = wide_step[:, lanes] * through + skip[:, lanes] * dp.astype(F32)
        put_split(high, low, lanes, x[:, lanes].astype(F32) * through)
        put_split(col_high, col_low, lanes, xp.astype(F32) * through)

    each_pair(pair)
    step_grad[...] = head_sum(high[...], low[...], spread)
    col_grad[...] = head_sum(col_high[...], col_low[...], spread)
    key_grad[...] = dot(score_grad[...].astype(BF16), queries[...])
    query_grad[...] = query_in[...] + dot(score_grad[...].T.astype(BF16), keys[...])


def close_body(
    pending, carried, keys, x, step, cum, x_grad, key_in, query_grad, step_in, col_in, cum_in,
    conv_in, rim, weight, bias, dt, dt_bias, a_log, valid, spread,
    act_grad, dt_low, dt_bias_grad, a_log_grad, bias_grad, weight_grad,
    ext, wide, back, weighted, column, high, low,
):
    ext[:8] = rim[...].astype(F32)
    ext[8:] = conv_in[...].astype(F32)
    total = cum[...]
    size = step[...]
    last = total[SPAN - 1 :]
    fade = jnp.exp(last - total)
    tail = fade * size
    late = pending[...].astype(BF16)
    wide[...] = dot(split3(tail), spread[...])
    back[...] = dot(keys[...], late)

    def through(lanes, grad):
        pre = conv_pre(ext, weight, bias, lanes)
        s = sigmoid(pre)
        ga = grad * (s * (1.0 + pre * (1.0 - s)))
        act_grad[:, lanes] = ga.astype(BF16)
        bias_grad[:, lanes] = jnp.sum(ga, axis=0, keepdims=True)
        for k in range(KCONV):
            at = 8 - (KCONV - 1 - k)
            weight_grad[k : k + 1, lanes] = jnp.sum(
                ga * ext[at : at + SPAN, lanes], axis=0, keepdims=True
            )

    def pair(p):
        lanes = lanes_of(p)
        xp = x[:, lanes].astype(F32)
        over = wide[:, lanes]
        gw = back[:, lanes]
        put_split(high, low, lanes, gw * xp)
        weighted[:, lanes] = (xp * over).astype(BF16)
        kept = pending[:, lanes] * carried[:, lanes].astype(F32)
        column[:, lanes] = jnp.broadcast_to(jnp.sum(kept, axis=0, keepdims=True), (8, LANES))
        through(lanes, x_grad[:, lanes] + gw * over)

    each_pair(pair)
    through(pl.ds(INNER, LANES), key_in[...] + dot_nt(weighted[...], late))
    through(pl.ds(INNER + LANES, LANES), query_grad[...])
    tg = head_sum(high[...], low[...], spread)
    top = column[...].astype(BF16)
    grow_grad = head_sum(top, (column[...] - top.astype(F32)).astype(BF16), spread)
    run = tg * tail
    cg = cum_in[...] - col_in[...] - run
    end = jnp.sum(run, axis=0, keepdims=True) + grow_grad[:1] * jnp.exp(last)
    cg = cg + jnp.where(iota((SPAN, LANES), 0) == SPAN - 1, end, 0.0)
    rate = jnp.exp(a_log[...])
    decay_grad = running(triangle(True), cg)
    sg = tg * fade + step_in[...] - rate * decay_grad
    a_log_grad[...] = jnp.sum(decay_grad * (-rate * size), axis=0, keepdims=True)
    pre_grad = sg * valid[...] * sigmoid(dt[...] + dt_bias[...])
    pre_grad = jnp.where(iota((SPAN, LANES), 1) < HEADS, pre_grad, 0.0)
    dt_bias_grad[...] = jnp.sum(pre_grad, axis=0, keepdims=True)
    dt_low[...] = pre_grad.astype(BF16)


def conv_back(act_grad, rim_grad, weight, dt_low, first, ext):
    ext[:SPAN] = act_grad[...].astype(F32)
    ext[SPAN:] = rim_grad[...].astype(F32)

    def conv(c, carry):
        for k in range(2):
            lanes = lanes_of(2 * c + k)
            total = weight[KCONV - 1 : KCONV, lanes] * ext[:SPAN, lanes]
            for s in range(1, KCONV):
                total = total + weight[KCONV - 1 - s : KCONV - s, lanes] * ext[s : s + SPAN, lanes]
            first[:, lanes] = total.astype(BF16)
        return carry

    lax.fori_loop(0, XBC // LANES // 2, conv, 0)
    first[:, XBC : XBC + LANES] = dt_low[...]


def norm_back(back, hidden, gain, grad, grad_out, gain_grad):
    h = hidden[...]
    scale = lax.rsqrt(jnp.mean(h * h, axis=-1, keepdims=True) + epsilon)
    gain_grad[...] = jnp.sum(back * h * scale, axis=0, keepdims=True)
    back = back * gain[...]
    share = jnp.mean(back * h, axis=-1, keepdims=True) * scale * scale * scale
    grad_out[...] = grad[...] + back * scale - h * share


def inward_body(act_grad, rim_grad, weight, dt_low, gate_part, wa, wb, hidden, gain, grad, first, grad_out, gain_grad, ext):
    conv_back(act_grad, rim_grad, weight, dt_low, first, ext)
    cut = wa.shape[1]
    back = gate_part[...] + dot_nt(first[:, :cut], wa[...]) + dot_nt(first[:, cut:], wb[...])
    norm_back(back, hidden, gain, grad, grad_out, gain_grad)


def inward_all_body(act_grad, rim_grad, weight, dt_low, gate_part, whole, hidden, gain, grad, first, grad_out, gain_grad, ext):
    conv_back(act_grad, rim_grad, weight, dt_low, first, ext)
    norm_back(gate_part[...] + dot_nt(first[...], whole[...]), hidden, gain, grad, grad_out, gain_grad)


def padded(row):
    return jnp.pad(row.astype(F32), (0, LANES - row.shape[0]))[None]


def layer_forward(hidden, weights, heads, keep, valid, spread):
    norm_gain, w_in, conv_weight, conv_bias, gate_gain, w_out = weights
    dt_bias, a_log, skip = heads
    count = hidden.shape[0]
    outs = [((count, hidden.shape[1]), BF16), ((count, XBC), BF16), ((count, LANES), F32)]
    body = project_body if len(w_in) == 3 else project_all_body
    normed, conv_in, dt = call(body, outs, hidden, norm_gain, *w_in[:-1])
    gate = dot(normed, w_in[-1]).astype(BF16)
    rim = (shifted(conv_in[count - 8 :], "fsdp", 1).astype(F32) * keep).astype(BF16)
    x, stepped, keys, queries, step, cum, fresh, growth = call(
        states_body,
        [
            ((count, INNER), BF16), ((count, INNER), BF16), ((count, STATE), BF16), ((count, STATE), BF16), ((count, LANES), F32),
            ((count, LANES), F32), ((STATE, INNER), F32), ((8, INNER), F32),
        ],
        conv_in, rim, conv_weight, conv_bias, dt, dt_bias, a_log, valid, spread,
        scratch=[
            pltpu.VMEM((count + 8, XBC), F32), pltpu.VMEM((count, INNER), F32), pltpu.VMEM((count, INNER), F32),
            pltpu.VMEM((count, INNER), BF16),
        ],
        flops=5e8,
    )
    growth = growth[:1]
    scan = scan_states(keep * growth, fresh, "fsdp", 1)
    stepped = tied(stepped, next(scan))
    (y,) = call(
        diag_body, [((count, INNER), F32)], x, stepped, keys, queries, cum, skip, spread,
        scratch=[
            pltpu.VMEM((SPAN, SPAN), F32), pltpu.VMEM((LANES, count), F32),
            pltpu.VMEM((count, INNER), F32),
        ],
        flops=4e9,
    )
    carried = (keep * next(scan)).astype(BF16)
    mixed, normed_out, result = call(
        finish_body,
        [((count, INNER), F32), ((count, INNER), BF16), (hidden.shape, F32)],
        y, gate, queries, carried, cum, gate_gain, w_out, hidden, spread,
        scratch=[
            pltpu.VMEM((count, INNER), F32), pltpu.VMEM((count, INNER), F32), pltpu.VMEM((count, LANES), F32),
            pltpu.VMEM((count, INNER), F32),
        ],
    )
    saved = (hidden, normed, conv_in, dt, rim, x, stepped, keys, queries, step, cum, growth, carried, gate, mixed, normed_out)
    return result, saved


def layer_backward(grad, saved, weights, heads, keep, valid, spread, grid):
    norm_gain, w_in, conv_weight, conv_bias, gate_gain, w_out = weights
    dt_bias, a_log, skip = heads
    hidden, normed, conv_in, dt, rim, x, stepped, keys, queries, step, cum, growth, carried, gate, mixed, normed_out = saved
    count = hidden.shape[0]
    row = (1, INNER)
    gain_grad, gate_low, diag_low, entering_grad, query_part, cum_part, skip_grad = call(
        open_body,
        [
            (row, F32), ((count, INNER), BF16), ((count, INNER), BF16), ((STATE, INNER), F32), ((count, STATE), F32),
            ((count, LANES), F32), (row, F32),
        ],
        grad, w_out, mixed, gate, gate_gain, queries, carried, cum, x, skip, spread,
        scratch=[
            pltpu.VMEM((count, INNER), F32), pltpu.VMEM((count, LANES), F32),
            pltpu.VMEM((count, LANES), F32), pltpu.VMEM((count, INNER), F32), pltpu.VMEM((count, INNER), BF16),
            pltpu.VMEM((count, INNER), BF16), pltpu.VMEM((count, INNER), BF16),
        ],
    )
    grad_w_out = dot(normed_out.T, grad.astype(BF16)).astype(BF16)
    scan = scan_states(keep * growth, keep * entering_grad, "fsdp", -1)
    diag_low = tied(diag_low, next(scan))
    x_grad, key_grad, query_grad, step_grad, col_grad = call(
        pairs_body,
        [
            ((count, INNER), F32), ((count, STATE), F32), ((count, STATE), F32), ((count, LANES), F32),
            ((count, LANES), F32),
        ],
        diag_low, x, stepped, keys, queries, step, cum, skip, spread, query_part,
        scratch=[
            pltpu.VMEM((SPAN, SPAN), F32), pltpu.VMEM((SPAN, SPAN), F32), pltpu.VMEM((LANES, count), F32),
            pltpu.VMEM((count, INNER), F32), pltpu.VMEM((count, INNER), F32),
            *[pltpu.VMEM((count, INNER), BF16)] * 4,
        ],
        flops=8e9,
    )
    split = len(w_in) == 3
    ready, moved = None, None
    grad_w_gate = dot(normed.T, gate_low).astype(BF16)
    gate_part = dot(gate_low, w_in[-1].T)
    if split:
        steps = scatter_near(grid, [grad_w_gate, grad_w_out])
        ready = next(steps)
        x_grad = tied(x_grad, *ready)
    pending = next(scan)
    act_grad, dt_low, dt_bias_grad, a_log_grad, bias_grad, weight_grad = call(
        close_body,
        [
            ((count, XBC), BF16), ((count, LANES), BF16), ((1, LANES), F32), ((1, LANES), F32), ((1, XBC), F32),
            ((KCONV, XBC), F32),
        ],
        pending, carried, keys, x, step, cum, x_grad, key_grad, query_grad, step_grad, col_grad, cum_part,
        conv_in, rim, conv_weight, conv_bias, dt, dt_bias, a_log, valid, spread,
        scratch=[
            pltpu.VMEM((count + 8, XBC), F32), pltpu.VMEM((count, INNER), F32), pltpu.VMEM((count, INNER), F32),
            pltpu.VMEM((count, INNER), BF16), pltpu.VMEM((8, INNER), F32), pltpu.VMEM((count, INNER), BF16),
            pltpu.VMEM((count, INNER), BF16),
        ],
    )
    rim_grad = shifted((act_grad[:8].astype(F32) * keep).astype(BF16), "fsdp", -1)
    outs = [((count, XBC + LANES), BF16), (hidden.shape, F32), ((1, hidden.shape[1]), F32)]
    scratch = [pltpu.VMEM((count + 8, XBC), F32)]
    if split:
        ready = next(steps)
        first, grad_out, norm_grad = call(
            inward_body, outs, act_grad, rim_grad, conv_weight, dt_low, gate_part, *w_in[:2], hidden, norm_gain, grad,
            scratch=scratch,
        )
        cut = w_in[0].shape[1]
        first_grads = [dot(normed.T, first[:, :cut]).astype(BF16), dot(normed.T, first[:, cut:]).astype(BF16)]
        mats = (ready, first_grads)
    else:
        first, grad_out, norm_grad = call(
            inward_all_body, outs, act_grad, rim_grad, conv_weight, dt_low, gate_part, w_in[0], hidden, norm_gain, grad,
            scratch=scratch,
        )
        mats = (dot(normed.T, first).astype(BF16), grad_w_gate, grad_w_out)
    skip_sum = jnp.sum(skip_grad.reshape(HEADS, HEAD_DIM), axis=1)
    rows = jnp.concatenate(
        [
            norm_grad[0],
            weight_grad.reshape(-1),
            bias_grad[0],
            gain_grad[0],
            dt_bias_grad[0],
            a_log_grad[0],
            padded(skip_sum)[0],
        ]
    )
    return grad_out, mats, rows


def shards(
    tokens,
    starts,
    valid,
    norm_gain,
    w_gate,
    w_xbc,
    w_dt,
    conv_weight,
    conv_bias,
    dt_bias,
    a_log,
    skip_weight,
    gate_gain,
    w_out,
    cotangent,
):
    layers = norm_gain.shape[0]
    grid = Grid()
    count = grid.count
    rows, outer = w_gate.shape[1], w_out.shape[1]
    taps, chans = conv_weight.shape[1:]
    pad = LANES - HEADS
    cut = XBC // 2 // LANES * LANES
    small = jnp.concatenate(
        [
            v.reshape(-1)
            for l in range(layers)
            for v in (norm_gain[l], conv_weight[l], conv_bias[l], gate_gain[l])
        ]
    )
    length = small.size
    small = jnp.pad(small, (0, -length % (8 * LANES))).reshape((1,) * grid.depth + (-1, LANES))
    firsts, seconds = [], []
    hidden_width = tokens.shape[1]
    for l in range(layers):
        tail = jnp.concatenate([w_xbc[l][:, cut:], w_dt[l], jnp.zeros((rows, pad), BF16)], 1)
        if l == 0:
            pair, last_far, last_near, small = gather_pack(grid, [w_xbc[l][:, :cut], tail], None, None, small)
            firsts.append(pair)
            pair, *_ = gather_pack(grid, [w_gate[l], w_out[l]], last_far, last_near)
            seconds.append(pair)
            continue
        first = jnp.concatenate([w_xbc[l][:, :cut], tail], axis=1)
        firsts.append([lax.all_gather(first, AXES, axis=0, tiled=True)])
        second = jnp.concatenate([w_out[l], w_gate[l].reshape(outer, -1)], axis=1)
        second = lax.all_gather(second, AXES, axis=0, tiled=True)
        seconds.append([second[:, hidden_width:].reshape(hidden_width, INNER), second[:, :hidden_width]])
    small = small.reshape(count, -1)[:, :length].astype(F32)
    wholes, heads = [], []
    at = 0
    for l in range(layers):
        rest = []
        for size in (rows, taps * chans, chans, outer):
            rest.append(small[:, at : at + size])
            at += size
        w_in = firsts[l]
        kernel = jnp.moveaxis(rest[1].reshape(count, taps, chans), 1, 0)
        wholes.append(
            (
                rest[0].reshape(1, -1),
                [*w_in, seconds[l][0]],
                kernel.reshape(taps, -1),
                rest[2].reshape(1, -1),
                rest[3].reshape(1, -1),
                seconds[l][1],
            )
        )
        heads.append((padded(dt_bias[l]), padded(a_log[l]), jnp.repeat(skip_weight[l], HEAD_DIM)[None]))
    spread = (iota((3 * LANES, INNER), 0) % LANES == iota((3 * LANES, INNER), 1) // HEAD_DIM).astype(BF16)
    keep = 1.0 - starts[0].astype(F32)
    valid = valid.astype(F32)[:, None]
    hidden = tokens.astype(F32)
    saves = []
    for l in range(layers):
        hidden, saved = layer_forward(hidden, wholes[l], heads[l], keep, valid, spread)
        saves.append(saved)
    grad = cotangent.astype(F32)
    owned, summed = [None] * layers, [None] * layers
    for l in reversed(range(layers)):
        grad, mats, summed[l] = layer_backward(grad, saves[l], wholes[l], heads[l], keep, valid, spread, grid)
        if l == 0:
            sums = jnp.stack(summed)
            (left, right), (gate_sum, out_sum), sums = scatter_last(grid, mats[1], mats[0], sums)
        else:
            outs = jnp.moveaxis(mats[2].reshape(count, 2, rows, -1), 1, 2).reshape(count * rows, -1)
            packed = jnp.concatenate([mats[0], mats[1], outs], axis=1)
            packed = lax.psum_scatter(packed, AXES, scatter_dimension=0, tiled=True).astype(F32)
            at = XBC + LANES
            left, right = packed[:, :cut], packed[:, cut:at]
            gate_sum = packed[:, at : at + INNER]
            out_sum = jnp.moveaxis(packed[:, at + INNER :].reshape(rows, 2, -1), 1, 0).reshape(outer, -1)
        owned[l] = (
            gate_sum,
            jnp.concatenate([left, right[:, : XBC - cut]], axis=1),
            right[:, XBC - cut : XBC - cut + HEADS],
            out_sum,
        )
    at_kernel = rows * count
    at_bias = at_kernel + taps * chans * count
    at_gain = at_bias + chans * count
    at_heads = at_gain + outer * count

    def own(first, size):
        return lax.dynamic_slice_in_dim(sums, first + grid.place * size, size, 1)

    kernel_sums = sums[:, at_kernel:at_bias].reshape(layers, taps, count * chans)
    kernel_sums = lax.dynamic_slice_in_dim(kernel_sums, grid.place * chans, chans, 2)
    head_sums = sums[:, at_heads:].reshape(layers, 3, LANES)[:, :, :HEADS]

    def stacked(position):
        return jnp.stack([member[position] for member in owned])

    return (
        hidden,
        grad,
        own(0, rows),
        stacked(0),
        stacked(1),
        stacked(2),
        kernel_sums,
        own(at_bias, chans),
        head_sums[:, 0],
        head_sums[:, 1],
        head_sums[:, 2],
        own(at_gain, outer),
        stacked(3),
    )


def solution(mesh):
    return jax.shard_map(
        shards,
        mesh=mesh,
        in_specs=(
            P(("dp", "fsdp"), None),
            P(("dp", "fsdp")),
            P(("dp", "fsdp")),
            P(None, ("dp", "fsdp")),
            P(None, ("dp", "fsdp"), None),
            P(None, ("dp", "fsdp"), None),
            P(None, ("dp", "fsdp"), None),
            P(None, None, ("dp", "fsdp")),
            P(None, ("dp", "fsdp")),
            P(),
            P(),
            P(),
            P(None, ("dp", "fsdp")),
            P(None, ("dp", "fsdp"), None),
            P(("dp", "fsdp"), None),
        ),
        out_specs=(
            P(("dp", "fsdp"), None),
            P(("dp", "fsdp"), None),
            P(None, ("dp", "fsdp")),
            P(None, ("dp", "fsdp"), None),
            P(None, ("dp", "fsdp"), None),
            P(None, ("dp", "fsdp"), None),
            P(None, None, ("dp", "fsdp")),
            P(None, ("dp", "fsdp")),
            P(),
            P(),
            P(),
            P(None, ("dp", "fsdp")),
            P(None, ("dp", "fsdp"), None),
        ),
        check_vma=False,
    )
```
